32 devices in a mesh: seq: 4 (over x, core), fsdp: 8 (over z, y).
Axes of the slice: x: 2, y: 2, z: 4, core: 2. Of those that a mesh axis runs over, the one named last changes fastest.
Arguments:
- latents_in: bfloat16 [8, 1024, 768], P('fsdp', 'seq'), may hold values from -6 to 6
- conditions: float32 [8, 768], P('fsdp'), may hold values from -6 to 6
- w_ada: bfloat16 [768, 4608], P('fsdp'), may hold values from -0.21875 to 0.21875
- b_ada: bfloat16 [4608], P('fsdp'), may hold values from -3 to 3
- w_qkv: bfloat16 [768, 2304], P('fsdp'), may hold values from -0.21875 to 0.21875
- b_qv: bfloat16 [1536], P('fsdp'), may hold values from -3 to 3
- w_proj: bfloat16 [768, 768], P('fsdp'), may hold values from -3 to 3
- b_proj: bfloat16 [768], P('fsdp'), may hold values from -3 to 3
- w_fc1: bfloat16 [768, 3072], P('fsdp'), may hold values from -0.21875 to 0.21875
- b_fc1: bfloat16 [3072], P('fsdp'), may hold values from -3 to 3
- w_fc2: bfloat16 [3072, 768], P('fsdp'), may hold values from -0.109375 to 0.109375
- b_fc2: bfloat16 [768], P('fsdp'), may hold values from -3 to 3
- out_grad: bfloat16 [8, 1024, 768], P('fsdp', 'seq'), may hold values from -6 to 6
Outputs:
- latents_out: bfloat16 [8, 1024, 768], P('fsdp', 'seq')
- latents_grad: float32 [8, 1024, 768], P('fsdp', 'seq')
- cond_grad: float32 [8, 768], P('fsdp')
- grad_w_ada: float32 [768, 4608], P('fsdp')
- grad_b_ada: float32 [4608], P('fsdp')
- grad_w_qkv: float32 [768, 2304], P('fsdp')
- grad_b_qv: float32 [1536], P('fsdp')
- grad_w_proj: float32 [768, 768], P('fsdp')
- grad_b_proj: float32 [768], P('fsdp')
- grad_w_fc1: float32 [768, 3072], P('fsdp')
- grad_b_fc1: float32 [3072], P('fsdp')
- grad_w_fc2: float32 [3072, 768], P('fsdp')
- grad_b_fc2: float32 [768], P('fsdp')
The draws below stay inside these ranges and needn't reach their ends.
All inputs are finite; a program needn't handle non-finite values.
Results may differ from the reference program's by a relative error of at most 0.015.
The reference program's roundings to bfloat16 on the way count: a program that leaves them out, or rounds other values in their place, can miss the bound.
Values may be sent and summed in bfloat16 or wider, within the bound.
No kernel may reach another device: no remote copies, remote signals or barrier semaphores. Data moves between devices by JAX's collectives and lax.ppermute only.
A program may use at most 192 MiB of HBM per device.

```python
import jax
import jax.numpy as jnp
from jax import lax

D = 768
HEADS = 12
HEAD = 64
FF = 3072
LENGTH = 1024
LATENTS = 8


def levels(key, dims, cuts, smallest, high):
    factor_of = 1.0
    for axis_at, shards_of in cuts:
        draws = jax.random.uniform(jax.random.fold_in(jax.random.fold_in(key, 6), axis_at), (shards_of,), jnp.float32, smallest / len(cuts), high / len(cuts))
        factor_of = factor_of * jnp.repeat(jnp.exp(draws), dims[axis_at] // shards_of).reshape((-1,) + (1,) * (len(dims) - 1 - axis_at))
    return factor_of


def bell_draw(stream_key, extent, spread, bound, cuts=(), dtype=jnp.bfloat16):
    values = jax.random.normal(stream_key, extent, jnp.float32) * spread
    if len(cuts) > 0:
        values = levels(stream_key, extent, cuts, -0.22, 0.18) * values
    return jnp.clip(values, min=-bound, max=bound).astype(dtype)


def setup_inputs(seed: int = 0) -> dict:
    key_of = jax.random.split(jax.random.key(seed), 14)
    latents_in = bell_draw(key_of[0], (LATENTS, LENGTH, D), 1.0, 6.0, ((0, 8), (1, 4)))
    conditions = bell_draw(key_of[1], (LATENTS, D), 1.0, 6.0, ((0, 8),), jnp.float32)
    w_ada = bell_draw(key_of[2], (D, 6 * D), D ** -0.5, 0.21875, ((0, 8),))
    b_ada = bell_draw(key_of[3], (6 * D,), 0.5, 3.0, ((0, 8),))
    w_qkv = bell_draw(key_of[4], (D, 3 * D), D ** -0.5, 0.21875, ((0, 8),))
    b_qv = bell_draw(key_of[5], (2 * D,), 0.5, 3.0, ((0, 8),))
    w_proj = bell_draw(key_of[6], (D, D), 4 ** -0.5, 3.0, ((0, 8),))
    b_proj = bell_draw(key_of[7], (D,), 0.5, 3.0, ((0, 8),))
    w_fc1 = bell_draw(key_of[8], (D, FF), D ** -0.5, 0.21875, ((0, 8),))
    b_fc1 = bell_draw(key_of[9], (FF,), 0.5, 3.0, ((0, 8),))
    w_fc2 = bell_draw(key_of[10], (FF, D), FF ** -0.5, 0.109375, ((0, 8),))
    b_fc2 = bell_draw(key_of[11], (D,), 0.5, 3.0, ((0, 8),))
    out_grad = bell_draw(key_of[12], (LATENTS, LENGTH, D), 1.0, 6.0, ((0, 8), (1, 4)))
    return {"latents_in": latents_in, "conditions": conditions, "w_ada": w_ada, "b_ada": b_ada, "w_qkv": w_qkv, "b_qv": b_qv, "w_proj": w_proj, "b_proj": b_proj, "w_fc1": w_fc1, "b_fc1": b_fc1, "w_fc2": w_fc2, "b_fc2": b_fc2, "out_grad": out_grad}


@jax.custom_vjp
def low(v):
    return lax.optimization_barrier(v.astype(jnp.bfloat16)).astype(jnp.float32)

@jax.custom_vjp
def low_back(v):
    return v

def low_keep(v):
    return (low(v), None)

def low_pass(kept, grad):
    return (grad,)

def back_keep(v):
    return (v, None)

def back_low(kept, grad):
    return (low(grad),)
low.defvjp(low_keep, low_pass)
low_back.defvjp(back_keep, back_low)
norm_eps = 1e-06
highest = lax.Precision.HIGHEST

def layer_norm(values):
    mean_val = lax.optimization_barrier(jnp.mean(values, axis=-1, keepdims=True))
    centred = values - mean_val
    var_val = lax.optimization_barrier(jnp.mean(centred * centred, axis=-1, keepdims=True))
    return centred * lax.rsqrt(var_val + norm_eps)

def one_latent(weights, latent, condition):
    w_ada, b_ada, w_qkv, b_qv, w_proj, b_proj, w_fc1, b_fc1, w_fc2, b_fc2 = weights
    cond_act = low(jax.nn.silu(condition))
    modulation = low_back(jnp.dot(cond_act, w_ada, precision=highest) + b_ada)
    shift_one, scale_one, gate_one, shift_two, scale_two, gate_two = jnp.split(modulation, 6)
    act_one = low(layer_norm(latent) * (1.0 + scale_one) + shift_one)
    qkv_all = jnp.dot(act_one, w_qkv, precision=highest)
    queries = low_back(low(qkv_all[:, :D] + b_qv[:D]))
    keys_all = low_back(low(qkv_all[:, D:2 * D]))
    values_all = low_back(low(qkv_all[:, 2 * D:] + b_qv[D:]))
    length = latent.shape[0]
    query_heads = queries.reshape(length, HEADS, HEAD)
    key_heads = keys_all.reshape(length, HEADS, HEAD)
    value_heads = values_all.reshape(length, HEADS, HEAD)
    scores = low_back(jnp.einsum('qhd,khd->hqk', query_heads, key_heads, precision=highest) * HEAD ** (-0.5))
    probs = low(jax.nn.softmax(scores, axis=-1))
    attn = jnp.einsum('hqk,khd->qhd', probs, value_heads, precision=highest).reshape(length, D)
    attn = low_back(low(attn))
    branch_one = low_back(jnp.dot(attn, w_proj, precision=highest) + b_proj)
    mid = latent + gate_one * branch_one
    act_two = low(layer_norm(mid) * (1.0 + scale_two) + shift_two)
    hidden_pre = low_back(jnp.dot(act_two, w_fc1, precision=highest) + b_fc1)
    hidden = low(jax.nn.gelu(hidden_pre, approximate=True))
    branch_two = low_back(jnp.dot(hidden, w_fc2, precision=highest) + b_fc2)
    return mid + gate_two * branch_two

def forward(latents, conds, *weights):

    def per_latent(pair):
        return one_latent(weights, pair[0], pair[1])
    return lax.map(jax.checkpoint(per_latent), (latents, conds))

def reference(latents_in, conditions, w_ada, b_ada, w_qkv, b_qv, w_proj, b_proj, w_fc1, b_fc1, w_fc2, b_fc2, out_grad):
    weights = [w.astype(jnp.float32) for w in (w_ada, b_ada, w_qkv, b_qv, w_proj, b_proj, w_fc1, b_fc1, w_fc2, b_fc2)]
    latents = latents_in.astype(jnp.float32)
    conds = conditions.astype(jnp.float32)
    result, pull_back = jax.vjp(forward, latents, conds, *weights)
    grads = pull_back(out_grad.astype(jnp.float32))
    return (result.astype(jnp.bfloat16), grads[0], grads[1], grads[2], grads[3], grads[4], grads[5], grads[6], grads[7], grads[8], grads[9], grads[10], grads[11])
```

```python
import functools

import jax
import jax.numpy as jnp
from jax import lax
from jax.sharding import PartitionSpec as P

HEAD = 64
RING_MAX = 16

norm_eps = 1e-06
f32 = jnp.float32
bf16 = jnp.bfloat16


def dot(a, b, dims):
    return lax.dot_general(a, b, (dims, ((), ())), preferred_element_type=f32)


def layer_norm(values):
    mean_val = jnp.mean(values, axis=-1, keepdims=True)
    centred = values - mean_val
    var_val = jnp.mean(centred * centred, axis=-1, keepdims=True)
    return centred * lax.rsqrt(var_val + norm_eps)


def gelu_tanh(values):
    return jax.nn.gelu(values, approximate=True)


def seq_swap(values, bit):
    count = lax.axis_size("seq")
    return lax.ppermute(values, "seq", [(i, i ^ bit) for i in range(count)])


swap_core = functools.partial(seq_swap, bit=1)
swap_x = functools.partial(seq_swap, bit=2)


def rolled(rows, shift):
    count = rows.shape[0]
    return lax.dynamic_slice_in_dim(jnp.concatenate([rows, rows]), count - shift, count, 0)


def gather_small(row, me):
    count = lax.axis_size("fsdp")
    if count > RING_MAX:
        rows = lax.all_gather(row, "fsdp", axis=0)
        return rolled(rows[::-1], jnp.mod(me + 1, count))
    got = [row]
    for r in range(1, count):
        got.append(lax.ppermute(row, "fsdp", [(i, (i + r) % count) for i in range(count)]))
    return jnp.stack(got)


def deal_small(rows, me):
    count = lax.axis_size("fsdp")
    if count > RING_MAX:
        placed = rolled(rows[::-1], jnp.mod(me + 1, count))
        got = lax.all_to_all(placed, "fsdp", split_axis=0, concat_axis=0, tiled=True)
        return rolled(got, jnp.mod(count - me, count))
    got = [rows[0]]
    for r in range(1, count):
        got.append(lax.ppermute(rows[r], "fsdp", [(i, (i - r) % count) for i in range(count)]))
    return jnp.stack(got)


def ring_tables(count):
    order = list(range(0, count, 2)) + list(range(count - 1, 0, -2))
    ahead = [(order[i], order[(i + 1) % count]) for i in range(count)]
    return order, ahead, [(b, a) for a, b in ahead]


def ring_place(me, offset):
    count = lax.axis_size("fsdp")
    mine = jnp.where(me % 2 == 0, me // 2, count - 1 - me // 2)
    place = jnp.mod(mine + offset + count, count)
    return jnp.where(place < count // 2, 2 * place, 2 * (count - 1 - place) + 1)


def ring_gather(block, me):
    count = lax.axis_size("fsdp")
    if count > RING_MAX:
        return lax.all_gather(block, "fsdp", axis=0, tiled=True)
    _, ahead, back = ring_tables(count)
    rows = block.shape[0]
    half = rows // 2
    far = count // 2
    out = jnp.zeros((rows * count,) + block.shape[1:], block.dtype)

    def put(out, piece, offset, shift):
        start = ring_place(me, offset) * rows + shift
        return lax.dynamic_update_slice_in_dim(out, piece, start, 0)

    out = put(out, block, 0, 0)
    up = down = block
    for step in range(1, far + 1):
        if step == far:
            up, down = up[:half], down[half:]
        up = lax.ppermute(up, "fsdp", ahead)
        down = lax.ppermute(down, "fsdp", back)
        out = put(out, up, -step, 0)
        out = put(out, down, step, half if step == far else 0)
    return out


def ring_reduce(values, me):
    count = lax.axis_size("fsdp")
    rows = values.shape[0] // count
    if count > RING_MAX:
        return lax.psum_scatter(
            values.astype(bf16), "fsdp", scatter_dimension=0, tiled=True
        ).astype(f32)
    _, ahead, back = ring_tables(count)
    half = rows // 2
    far = count // 2

    def take(offset, start, size):
        return lax.dynamic_slice_in_dim(
            values, ring_place(me, offset) * rows + start, size, 0
        ).astype(f32)

    up = take(far, 0, half)
    down = take(-far, half, half)
    for step in range(1, far + 1):
        up = lax.ppermute(up.astype(bf16), "fsdp", ahead).astype(f32)
        down = lax.ppermute(down.astype(bf16), "fsdp", back).astype(f32)
        if step == far:
            break
        if step == 1:
            up = jnp.concatenate(
                [take(far - 1, 0, half) + up, take(far - 1, half, rows - half)]
            )
            down = jnp.concatenate(
                [take(1 - far, 0, half), take(1 - far, half, rows - half) + down]
            )
        else:
            up = up + take(far - step, 0, rows)
            down = down + take(step - far, 0, rows)
    return take(0, 0, rows) + up + down


def attend_forward(queries, keys, values, scale_val):
    rows = queries.shape[0]
    heads = queries.shape[1] // HEAD
    q = queries.reshape(rows, heads, HEAD)
    k = keys.reshape(rows, heads, HEAD)
    v = values.reshape(rows, heads, HEAD)
    scores = jnp.einsum("qhd,khd->hqk", q, k, preferred_element_type=f32) * scale_val
    top_val = jnp.max(scores, axis=-1, keepdims=True)
    expd_val = jnp.exp(scores - top_val)
    totals = jnp.sum(expd_val, axis=-1, keepdims=True)
    probs = (expd_val / totals).astype(bf16)
    out = jnp.einsum("hqk,khd->qhd", probs, v, preferred_element_type=f32)
    return out.astype(bf16).reshape(rows, heads * HEAD), (top_val + jnp.log(totals))


def attend_backward(queries, keys, values, grad, lse, scale_val):
    rows = queries.shape[0]
    heads = queries.shape[1] // HEAD
    q, k, v, g = (a.reshape(rows, heads, HEAD) for a in (queries, keys, values, grad))
    scores = jnp.einsum("qhd,khd->hqk", q, k, preferred_element_type=f32) * scale_val
    probs = jnp.exp(scores - lse)
    grad_probs = jnp.einsum("qhd,khd->hqk", g, v, preferred_element_type=f32)
    inner = jnp.sum(probs * grad_probs, axis=-1, keepdims=True)
    grad_scores = (probs * (grad_probs - inner)).astype(bf16)
    grad_q = jnp.einsum("hqk,khd->qhd", grad_scores, k, preferred_element_type=f32) * scale_val
    grad_k = jnp.einsum("hqk,qhd->khd", grad_scores, q, preferred_element_type=f32) * scale_val
    grad_v = jnp.einsum("hqk,qhd->khd", probs.astype(bf16), g, preferred_element_type=f32)
    flat = heads * HEAD
    return [a.astype(bf16).reshape(rows, flat) for a in (grad_q, grad_k, grad_v)]


def local(
    latents_in,
    conditions,
    w_ada,
    b_ada,
    w_qkv,
    b_qv,
    w_proj,
    b_proj,
    w_fc1,
    b_fc1,
    w_fc2,
    b_fc2,
    out_grad,
):
    width = latents_in.shape[2]
    tokens = latents_in.shape[1]
    seq_count = lax.axis_size("seq")
    owners = lax.axis_size("fsdp")
    me = lax.axis_index("fsdp")
    place = lax.axis_index("seq")
    core = place % 2
    own_rows = w_ada.shape[0]
    quarter = width // seq_count
    units = w_fc2.shape[0] // 2
    scale_val = HEAD ** (-0.5)

    condition = conditions[0]
    cond_act, silu_pull = jax.vjp(jax.nn.silu, condition)
    cond_low = cond_act.astype(bf16)
    small = jnp.concatenate([cond_low, b_qv, b_proj, b_fc1, b_fc2])
    small_rel = gather_small(small, me)
    cond_rows = lax.dynamic_slice_in_dim(small_rel, me * own_rows, own_rows, 1)
    mod_partial = dot(cond_rows, w_ada, ((1,), (0,)))
    bias_at = b_ada.shape[0]
    placed_bias = jnp.where(
        jnp.arange(owners)[:, None] == me, b_ada.astype(f32)[None, :], 0.0
    ).reshape(1, owners * bias_at)
    mod_partial = mod_partial + placed_bias
    modulation = jnp.sum(deal_small(mod_partial, me), axis=0)
    shift_one, scale_one, gate_one, shift_two, scale_two, gate_two = jnp.split(modulation, 6)

    bias_rel = small_rel[:, width:].astype(f32)
    bias_all = rolled(bias_rel[::-1], jnp.mod(me + 1, owners))
    at = 0
    biases = []
    for b in (b_qv, b_proj, b_fc1, b_fc2):
        biases.append(bias_all[:, at : at + b.shape[0]])
        at += b.shape[0]
    qv_full = biases[0].reshape(2, seq_count, quarter)
    bias_q, bias_v = lax.dynamic_index_in_dim(qv_full, place, 1, keepdims=False)
    bias_proj = biases[1].reshape(width)
    bias_fc1 = lax.dynamic_index_in_dim(
        biases[2].reshape(owners, 2, units), core, 1, keepdims=False
    ).reshape(owners * units)
    bias_fc2 = biases[3].reshape(width)

    mine_qkv = lax.dynamic_index_in_dim(
        w_qkv.reshape(own_rows, 3, seq_count, quarter), place, 2, keepdims=False
    ).reshape(own_rows, 3 * quarter)
    use_qkv = ring_gather(mine_qkv, me)
    mine_proj = lax.dynamic_slice_in_dim(w_proj, core * (width // 2), width // 2, 1)
    proj_half = ring_gather(mine_proj, me)
    proj_other = swap_core(proj_half)
    full_proj = jnp.where(
        core == 0,
        jnp.concatenate([proj_half, proj_other], axis=1),
        jnp.concatenate([proj_other, proj_half], axis=1),
    )
    use_proj = jnp.concatenate(
        [
            lax.dynamic_slice_in_dim(full_proj, (place ^ k) * quarter, quarter, 0)
            for k in range(seq_count)
        ]
    )
    mine_fc1 = lax.dynamic_index_in_dim(
        w_fc1.reshape(own_rows, owners, 2, units), core, 2, keepdims=False
    ).reshape(own_rows, owners * units)
    use_fc1 = ring_gather(mine_fc1, me)
    mine_fc2 = lax.dynamic_slice_in_dim(w_fc2, core * units, units, 0)
    use_fc2 = ring_gather(mine_fc2, me)

    own_latent = latents_in[0]
    from_x = swap_x(own_latent)
    from_core = swap_core(own_latent)
    from_both = swap_core(from_x)
    all_latent = jnp.concatenate([own_latent, from_core, from_x, from_both]).astype(f32)
    latent = own_latent.astype(f32)
    grad_own = out_grad[0]
    grad_pair = jnp.concatenate([grad_own, swap_core(grad_own)]).astype(f32)
    grad_out = grad_own.astype(f32)

    normed_all = layer_norm(all_latent)
    act_one = (normed_all * (1.0 + scale_one) + shift_one).astype(bf16)
    bias_three = jnp.concatenate([bias_q, jnp.zeros_like(bias_q), bias_v])
    qkv = (dot(act_one, use_qkv, ((1,), (0,))) + bias_three).astype(bf16)
    queries, keys, values = jnp.split(qkv, 3, axis=1)
    attn_heads, lse = attend_forward(queries, keys, values, scale_val)

    def to_tokens(blocks):
        return [blocks[0]] + [seq_swap(blocks[k], k) for k in range(1, seq_count)]

    attn_own = jnp.concatenate(
        to_tokens([attn_heads[k * tokens : (k + 1) * tokens] for k in range(seq_count)]), axis=1
    )
    branch_one = dot(attn_own, use_proj, ((1,), (0,))) + bias_proj
    middle = latent + gate_one * branch_one
    normed_two, norm_pull_two = jax.vjp(layer_norm, middle)
    act_two_own = (normed_two * (1.0 + scale_two) + shift_two).astype(bf16)

    act_two = jnp.concatenate([act_two_own, swap_core(act_two_own)])
    hidden_pre = dot(act_two, use_fc1, ((1,), (0,))) + bias_fc1
    hidden_act, gelu_pull = jax.vjp(gelu_tanh, hidden_pre)
    hidden_low = hidden_act.astype(bf16)
    grad_two = (gate_two * grad_pair).astype(bf16)
    grad_hidden = dot(grad_two, use_fc2, ((1,), (1,)))
    grad_pre = gelu_pull(grad_hidden)[0].astype(bf16)
    partial_act = dot(grad_pre, use_fc1, ((1,), (1,)))
    grad_act_two = partial_act[:tokens] + swap_core(partial_act[tokens:])
    grad_shift_two = jnp.sum(grad_act_two, axis=0)
    grad_scale_two = jnp.sum(grad_act_two * normed_two, axis=0)
    grad_middle = grad_out + norm_pull_two(grad_act_two * (1.0 + scale_two))[0]
    grad_one = (gate_one * grad_middle).astype(bf16)
    grad_gate_one = jnp.sum(grad_middle * branch_one, axis=0)
    grad_attn = dot(grad_one, use_proj, ((1,), (1,))).astype(bf16)
    grad_heads = jnp.concatenate(
        to_tokens([grad_attn[:, k * quarter : (k + 1) * quarter] for k in range(seq_count)])
    )

    partial_two = dot(hidden_low, use_fc2, ((1,), (0,)))
    branch_two = partial_two[:tokens] + swap_core(partial_two[tokens:]) + bias_fc2
    result = middle + gate_two * branch_two
    grad_gate_two = jnp.sum(grad_out * branch_two, axis=0)
    grad_b_fc2 = jnp.sum(grad_two[:tokens].astype(f32), axis=0)
    grad_b_fc1 = jnp.sum(grad_pre.astype(f32), axis=0)
    grad_b_proj = jnp.sum(grad_one.astype(f32), axis=0)

    red_fc2 = ring_reduce(dot(hidden_low, grad_two, ((0,), (0,))).astype(bf16), me)
    red_fc1 = ring_reduce(dot(act_two, grad_pre, ((0,), (0,))).astype(bf16), me)

    def add_x(block):
        low = block.astype(bf16)
        return low.astype(f32) + swap_x(low).astype(f32)

    def in_core_order(block):
        other = swap_core(block)
        return jnp.where(core == 0, block, other), jnp.where(core == 0, other, block)

    grad_w_fc2 = jnp.concatenate(in_core_order(add_x(red_fc2)))
    first_fc1, second_fc1 = in_core_order(add_x(red_fc1))
    grad_w_fc1 = jnp.concatenate(
        [first_fc1.reshape(own_rows, owners, 1, units), second_fc1.reshape(own_rows, owners, 1, units)],
        axis=2,
    ).reshape(own_rows, 2 * owners * units)

    proj_rel = dot(attn_own, grad_one, ((0,), (0,))).astype(bf16)
    proj_abs = jnp.concatenate(
        [
            lax.dynamic_slice_in_dim(proj_rel, (place ^ k) * quarter, quarter, 0)
            for k in range(seq_count)
        ]
    )
    half_width = width // 2
    keep = lax.dynamic_slice_in_dim(proj_abs, core * half_width, half_width, 1)
    give = lax.dynamic_slice_in_dim(proj_abs, (1 - core) * half_width, half_width, 1)
    proj_sum = (keep.astype(f32) + swap_core(give).astype(f32)).astype(bf16)
    grad_w_proj = jnp.concatenate(in_core_order(add_x(ring_reduce(proj_sum, me))), axis=1)

    grad_q, grad_k, grad_v = attend_backward(queries, keys, values, grad_heads, lse, scale_val)
    grad_qkv = jnp.concatenate([grad_q, grad_k, grad_v], axis=1)
    red_qkv = ring_reduce(dot(act_one, grad_qkv, ((0,), (0,))).astype(bf16), me).astype(bf16)
    across = swap_x(red_qkv)
    blocks = [red_qkv, swap_core(red_qkv), across, swap_core(across)]
    for bit in (1, 2):
        flip = (place & bit) != 0
        blocks = [jnp.where(flip, blocks[j ^ bit], blocks[j]) for j in range(seq_count)]
    grad_w_qkv = jnp.concatenate(
        [b.astype(f32).reshape(own_rows, 3, 1, quarter) for b in blocks], axis=2
    ).reshape(own_rows, 3 * width)

    partial_one = dot(grad_qkv, use_qkv, ((1,), (1,)))
    grad_shift_one = jnp.sum(partial_one, axis=0)
    grad_scale_one = jnp.sum(partial_one * normed_all, axis=0)
    far_low = partial_one[2 * tokens :].astype(bf16)
    far_sum = far_low[:tokens].astype(f32) + swap_core(far_low[tokens:]).astype(f32)
    near_low = partial_one[tokens : 2 * tokens].astype(bf16)
    near_sum = partial_one[:tokens] + swap_core(near_low).astype(f32)
    grad_act_one = near_sum + swap_x(far_sum.astype(bf16)).astype(f32)
    _, norm_pull_one = jax.vjp(layer_norm, latent)
    grad_latent = grad_middle + norm_pull_one(grad_act_one * (1.0 + scale_one))[0]

    grad_b_qv = jnp.where(
        jnp.arange(seq_count)[None, :, None] == place,
        jnp.stack(
            [jnp.sum(grad_q.astype(f32), axis=0), jnp.sum(grad_v.astype(f32), axis=0)]
        )[:, None, :],
        0.0,
    ).reshape(2 * width)
    placed_fc1 = jnp.where(
        jnp.arange(2)[None, :, None] == core, grad_b_fc1.reshape(owners, 1, units), 0.0
    ).reshape(2 * owners * units)
    terms = jnp.concatenate(
        [
            grad_shift_one,
            grad_scale_one,
            grad_gate_one,
            grad_shift_two,
            grad_scale_two,
            grad_gate_two,
            grad_b_qv,
            grad_b_proj,
            placed_fc1,
            grad_b_fc2,
        ]
    )
    sums = (terms + seq_swap(terms, 1)) + (seq_swap(terms, 2) + seq_swap(terms, 3))
    low_sums = sums.astype(bf16)
    grad_mod = low_sums[: 6 * width]
    at = 6 * width
    by_owner = []
    for b in (b_qv, b_proj, b_fc1, b_fc2):
        size = b.shape[0] * owners
        by_owner.append(low_sums[at : at + size].reshape(owners, b.shape[0]))
        at += size
    by_owner = jnp.concatenate(by_owner, axis=1)
    sent_bias = rolled(by_owner[::-1], jnp.mod(me + 1, owners))
    mail = jnp.concatenate(
        [jnp.broadcast_to(grad_mod[None, :], (owners, 6 * width)), sent_bias], axis=1
    )
    got = deal_small(mail, me)
    mod_rel = got[:, : 6 * width]
    bias_sums = jnp.sum(got[:, 6 * width :].astype(f32), axis=0)
    back_cond = jnp.concatenate([cond_rows[:1], cond_rows[1:][::-1]])
    owned_w_ada = dot(back_cond, mod_rel, ((0,), (0,)))
    owned_b_ada = jnp.sum(
        lax.dynamic_slice_in_dim(mod_rel, me * bias_at, bias_at, 1).astype(f32), axis=0
    )
    cond_partial = dot(mod_rel, w_ada, ((1,), (1,)))
    back_partial = jnp.concatenate([cond_partial[:1], cond_partial[1:][::-1]])
    cond_got = rolled(deal_small(back_partial, me), me)
    grad_cond = silu_pull(cond_got.reshape(width))[0]
    at = 0
    owned_bias = []
    for b in (b_qv, b_proj, b_fc1, b_fc2):
        owned_bias.append(bias_sums[at : at + b.shape[0]])
        at += b.shape[0]
    return (
        result.astype(bf16)[None],
        grad_latent[None],
        grad_cond[None],
        owned_w_ada,
        owned_b_ada,
        grad_w_qkv,
        owned_bias[0],
        grad_w_proj,
        owned_bias[1],
        grad_w_fc1,
        owned_bias[2],
        grad_w_fc2,
        owned_bias[3],
    )


def solution(mesh):
    return jax.shard_map(
        local,
        mesh=mesh,
        in_specs=(
            P("fsdp", "seq", None),
            P("fsdp", None),
            P("fsdp", None),
            P("fsdp"),
            P("fsdp", None),
            P("fsdp"),
            P("fsdp", None),
            P("fsdp"),
            P("fsdp", None),
            P("fsdp"),
            P("fsdp", None),
            P("fsdp"),
            P("fsdp", "seq", None),
        ),
        out_specs=(
            P("fsdp", "seq", None),
            P("fsdp", "seq", None),
            P("fsdp", None),
            P("fsdp", None),
            P("fsdp"),
            P("fsdp", None),
            P("fsdp"),
            P("fsdp", None),
            P("fsdp"),
            P("fsdp", None),
            P("fsdp"),
            P("fsdp", None),
            P("fsdp"),
        ),
        check_vma=False,
    )
```

```python
import functools

import jax
import jax.numpy as jnp
from jax import lax
from jax.experimental import pallas as pl
from jax.experimental.pallas import tpu as pltpu
from jax.sharding import PartitionSpec as P

HEAD = 64
RING_MAX = 16

norm_eps = 1e-06
f32 = jnp.float32
bf16 = jnp.bfloat16


def dot(a, b, dims):
    return lax.dot_general(a, b, (dims, ((), ())), preferred_element_type=f32)


def layer_norm(values):
    mean_val = jnp.mean(values, axis=-1, keepdims=True)
    centred = values - mean_val
    var_val = jnp.mean(centred * centred, axis=-1, keepdims=True)
    return centred * lax.rsqrt(var_val + norm_eps)


def gelu_tanh(values):
    return jax.nn.gelu(values, approximate=True)


def seq_swap(values, bit):
    count = lax.axis_size("seq")
    return lax.ppermute(values, "seq", [(i, i ^ bit) for i in range(count)])


swap_core = functools.partial(seq_swap, bit=1)
swap_x = functools.partial(seq_swap, bit=2)


def rolled(rows, shift):
    count = rows.shape[0]
    return lax.dynamic_slice_in_dim(jnp.concatenate([rows, rows]), count - shift, count, 0)


def gather_small(row, me):
    count = lax.axis_size("fsdp")
    if count > RING_MAX:
        rows = lax.all_gather(row, "fsdp", axis=0)
        return rolled(rows[::-1], jnp.mod(me + 1, count))
    got = [row]
    for r in range(1, count):
        got.append(lax.ppermute(row, "fsdp", [(i, (i + r) % count) for i in range(count)]))
    return jnp.stack(got)


def deal_small(rows, me):
    count = lax.axis_size("fsdp")
    if count > RING_MAX:
        placed = rolled(rows[::-1], jnp.mod(me + 1, count))
        got = lax.all_to_all(placed, "fsdp", split_axis=0, concat_axis=0, tiled=True)
        return rolled(got, jnp.mod(count - me, count))
    got = [rows[0]]
    for r in range(1, count):
        got.append(lax.ppermute(rows[r], "fsdp", [(i, (i - r) % count) for i in range(count)]))
    return jnp.stack(got)


def ring_tables(count):
    order = list(range(0, count, 2)) + list(range(count - 1, 0, -2))
    ahead = [(order[i], order[(i + 1) % count]) for i in range(count)]
    return order, ahead, [(b, a) for a, b in ahead]


def ring_place(me, offset):
    count = lax.axis_size("fsdp")
    mine = jnp.where(me % 2 == 0, me // 2, count - 1 - me // 2)
    place = jnp.mod(mine + offset + count, count)
    return jnp.where(place < count // 2, 2 * place, 2 * (count - 1 - place) + 1)


def ring_gather(block, me):
    count = lax.axis_size("fsdp")
    if count > RING_MAX:
        return lax.all_gather(block, "fsdp", axis=0, tiled=True)
    _, ahead, back = ring_tables(count)
    rows = block.shape[0]
    half = rows // 2
    far = count // 2
    out = jnp.zeros((rows * count,) + block.shape[1:], block.dtype)

    def put(out, piece, offset, shift):
        start = ring_place(me, offset) * rows + shift
        return lax.dynamic_update_slice_in_dim(out, piece, start, 0)

    out = put(out, block, 0, 0)
    up = down = block
    for step in range(1, far + 1):
        if step == far:
            up, down = up[:half], down[half:]
        up = lax.ppermute(up, "fsdp", ahead)
        down = lax.ppermute(down, "fsdp", back)
        out = put(out, up, -step, 0)
        out = put(out, down, step, half if step == far else 0)
    return out


def ring_reduce(values, me):
    count = lax.axis_size("fsdp")
    rows = values.shape[0] // count
    if count > RING_MAX:
        return lax.psum_scatter(
            values.astype(bf16), "fsdp", scatter_dimension=0, tiled=True
        ).astype(f32)
    _, ahead, back = ring_tables(count)
    half = rows // 2
    far = count // 2

    def take(offset, start, size):
        return lax.dynamic_slice_in_dim(
            values, ring_place(me, offset) * rows + start, size, 0
        ).astype(f32)

    up = take(far, 0, half)
    down = take(-far, half, half)
    for step in range(1, far + 1):
        up = lax.ppermute(up.astype(bf16), "fsdp", ahead).astype(f32)
        down = lax.ppermute(down.astype(bf16), "fsdp", back).astype(f32)
        if step == far:
            break
        if step == 1:
            up = jnp.concatenate(
                [take(far - 1, 0, half) + up, take(far - 1, half, rows - half)]
            )
            down = jnp.concatenate(
                [take(1 - far, 0, half), take(1 - far, half, rows - half) + down]
            )
        else:
            up = up + take(far - step, 0, rows)
            down = down + take(step - far, 0, rows)
    return take(0, 0, rows) + up + down


def attend_forward(queries, keys, values, scale_val):
    rows = queries.shape[0]
    heads = queries.shape[1] // HEAD
    q = queries.reshape(rows, heads, HEAD)
    k = keys.reshape(rows, heads, HEAD)
    v = values.reshape(rows, heads, HEAD)
    scores = jnp.einsum("qhd,khd->hqk", q, k, preferred_element_type=f32) * scale_val
    top_val = jnp.max(scores, axis=-1, keepdims=True)
    expd_val = jnp.exp(scores - top_val)
    totals = jnp.sum(expd_val, axis=-1, keepdims=True)
    probs = (expd_val / totals).astype(bf16)
    out = jnp.einsum("hqk,khd->qhd", probs, v, preferred_element_type=f32)
    return out.astype(bf16).reshape(rows, heads * HEAD), (top_val + jnp.log(totals))


def attend_backward(queries, keys, values, grad, lse, scale_val):
    rows = queries.shape[0]
    heads = queries.shape[1] // HEAD
    q, k, v, g = (a.reshape(rows, heads, HEAD) for a in (queries, keys, values, grad))
    scores = jnp.einsum("qhd,khd->hqk", q, k, preferred_element_type=f32) * scale_val
    probs = jnp.exp(scores - lse)
    grad_probs = jnp.einsum("qhd,khd->hqk", g, v, preferred_element_type=f32)
    inner = jnp.sum(probs * grad_probs, axis=-1, keepdims=True)
    grad_scores = (probs * (grad_probs - inner)).astype(bf16)
    grad_q = jnp.einsum("hqk,khd->qhd", grad_scores, k, preferred_element_type=f32) * scale_val
    grad_k = jnp.einsum("hqk,qhd->khd", grad_scores, q, preferred_element_type=f32) * scale_val
    grad_v = jnp.einsum("hqk,qhd->khd", probs.astype(bf16), g, preferred_element_type=f32)
    flat = heads * HEAD
    return [a.astype(bf16).reshape(rows, flat) for a in (grad_q, grad_k, grad_v)]


def local_wide(
    latents_in,
    conditions,
    w_ada,
    b_ada,
    w_qkv,
    b_qv,
    w_proj,
    b_proj,
    w_fc1,
    b_fc1,
    w_fc2,
    b_fc2,
    out_grad,
):
    width = latents_in.shape[2]
    tokens = latents_in.shape[1]
    seq_count = lax.axis_size("seq")
    owners = lax.axis_size("fsdp")
    me = lax.axis_index("fsdp")
    place = lax.axis_index("seq")
    core = place % 2
    own_rows = w_ada.shape[0]
    quarter = width // seq_count
    units = w_fc2.shape[0] // 2
    scale_val = HEAD ** (-0.5)

    condition = conditions[0]
    cond_act, silu_pull = jax.vjp(jax.nn.silu, condition)
    cond_low = cond_act.astype(bf16)
    small = jnp.concatenate([cond_low, b_qv, b_proj, b_fc1, b_fc2])
    small_rel = gather_small(small, me)
    cond_rows = lax.dynamic_slice_in_dim(small_rel, me * own_rows, own_rows, 1)
    mod_partial = dot(cond_rows, w_ada, ((1,), (0,)))
    bias_at = b_ada.shape[0]
    placed_bias = jnp.where(
        jnp.arange(owners)[:, None] == me, b_ada.astype(f32)[None, :], 0.0
    ).reshape(1, owners * bias_at)
    mod_partial = mod_partial + placed_bias
    modulation = jnp.sum(deal_small(mod_partial, me), axis=0)
    shift_one, scale_one, gate_one, shift_two, scale_two, gate_two = jnp.split(modulation, 6)

    bias_rel = small_rel[:, width:].astype(f32)
    bias_all = rolled(bias_rel[::-1], jnp.mod(me + 1, owners))
    at = 0
    biases = []
    for b in (b_qv, b_proj, b_fc1, b_fc2):
        biases.append(bias_all[:, at : at + b.shape[0]])
        at += b.shape[0]
    qv_full = biases[0].reshape(2, seq_count, quarter)
    bias_q, bias_v = lax.dynamic_index_in_dim(qv_full, place, 1, keepdims=False)
    bias_proj = biases[1].reshape(width)
    bias_fc1 = lax.dynamic_index_in_dim(
        biases[2].reshape(owners, 2, units), core, 1, keepdims=False
    ).reshape(owners * units)
    bias_fc2 = biases[3].reshape(width)

    mine_qkv = lax.dynamic_index_in_dim(
        w_qkv.reshape(own_rows, 3, seq_count, quarter), place, 2, keepdims=False
    ).reshape(own_rows, 3 * quarter)
    use_qkv = ring_gather(mine_qkv, me)
    mine_proj = lax.dynamic_slice_in_dim(w_proj, core * (width // 2), width // 2, 1)
    proj_half = ring_gather(mine_proj, me)
    proj_other = swap_core(proj_half)
    full_proj = jnp.where(
        core == 0,
        jnp.concatenate([proj_half, proj_other], axis=1),
        jnp.concatenate([proj_other, proj_half], axis=1),
    )
    use_proj = jnp.concatenate(
        [
            lax.dynamic_slice_in_dim(full_proj, (place ^ k) * quarter, quarter, 0)
            for k in range(seq_count)
        ]
    )
    mine_fc1 = lax.dynamic_index_in_dim(
        w_fc1.reshape(own_rows, owners, 2, units), core, 2, keepdims=False
    ).reshape(own_rows, owners * units)
    use_fc1 = ring_gather(mine_fc1, me)
    mine_fc2 = lax.dynamic_slice_in_dim(w_fc2, core * units, units, 0)
    use_fc2 = ring_gather(mine_fc2, me)

    own_latent = latents_in[0]
    from_x = swap_x(own_latent)
    from_core = swap_core(own_latent)
    from_both = swap_core(from_x)
    all_latent = jnp.concatenate([own_latent, from_core, from_x, from_both]).astype(f32)
    latent = own_latent.astype(f32)
    grad_own = out_grad[0]
    grad_pair = jnp.concatenate([grad_own, swap_core(grad_own)]).astype(f32)
    grad_out = grad_own.astype(f32)

    normed_all = layer_norm(all_latent)
    act_one = (normed_all * (1.0 + scale_one) + shift_one).astype(bf16)
    bias_three = jnp.concatenate([bias_q, jnp.zeros_like(bias_q), bias_v])
    qkv = (dot(act_one, use_qkv, ((1,), (0,))) + bias_three).astype(bf16)
    queries, keys, values = jnp.split(qkv, 3, axis=1)
    attn_heads, lse = attend_forward(queries, keys, values, scale_val)

    def to_tokens(blocks):
        return [blocks[0]] + [seq_swap(blocks[k], k) for k in range(1, seq_count)]

    attn_own = jnp.concatenate(
        to_tokens([attn_heads[k * tokens : (k + 1) * tokens] for k in range(seq_count)]), axis=1
    )
    branch_one = dot(attn_own, use_proj, ((1,), (0,))) + bias_proj
    middle = latent + gate_one * branch_one
    normed_two, norm_pull_two = jax.vjp(layer_norm, middle)
    act_two_own = (normed_two * (1.0 + scale_two) + shift_two).astype(bf16)

    act_two = jnp.concatenate([act_two_own, swap_core(act_two_own)])
    hidden_pre = dot(act_two, use_fc1, ((1,), (0,))) + bias_fc1
    hidden_act, gelu_pull = jax.vjp(gelu_tanh, hidden_pre)
    hidden_low = hidden_act.astype(bf16)
    grad_two = (gate_two * grad_pair).astype(bf16)
    grad_hidden = dot(grad_two, use_fc2, ((1,), (1,)))
    grad_pre = gelu_pull(grad_hidden)[0].astype(bf16)
    partial_act = dot(grad_pre, use_fc1, ((1,), (1,)))
    grad_act_two = partial_act[:tokens] + swap_core(partial_act[tokens:])
    grad_shift_two = jnp.sum(grad_act_two, axis=0)
    grad_scale_two = jnp.sum(grad_act_two * normed_two, axis=0)
    grad_middle = grad_out + norm_pull_two(grad_act_two * (1.0 + scale_two))[0]
    grad_one = (gate_one * grad_middle).astype(bf16)
    grad_gate_one = jnp.sum(grad_middle * branch_one, axis=0)
    grad_attn = dot(grad_one, use_proj, ((1,), (1,))).astype(bf16)
    grad_heads = jnp.concatenate(
        to_tokens([grad_attn[:, k * quarter : (k + 1) * quarter] for k in range(seq_count)])
    )

    partial_two = dot(hidden_low, use_fc2, ((1,), (0,)))
    branch_two = partial_two[:tokens] + swap_core(partial_two[tokens:]) + bias_fc2
    result = middle + gate_two * branch_two
    grad_gate_two = jnp.sum(grad_out * branch_two, axis=0)
    grad_b_fc2 = jnp.sum(grad_two[:tokens].astype(f32), axis=0)
    grad_b_fc1 = jnp.sum(grad_pre.astype(f32), axis=0)
    grad_b_proj = jnp.sum(grad_one.astype(f32), axis=0)

    red_fc2 = ring_reduce(dot(hidden_low, grad_two, ((0,), (0,))).astype(bf16), me)
    red_fc1 = ring_reduce(dot(act_two, grad_pre, ((0,), (0,))).astype(bf16), me)

    def add_x(block):
        low = block.astype(bf16)
        return low.astype(f32) + swap_x(low).astype(f32)

    def in_core_order(block):
        other = swap_core(block)
        return jnp.where(core == 0, block, other), jnp.where(core == 0, other, block)

    grad_w_fc2 = jnp.concatenate(in_core_order(add_x(red_fc2)))
    first_fc1, second_fc1 = in_core_order(add_x(red_fc1))
    grad_w_fc1 = jnp.concatenate(
        [first_fc1.reshape(own_rows, owners, 1, units), second_fc1.reshape(own_rows, owners, 1, units)],
        axis=2,
    ).reshape(own_rows, 2 * owners * units)

    proj_rel = dot(attn_own, grad_one, ((0,), (0,))).astype(bf16)
    proj_abs = jnp.concatenate(
        [
            lax.dynamic_slice_in_dim(proj_rel, (place ^ k) * quarter, quarter, 0)
            for k in range(seq_count)
        ]
    )
    half_width = width // 2
    keep = lax.dynamic_slice_in_dim(proj_abs, core * half_width, half_width, 1)
    give = lax.dynamic_slice_in_dim(proj_abs, (1 - core) * half_width, half_width, 1)
    proj_sum = (keep.astype(f32) + swap_core(give).astype(f32)).astype(bf16)
    grad_w_proj = jnp.concatenate(in_core_order(add_x(ring_reduce(proj_sum, me))), axis=1)

    grad_q, grad_k, grad_v = attend_backward(queries, keys, values, grad_heads, lse, scale_val)
    grad_qkv = jnp.concatenate([grad_q, grad_k, grad_v], axis=1)
    red_qkv = ring_reduce(dot(act_one, grad_qkv, ((0,), (0,))).astype(bf16), me).astype(bf16)
    across = swap_x(red_qkv)
    blocks = [red_qkv, swap_core(red_qkv), across, swap_core(across)]
    for bit in (1, 2):
        flip = (place & bit) != 0
        blocks = [jnp.where(flip, blocks[j ^ bit], blocks[j]) for j in range(seq_count)]
    grad_w_qkv = jnp.concatenate(
        [b.astype(f32).reshape(own_rows, 3, 1, quarter) for b in blocks], axis=2
    ).reshape(own_rows, 3 * width)

    partial_one = dot(grad_qkv, use_qkv, ((1,), (1,)))
    grad_shift_one = jnp.sum(partial_one, axis=0)
    grad_scale_one = jnp.sum(partial_one * normed_all, axis=0)
    far_low = partial_one[2 * tokens :].astype(bf16)
    far_sum = far_low[:tokens].astype(f32) + swap_core(far_low[tokens:]).astype(f32)
    near_low = partial_one[tokens : 2 * tokens].astype(bf16)
    near_sum = partial_one[:tokens] + swap_core(near_low).astype(f32)
    grad_act_one = near_sum + swap_x(far_sum.astype(bf16)).astype(f32)
    _, norm_pull_one = jax.vjp(layer_norm, latent)
    grad_latent = grad_middle + norm_pull_one(grad_act_one * (1.0 + scale_one))[0]

    grad_b_qv = jnp.where(
        jnp.arange(seq_count)[None, :, None] == place,
        jnp.stack(
            [jnp.sum(grad_q.astype(f32), axis=0), jnp.sum(grad_v.astype(f32), axis=0)]
        )[:, None, :],
        0.0,
    ).reshape(2 * width)
    placed_fc1 = jnp.where(
        jnp.arange(2)[None, :, None] == core, grad_b_fc1.reshape(owners, 1, units), 0.0
    ).reshape(2 * owners * units)
    terms = jnp.concatenate(
        [
            grad_shift_one,
            grad_scale_one,
            grad_gate_one,
            grad_shift_two,
            grad_scale_two,
            grad_gate_two,
            grad_b_qv,
            grad_b_proj,
            placed_fc1,
            grad_b_fc2,
        ]
    )
    sums = (terms + seq_swap(terms, 1)) + (seq_swap(terms, 2) + seq_swap(terms, 3))
    low_sums = sums.astype(bf16)
    grad_mod = low_sums[: 6 * width]
    at = 6 * width
    by_owner = []
    for b in (b_qv, b_proj, b_fc1, b_fc2):
        size = b.shape[0] * owners
        by_owner.append(low_sums[at : at + size].reshape(owners, b.shape[0]))
        at += size
    by_owner = jnp.concatenate(by_owner, axis=1)
    sent_bias = rolled(by_owner[::-1], jnp.mod(me + 1, owners))
    mail = jnp.concatenate(
        [jnp.broadcast_to(grad_mod[None, :], (owners, 6 * width)), sent_bias], axis=1
    )
    got = deal_small(mail, me)
    mod_rel = got[:, : 6 * width]
    bias_sums = jnp.sum(got[:, 6 * width :].astype(f32), axis=0)
    back_cond = jnp.concatenate([cond_rows[:1], cond_rows[1:][::-1]])
    owned_w_ada = dot(back_cond, mod_rel, ((0,), (0,)))
    owned_b_ada = jnp.sum(
        lax.dynamic_slice_in_dim(mod_rel, me * bias_at, bias_at, 1).astype(f32), axis=0
    )
    cond_partial = dot(mod_rel, w_ada, ((1,), (1,)))
    back_partial = jnp.concatenate([cond_partial[:1], cond_partial[1:][::-1]])
    cond_got = rolled(deal_small(back_partial, me), me)
    grad_cond = silu_pull(cond_got.reshape(width))[0]
    at = 0
    owned_bias = []
    for b in (b_qv, b_proj, b_fc1, b_fc2):
        owned_bias.append(bias_sums[at : at + b.shape[0]])
        at += b.shape[0]
    return (
        result.astype(bf16)[None],
        grad_latent[None],
        grad_cond[None],
        owned_w_ada,
        owned_b_ada,
        grad_w_qkv,
        owned_bias[0],
        grad_w_proj,
        owned_bias[1],
        grad_w_fc1,
        owned_bias[2],
        grad_w_fc2,
        owned_bias[3],
    )


def swap_f(values, bit):
    count = lax.axis_size("fsdp")
    return lax.ppermute(values, "fsdp", [(i, i ^ bit) for i in range(count)])


def cube_bits():
    return [1 << b for b in range(lax.axis_size("fsdp").bit_length() - 1)]


def cube_places():
    places = [0]
    for bit in reversed(cube_bits()):
        places = places + [r | bit for r in places]
    return places


def cube_gather(row):
    rows = row[None]
    for bit in reversed(cube_bits()):
        rows = jnp.concatenate([rows, swap_f(rows, bit)])
    return rows


def cube_sum(rows):
    for bit in cube_bits():
        half = rows.shape[0] // 2
        rows = rows[:half] + swap_f(rows[half:], bit)
    return rows[0]


def cube_deal(rows):
    count = rows.shape[0]
    done = 1
    for bit in cube_bits():
        parts = rows.reshape((done, 2, count // (2 * done)) + rows.shape[1:])
        got = swap_f(parts[:, 1], bit)
        rows = jnp.stack([parts[:, 0], got], axis=1).reshape(rows.shape)
        done *= 2
    return rows


def cube_to_order(rows, me):
    places = jnp.array(cube_places())
    count = rows.shape[0]
    hit = jnp.arange(count)[:, None] == jnp.bitwise_xor(places, me)[None, :]
    return jnp.sum(jnp.where(hit[:, :, None], rows[None], jnp.zeros_like(rows)[None]), axis=1)


SMEM = pl.BlockSpec(memory_space=pltpu.SMEM)
VMEM = pl.BlockSpec(memory_space=pltpu.VMEM)


def bytes_of(*arrays):
    return sum(a.size * a.dtype.itemsize for a in arrays)


def call_whole(body, outs, scalars, *arrays, flops=0):
    table = jnp.stack([jnp.asarray(s, jnp.int32) for s in scalars])
    return pl.pallas_call(
        body,
        out_shape=outs,
        in_specs=[SMEM] + [VMEM] * len(arrays),
        out_specs=jax.tree.map(lambda _: VMEM, outs),
        cost_estimate=pl.CostEstimate(
            flops=flops,
            bytes_accessed=bytes_of(*arrays) + bytes_of(*jax.tree.leaves(outs)),
            transcendentals=0,
        ),
    )(table, *arrays)


def shaped(rows, cols, dtype=bf16):
    return jax.ShapeDtypeStruct((rows, cols), dtype)


def pack_first(place, w_proj, w_qkv, seq_count):
    rows, width = w_proj.shape
    half = width // 2
    quarter = width // seq_count

    def body(at, proj, qkv, out):
        for s in range(seq_count):

            @pl.when(at[0] == s)
            def _(s=s):
                out[:, :half] = proj[:, (s % 2) * half : (s % 2 + 1) * half]
                for t in range(3):
                    to = half + t * quarter
                    start = t * width + s * quarter
                    out[:, to : to + quarter] = qkv[:, start : start + quarter]

    return call_whole(body, shaped(rows, half + 3 * quarter), [place], w_proj, w_qkv)


def pack_second(core, w_fc1, w_fc2, owners):
    rows = w_fc1.shape[0]
    width = w_fc2.shape[1]
    units = w_fc2.shape[0] // 2
    span = owners * units
    parts = units // rows

    def body(at, fc1, fc2, out):
        for c in range(2):

            @pl.when(at[0] == c)
            def _(c=c):
                for f in range(owners):
                    start = (2 * f + c) * units
                    out[:, f * units : (f + 1) * units] = fc1[:, start : start + units]
                for n in range(parts):
                    start = c * units + n * rows
                    to = span + n * width
                    out[:, to : to + width] = fc2[start : start + rows, :]

    return call_whole(body, shaped(rows, span + parts * width), [core], w_fc1, w_fc2)


def ring_pieces(block):
    count = lax.axis_size("fsdp")
    _, ahead, back = ring_tables(count)
    half = block.shape[0] // 2
    far = count // 2
    pieces = [(0, 0, block)]
    up = down = block
    for step in range(1, far + 1):
        if step == far:
            up, down = up[:half], down[half:]
        up = lax.ppermute(up, "fsdp", ahead)
        down = lax.ppermute(down, "fsdp", back)
        pieces.append((-step, 0, up))
        pieces.append((step, half if step == far else 0, down))
    return pieces


def assemble(pieces, layout, outs, me, rows):
    shifts = [first for _, first, _ in pieces]

    def body(at, *refs):
        ins, results = refs[: len(pieces)], refs[len(pieces) :]
        for n, (ref, shift) in enumerate(zip(ins, shifts)):
            size = ref.shape[0]
            for out, per, base, col, cols in layout:
                start = pl.multiple_of(at[n] * per + base + shift, 16)
                results[out][pl.ds(start, size), :] = ref[:, col : col + cols]

    return call_whole(
        body, outs, [ring_place(me, off) for off, _, _ in pieces], *[p for _, _, p in pieces]
    )


def mix_proj(place, own, other, seq_count):
    width, half = own.shape
    quarter = width // seq_count

    def body(at, mine, theirs, out):
        for s in range(seq_count):

            @pl.when(at[0] == s)
            def _(s=s):
                c = s % 2
                for k in range(seq_count):
                    src = slice((s ^ k) * quarter, ((s ^ k) + 1) * quarter)
                    dst = slice(k * quarter, (k + 1) * quarter)
                    out[dst, c * half : (c + 1) * half] = mine[src, :]
                    out[dst, (1 - c) * half : (2 - c) * half] = theirs[src, :]

    return call_whole(body, shaped(width, width), [place], own, other)


def split_proj(place, values, seq_count):
    width = values.shape[1]
    half = width // 2
    quarter = width // seq_count

    def body(at, ref, keep, give):
        for s in range(seq_count):

            @pl.when(at[0] == s)
            def _(s=s):
                c = s % 2
                for k in range(seq_count):
                    dst = slice((s ^ k) * quarter, ((s ^ k) + 1) * quarter)
                    src = slice(k * quarter, (k + 1) * quarter)
                    keep[dst, :] = ref[src, c * half : (c + 1) * half]
                    give[dst, :] = ref[src, (1 - c) * half : (2 - c) * half]

    return call_whole(body, (shaped(width, half), shaped(width, half)), [place], values)


def ring_sum(arrays, layout, me, rows):
    count = lax.axis_size("fsdp")
    _, ahead, back = ring_tables(count)
    half = rows // 2
    far = count // 2
    total = sum(cols for _, _, cols in layout)

    def step_call(kind, up_at, down_at, *got):
        def body(at, *refs):
            del at
            ups = refs[: len(arrays)]
            downs = refs[len(arrays) : 2 * len(arrays)]
            rest = refs[2 * len(arrays) :]
            col = 0
            for a, base, cols in layout:
                to = slice(col, col + cols)
                col += cols

                def own(blocks, lo, hi):
                    return blocks[a][base + lo : base + hi, :].astype(f32)

                if kind == "first":
                    rest[0][:, to] = ups[a][base : base + half, :]
                    rest[1][:, to] = downs[a][base + half : base + rows, :]
                elif kind == "second":
                    up, down, next_up, next_down = rest
                    next_up[:half, to] = (own(ups, 0, half) + up[:, to].astype(f32)).astype(bf16)
                    next_up[half:, to] = ups[a][base + half : base + rows, :]
                    next_down[:half, to] = downs[a][base : base + half, :]
                    next_down[half:, to] = (
                        own(downs, half, rows) + down[:, to].astype(f32)
                    ).astype(bf16)
                elif kind == "middle":
                    up, down, next_up, next_down = rest
                    next_up[:, to] = (own(ups, 0, rows) + up[:, to].astype(f32)).astype(bf16)
                    next_down[:, to] = (own(downs, 0, rows) + down[:, to].astype(f32)).astype(bf16)
                else:
                    up, down, out = rest
                    out[:, to] = (
                        own(ups, 0, rows) + up[:, to].astype(f32) + down[:, to].astype(f32)
                    ).astype(bf16)

        blocks = [(a.shape[0] // count, a.shape[1]) for a in arrays]
        up_specs = [pl.BlockSpec(b, lambda i, at: (at[0], 0)) for b in blocks]
        down_specs = [pl.BlockSpec(b, lambda i, at: (at[1], 0)) for b in blocks]
        got_specs = [pl.BlockSpec(g.shape, lambda i, at: (0, 0)) for g in got]
        size = half if kind == "first" else rows
        outs = [shaped(size, total)] * (1 if kind == "last" else 2)
        out_specs = [pl.BlockSpec((size, total), lambda i, at: (0, 0))] * len(outs)
        return pl.pallas_call(
            body,
            out_shape=outs,
            grid_spec=pltpu.PrefetchScalarGridSpec(
                num_scalar_prefetch=1,
                grid=(1,),
                in_specs=up_specs + down_specs + got_specs,
                out_specs=out_specs,
            ),
            cost_estimate=pl.CostEstimate(
                flops=4 * rows * total, bytes_accessed=12 * rows * total, transcendentals=0
            ),
        )(
            jnp.stack([jnp.asarray(up_at, jnp.int32), jnp.asarray(down_at, jnp.int32)]),
            *arrays,
            *arrays,
            *got,
        )

    far_at = ring_place(me, far)
    up, down = step_call("first", far_at, far_at)
    for step in range(1, far + 1):
        up = lax.ppermute(up, "fsdp", ahead)
        down = lax.ppermute(down, "fsdp", back)
        if step == far:
            break
        kind = "second" if step == 1 else "middle"
        up, down = step_call(kind, ring_place(me, far - step), ring_place(me, step - far), up, down)
    return step_call("last", ring_place(me, 0), ring_place(me, 0), up, down)[0]


def place_second(core, own, other, owners, rows, units, width):
    span = owners * units
    parts = units // rows

    def body(at, mine, theirs, fc1, fc2):
        for c in range(2):

            @pl.when(at[0] == c)
            def _(c=c):
                for ref, cc in ((mine, c), (theirs, 1 - c)):
                    for f in range(owners):
                        start = (2 * f + cc) * units
                        fc1[:, start : start + units] = ref[
                            :, f * units : (f + 1) * units
                        ].astype(f32)
                    for n in range(parts):
                        start = cc * units + n * rows
                        to = span + n * width
                        fc2[start : start + rows, :] = ref[:, to : to + width].astype(f32)

    outs = (shaped(rows, 2 * span, f32), shaped(2 * units, width, f32))
    return call_whole(body, outs, [core], own, other)


def place_first(place, blocks, sums, seq_count, width):
    rows = blocks[0].shape[0]
    half = width // 2
    quarter = width // seq_count

    def body(at, *refs):
        quarters, own, other, proj, qkv = refs[:seq_count], *refs[seq_count:]
        for s in range(seq_count):

            @pl.when(at[0] == s)
            def _(s=s):
                c = s % 2
                proj[:, c * half : (c + 1) * half] = own[...].astype(f32)
                proj[:, (1 - c) * half : (2 - c) * half] = other[...].astype(f32)
                for k in range(seq_count):
                    for t in range(3):
                        start = t * width + (s ^ k) * quarter
                        qkv[:, start : start + quarter] = quarters[k][
                            :, t * quarter : (t + 1) * quarter
                        ].astype(f32)

    outs = (shaped(rows, width, f32), shaped(rows, 3 * width, f32))
    return call_whole(body, outs, [place], *blocks, *sums)


def heads_forward(qkv, scale_val):
    length = qkv.shape[0]
    flat = qkv.shape[1] // 3
    heads = flat // HEAD
    block = min(256, length)

    def body(here, whole, out, lse):
        for h in range(heads):
            q = here[:, h * HEAD : (h + 1) * HEAD]
            q = (q.astype(f32) * scale_val).astype(bf16)
            k = whole[:, flat + h * HEAD : flat + (h + 1) * HEAD]
            v = whole[:, 2 * flat + h * HEAD : 2 * flat + (h + 1) * HEAD]
            scores = dot(k, q, ((1,), (1,)))
            top_val = jnp.max(scores, axis=0, keepdims=True)
            expd = jnp.exp(scores - top_val)
            totals = jnp.sum(expd, axis=0, keepdims=True)
            probs = (expd * (1.0 / totals)).astype(bf16)
            mixed = dot(v, probs, ((0,), (0,)))
            out[:, h * HEAD : (h + 1) * HEAD] = mixed.T.astype(bf16)
            lse[h : h + 1, :] = top_val + jnp.log(totals)

    return pl.pallas_call(
        body,
        grid=(length // block,),
        in_specs=[
            pl.BlockSpec((block, 3 * flat), lambda i: (i, 0)),
            pl.BlockSpec((length, 3 * flat), lambda i: (0, 0)),
        ],
        out_specs=[
            pl.BlockSpec((block, flat), lambda i: (i, 0)),
            pl.BlockSpec((heads, block), lambda i: (0, i)),
        ],
        out_shape=[shaped(length, flat), shaped(heads, length, f32)],
        cost_estimate=pl.CostEstimate(
            flops=4 * length * length * flat,
            bytes_accessed=8 * length * flat,
            transcendentals=heads * length * length,
        ),
    )(qkv, qkv)


def heads_backward(qkv, grad, lse, scale_val):
    length = qkv.shape[0]
    flat = qkv.shape[1] // 3
    heads = flat // HEAD
    block = min(256, length)
    steps = length // block

    def body(here, whole, grad_here, lse_here, out, sum_k, sum_v):
        i = pl.program_id(0)

        @pl.when(i == 0)
        def _():
            sum_k[...] = jnp.zeros_like(sum_k)
            sum_v[...] = jnp.zeros_like(sum_v)

        rows = pl.ds(pl.multiple_of(i * block, block), block)
        for h in range(heads):
            cols = slice(h * HEAD, (h + 1) * HEAD)
            q = here[:, cols]
            q = (q.astype(f32) * scale_val).astype(bf16)
            k = whole[:, flat + h * HEAD : flat + (h + 1) * HEAD]
            v = whole[:, 2 * flat + h * HEAD : 2 * flat + (h + 1) * HEAD]
            g = grad_here[:, cols]
            probs = jnp.exp(dot(k, q, ((1,), (1,))) - lse_here[h : h + 1, :])
            grad_probs = dot(v, g, ((1,), (1,)))
            inner = jnp.sum(probs * grad_probs, axis=0, keepdims=True)
            grad_scores = (probs * (grad_probs - inner)).astype(bf16)
            grad_q = dot(k, grad_scores, ((0,), (0,))) * scale_val
            out[rows, cols] = grad_q.T.astype(bf16)
            sum_k[:, cols] += dot(grad_scores, q, ((1,), (0,)))
            sum_v[:, cols] += dot(probs.astype(bf16), g, ((1,), (0,)))

        @pl.when(i == steps - 1)
        def _():
            out[:, flat : 2 * flat] = sum_k[...].astype(bf16)
            out[:, 2 * flat :] = sum_v[...].astype(bf16)

    return pl.pallas_call(
        body,
        grid=(steps,),
        in_specs=[
            pl.BlockSpec((block, 3 * flat), lambda i: (i, 0)),
            pl.BlockSpec((length, 3 * flat), lambda i: (0, 0)),
            pl.BlockSpec((block, flat), lambda i: (i, 0)),
            pl.BlockSpec((heads, block), lambda i: (0, i)),
        ],
        out_specs=pl.BlockSpec((length, 3 * flat), lambda i: (0, 0)),
        out_shape=shaped(length, 3 * flat),
        scratch_shapes=[pltpu.VMEM((length, flat), f32), pltpu.VMEM((length, flat), f32)],
        cost_estimate=pl.CostEstimate(
            flops=10 * length * length * flat,
            bytes_accessed=16 * length * flat,
            transcendentals=heads * length * length,
        ),
    )(qkv, qkv, grad, lse)


def local_ring(
    latents_in,
    conditions,
    w_ada,
    b_ada,
    w_qkv,
    b_qv,
    w_proj,
    b_proj,
    w_fc1,
    b_fc1,
    w_fc2,
    b_fc2,
    out_grad,
):
    width = latents_in.shape[2]
    tokens = latents_in.shape[1]
    seq_count = lax.axis_size("seq")
    owners = lax.axis_size("fsdp")
    me = lax.axis_index("fsdp")
    place = lax.axis_index("seq")
    core = place % 2
    own_rows = w_ada.shape[0]
    quarter = width // seq_count
    units = w_fc2.shape[0] // 2
    scale_val = HEAD ** (-0.5)

    condition = conditions[0]
    cond_act, silu_pull = jax.vjp(jax.nn.silu, condition)
    cond_low = cond_act.astype(bf16)
    small = jnp.concatenate([cond_low, b_qv, b_proj, b_fc1, b_fc2])
    small_rel = cube_gather(small)
    cond_rows = lax.dynamic_slice_in_dim(small_rel, me * own_rows, own_rows, 1)
    mod_partial = dot(cond_rows, w_ada, ((1,), (0,)))
    bias_at = b_ada.shape[0]
    owned = jnp.arange(owners)[:, None] == me
    placed_bias = jnp.where(owned, b_ada.astype(f32)[None, :], 0.0)
    mod_partial = mod_partial + placed_bias.reshape(1, owners * bias_at)
    modulation = cube_sum(mod_partial)
    shift_one, scale_one, gate_one, shift_two, scale_two, gate_two = jnp.split(modulation, 6)

    bias_all = cube_to_order(small_rel[:, width:], me).astype(f32)
    at = 0
    biases = []
    for b in (b_qv, b_proj, b_fc1, b_fc2):
        biases.append(bias_all[:, at : at + b.shape[0]])
        at += b.shape[0]
    qv_full = biases[0].reshape(2, seq_count, quarter)
    bias_q, bias_v = lax.dynamic_index_in_dim(qv_full, place, 1, keepdims=False)
    bias_proj = biases[1].reshape(width)
    bias_fc1 = lax.dynamic_index_in_dim(
        biases[2].reshape(owners, 2, units), core, 1, keepdims=False
    ).reshape(owners * units)
    bias_fc2 = biases[3].reshape(width)

    half_width = width // 2
    first = ring_pieces(pack_first(place, w_proj, w_qkv, seq_count))
    proj_half, use_qkv = assemble(
        first,
        [(0, own_rows, 0, 0, half_width), (1, own_rows, 0, half_width, 3 * quarter)],
        (shaped(width, half_width), shaped(width, 3 * quarter)),
        me,
        own_rows,
    )
    use_proj = mix_proj(place, proj_half, swap_core(proj_half), seq_count)
    span = owners * units
    parts = units // own_rows
    packed = pack_second(core, w_fc1, w_fc2, owners)
    packed, _ = lax.optimization_barrier((packed, first[-1][2]))
    use_fc1, use_fc2 = assemble(
        ring_pieces(packed),
        [(0, own_rows, 0, 0, span)]
        + [(1, units, n * own_rows, span + n * width, width) for n in range(parts)],
        (shaped(width, span), shaped(span, width)),
        me,
        own_rows,
    )

    own_latent = latents_in[0]
    from_x = swap_x(own_latent)
    from_core = swap_core(own_latent)
    from_both = swap_core(from_x)
    all_latent = jnp.concatenate([own_latent, from_core, from_x, from_both]).astype(f32)
    latent = own_latent.astype(f32)
    grad_own = out_grad[0]
    grad_pair = jnp.concatenate([grad_own, swap_core(grad_own)]).astype(f32)
    grad_out = grad_own.astype(f32)

    normed_all = layer_norm(all_latent)
    act_one = (normed_all * (1.0 + scale_one) + shift_one).astype(bf16)
    bias_three = jnp.concatenate([bias_q, jnp.zeros_like(bias_q), bias_v])
    qkv = (dot(act_one, use_qkv, ((1,), (0,))) + bias_three).astype(bf16)
    attn_heads, lse = heads_forward(qkv, scale_val)

    def to_tokens(blocks):
        return [blocks[0]] + [seq_swap(blocks[k], k) for k in range(1, seq_count)]

    attn_own = jnp.concatenate(
        to_tokens([attn_heads[k * tokens : (k + 1) * tokens] for k in range(seq_count)]), axis=1
    )
    branch_one = dot(attn_own, use_proj, ((1,), (0,))) + bias_proj
    middle = latent + gate_one * branch_one
    normed_two, norm_pull_two = jax.vjp(layer_norm, middle)
    act_two_own = (normed_two * (1.0 + scale_two) + shift_two).astype(bf16)

    act_two = jnp.concatenate([act_two_own, swap_core(act_two_own)])
    hidden_pre = dot(act_two, use_fc1, ((1,), (0,))) + bias_fc1
    hidden_act, gelu_pull = jax.vjp(gelu_tanh, hidden_pre)
    hidden_low = hidden_act.astype(bf16)
    grad_two = (gate_two * grad_pair).astype(bf16)
    grad_hidden = dot(grad_two, use_fc2, ((1,), (1,)))
    grad_pre = gelu_pull(grad_hidden)[0].astype(bf16)
    partial_act = dot(grad_pre, use_fc1, ((1,), (1,)))
    grad_act_two = partial_act[:tokens] + swap_core(partial_act[tokens:])
    grad_shift_two = jnp.sum(grad_act_two, axis=0)
    grad_scale_two = jnp.sum(grad_act_two * normed_two, axis=0)
    grad_middle = grad_out + norm_pull_two(grad_act_two * (1.0 + scale_two))[0]
    grad_one = (gate_one * grad_middle).astype(bf16)
    grad_gate_one = jnp.sum(grad_middle * branch_one, axis=0)
    grad_attn = dot(grad_one, use_proj, ((1,), (1,))).astype(bf16)
    grad_heads = jnp.concatenate(
        to_tokens([grad_attn[:, k * quarter : (k + 1) * quarter] for k in range(seq_count)])
    )

    partial_two = dot(hidden_low, use_fc2, ((1,), (0,)))
    branch_two = partial_two[:tokens] + swap_core(partial_two[tokens:]) + bias_fc2
    result = middle + gate_two * branch_two
    grad_gate_two = jnp.sum(grad_out * branch_two, axis=0)
    grad_b_fc2 = jnp.sum(grad_two[:tokens].astype(f32), axis=0)
    grad_b_fc1 = jnp.sum(grad_pre.astype(f32), axis=0)
    grad_b_proj = jnp.sum(grad_one.astype(f32), axis=0)

    def add_x(low):
        return (low.astype(f32) + swap_x(low).astype(f32)).astype(bf16)

    grad_fc1 = dot(act_two, grad_pre, ((0,), (0,))).astype(bf16)
    grad_fc2 = dot(hidden_low, grad_two, ((0,), (0,))).astype(bf16)
    second_sum = add_x(
        ring_sum(
            [grad_fc1, grad_fc2],
            [(0, 0, span)] + [(1, n * own_rows, width) for n in range(parts)],
            me,
            own_rows,
        )
    )
    grad_w_fc1, grad_w_fc2 = place_second(
        core, second_sum, swap_core(second_sum), owners, own_rows, units, width
    )

    proj_rel = dot(attn_own, grad_one, ((0,), (0,))).astype(bf16)
    keep, give = split_proj(place, proj_rel, seq_count)
    proj_sum = (keep.astype(f32) + swap_core(give).astype(f32)).astype(bf16)

    grad_qkv = heads_backward(qkv, grad_heads, lse, scale_val)
    grad_own_qkv = dot(act_one, grad_qkv, ((0,), (0,))).astype(bf16)
    tail = ring_sum(
        [proj_sum, grad_own_qkv], [(0, 0, half_width), (1, 0, 3 * quarter)], me, own_rows
    )
    tail_x = swap_x(tail)
    own_half = (tail[:, :half_width].astype(f32) + tail_x[:, :half_width].astype(f32)).astype(bf16)
    own_part, x_part = tail[:, half_width:], tail_x[:, half_width:]
    core_mail = swap_core(jnp.concatenate([own_half, own_part, x_part], axis=1))
    cut_at = half_width + 3 * quarter
    grad_w_proj, grad_w_qkv = place_first(
        place,
        [own_part, core_mail[:, half_width:cut_at], x_part, core_mail[:, cut_at:]],
        [own_half, core_mail[:, :half_width]],
        seq_count,
        width,
    )
    partial_one = dot(grad_qkv, use_qkv, ((1,), (1,)))
    grad_shift_one = jnp.sum(partial_one, axis=0)
    grad_scale_one = jnp.sum(partial_one * normed_all, axis=0)
    far_low = partial_one[2 * tokens :].astype(bf16)
    far_sum = far_low[:tokens].astype(f32) + swap_core(far_low[tokens:]).astype(f32)
    near_low = partial_one[tokens : 2 * tokens].astype(bf16)
    near_sum = partial_one[:tokens] + swap_core(near_low).astype(f32)
    grad_act_one = near_sum + swap_x(far_sum.astype(bf16)).astype(f32)
    _, norm_pull_one = jax.vjp(layer_norm, latent)
    grad_latent = grad_middle + norm_pull_one(grad_act_one * (1.0 + scale_one))[0]

    qkv_sums = jnp.sum(grad_qkv.astype(f32), axis=0).reshape(3, 1, quarter)
    grad_b_qv = jnp.where(
        jnp.arange(seq_count)[None, :, None] == place,
        jnp.concatenate([qkv_sums[:1], qkv_sums[2:]]),
        0.0,
    ).reshape(2 * width)
    placed_fc1 = jnp.where(
        jnp.arange(2)[None, :, None] == core, grad_b_fc1.reshape(owners, 1, units), 0.0
    ).reshape(2 * owners * units)
    terms = jnp.concatenate(
        [
            grad_shift_one,
            grad_scale_one,
            grad_gate_one,
            grad_shift_two,
            grad_scale_two,
            grad_gate_two,
            grad_b_qv,
            grad_b_proj,
            placed_fc1,
            grad_b_fc2,
        ]
    )
    sums = (terms + seq_swap(terms, 1)) + (seq_swap(terms, 2) + seq_swap(terms, 3))
    low_sums = sums.astype(bf16)
    got = cube_gather(low_sums)
    mod_rel = got[:, : 6 * width]
    all_sums = jnp.sum(got[:, 6 * width :].astype(f32), axis=0)
    owned_w_ada = dot(cond_rows, mod_rel, ((0,), (0,)))
    owned_b_ada = jnp.sum(
        lax.dynamic_slice_in_dim(mod_rel, me * bias_at, bias_at, 1).astype(f32), axis=0
    )
    cond_partial = dot(mod_rel, w_ada, ((1,), (1,)))
    cond_got = cube_to_order(cube_deal(cond_partial), me)
    grad_cond = silu_pull(cond_got.reshape(width))[0]
    at = 0
    owned_bias = []
    for b in (b_qv, b_proj, b_fc1, b_fc2):
        size = b.shape[0]
        owned_bias.append(lax.dynamic_slice_in_dim(all_sums, at + me * size, size, 0))
        at += size * owners
    return (
        result.astype(bf16)[None],
        grad_latent[None],
        grad_cond[None],
        owned_w_ada,
        owned_b_ada,
        grad_w_qkv,
        owned_bias[0],
        grad_w_proj,
        owned_bias[1],
        grad_w_fc1,
        owned_bias[2],
        grad_w_fc2,
        owned_bias[3],
    )


def local(*args):
    count = lax.axis_size("fsdp")
    short = count <= RING_MAX and count & (count - 1) == 0 and count > 2
    if short and lax.axis_size("seq") == 4 and args[2].shape[0] % 32 == 0:
        return local_ring(*args)
    return local_wide(*args)


def solution(mesh):
    return jax.shard_map(
        local,
        mesh=mesh,
        in_specs=(
            P("fsdp", "seq", None),
            P("fsdp", None),
            P("fsdp", None),
            P("fsdp"),
            P("fsdp", None),
            P("fsdp"),
            P("fsdp", None),
            P("fsdp"),
            P("fsdp", None),
            P("fsdp"),
            P("fsdp", None),
            P("fsdp"),
            P("fsdp", "seq", None),
        ),
        out_specs=(
            P("fsdp", "seq", None),
            P("fsdp", "seq", None),
            P("fsdp", None),
            P("fsdp", None),
            P("fsdp"),
            P("fsdp", None),
            P("fsdp"),
            P("fsdp", None),
            P("fsdp"),
            P("fsdp", None),
            P("fsdp"),
            P("fsdp", None),
            P("fsdp"),
        ),
        check_vma=False,
    )
```

```python
import functools

import jax
import jax.numpy as jnp
from jax import lax
from jax.experimental import pallas as pl
from jax.experimental.pallas import tpu as pltpu
from jax.sharding import PartitionSpec as P


HEAD = 64
RING_MAX = 16

norm_eps = 1e-06
f32 = jnp.float32
bf16 = jnp.bfloat16


def dot(a, b, dims):
    return lax.dot_general(a, b, (dims, ((), ())), preferred_element_type=f32)


def layer_norm(values):
    mean_val = jnp.mean(values, axis=-1, keepdims=True)
    centred = values - mean_val
    var_val = jnp.mean(centred * centred, axis=-1, keepdims=True)
    return centred * lax.rsqrt(var_val + norm_eps)


def gelu_tanh(values):
    return jax.nn.gelu(values, approximate=True)


def seq_swap(values, bit):
    count = lax.axis_size("seq")
    return lax.ppermute(values, "seq", [(i, i ^ bit) for i in range(count)])


swap_core = functools.partial(seq_swap, bit=1)
swap_x = functools.partial(seq_swap, bit=2)


def rolled(rows, shift):
    count = rows.shape[0]
    return lax.dynamic_slice_in_dim(jnp.concatenate([rows, rows]), count - shift, count, 0)


def gather_small(row, me):
    count = lax.axis_size("fsdp")
    if count > RING_MAX:
        rows = lax.all_gather(row, "fsdp", axis=0)
        return rolled(rows[::-1], jnp.mod(me + 1, count))
    got = [row]
    for r in range(1, count):
        got.append(lax.ppermute(row, "fsdp", [(i, (i + r) % count) for i in range(count)]))
    return jnp.stack(got)


def deal_small(rows, me):
    count = lax.axis_size("fsdp")
    if count > RING_MAX:
        placed = rolled(rows[::-1], jnp.mod(me + 1, count))
        got = lax.all_to_all(placed, "fsdp", split_axis=0, concat_axis=0, tiled=True)
        return rolled(got, jnp.mod(count - me, count))
    got = [rows[0]]
    for r in range(1, count):
        got.append(lax.ppermute(rows[r], "fsdp", [(i, (i - r) % count) for i in range(count)]))
    return jnp.stack(got)


def ring_tables(count):
    order = list(range(0, count, 2)) + list(range(count - 1, 0, -2))
    ahead = [(order[i], order[(i + 1) % count]) for i in range(count)]
    return order, ahead, [(b, a) for a, b in ahead]


def ring_place(me, offset):
    count = lax.axis_size("fsdp")
    mine = jnp.where(me % 2 == 0, me // 2, count - 1 - me // 2)
    place = jnp.mod(mine + offset + count, count)
    return jnp.where(place < count // 2, 2 * place, 2 * (count - 1 - place) + 1)


def ring_gather(block, me):
    count = lax.axis_size("fsdp")
    if count > RING_MAX:
        return lax.all_gather(block, "fsdp", axis=0, tiled=True)
    _, ahead, back = ring_tables(count)
    rows = block.shape[0]
    half = rows // 2
    far = count // 2
    out = jnp.zeros((rows * count,) + block.shape[1:], block.dtype)

    def put(out, piece, offset, shift):
        start = ring_place(me, offset) * rows + shift
        return lax.dynamic_update_slice_in_dim(out, piece, start, 0)

    out = put(out, block, 0, 0)
    up = down = block
    for step in range(1, far + 1):
        if step == far:
            up, down = up[:half], down[half:]
        up = lax.ppermute(up, "fsdp", ahead)
        down = lax.ppermute(down, "fsdp", back)
        out = put(out, up, -step, 0)
        out = put(out, down, step, half if step == far else 0)
    return out


def ring_reduce(values, me):
    count = lax.axis_size("fsdp")
    rows = values.shape[0] // count
    if count > RING_MAX:
        return lax.psum_scatter(
            values.astype(bf16), "fsdp", scatter_dimension=0, tiled=True
        ).astype(f32)
    _, ahead, back = ring_tables(count)
    half = rows // 2
    far = count // 2

    def take(offset, start, size):
        return lax.dynamic_slice_in_dim(
            values, ring_place(me, offset) * rows + start, size, 0
        ).astype(f32)

    up = take(far, 0, half)
    down = take(-far, half, half)
    for step in range(1, far + 1):
        up = lax.ppermute(up.astype(bf16), "fsdp", ahead).astype(f32)
        down = lax.ppermute(down.astype(bf16), "fsdp", back).astype(f32)
        if step == far:
            break
        if step == 1:
            up = jnp.concatenate(
                [take(far - 1, 0, half) + up, take(far - 1, half, rows - half)]
            )
            down = jnp.concatenate(
                [take(1 - far, 0, half), take(1 - far, half, rows - half) + down]
            )
        else:
            up = up + take(far - step, 0, rows)
            down = down + take(step - far, 0, rows)
    return take(0, 0, rows) + up + down


def attend_forward(queries, keys, values, scale_val):
    rows = queries.shape[0]
    heads = queries.shape[1] // HEAD
    q = queries.reshape(rows, heads, HEAD)
    k = keys.reshape(rows, heads, HEAD)
    v = values.reshape(rows, heads, HEAD)
    scores = jnp.einsum("qhd,khd->hqk", q, k, preferred_element_type=f32) * scale_val
    top_val = jnp.max(scores, axis=-1, keepdims=True)
    expd_val = jnp.exp(scores - top_val)
    totals = jnp.sum(expd_val, axis=-1, keepdims=True)
    probs = (expd_val / totals).astype(bf16)
    out = jnp.einsum("hqk,khd->qhd", probs, v, preferred_element_type=f32)
    return out.astype(bf16).reshape(rows, heads * HEAD), (top_val + jnp.log(totals))


def attend_backward(queries, keys, values, grad, lse, scale_val):
    rows = queries.shape[0]
    heads = queries.shape[1] // HEAD
    q, k, v, g = (a.reshape(rows, heads, HEAD) for a in (queries, keys, values, grad))
    scores = jnp.einsum("qhd,khd->hqk", q, k, preferred_element_type=f32) * scale_val
    probs = jnp.exp(scores - lse)
    grad_probs = jnp.einsum("qhd,khd->hqk", g, v, preferred_element_type=f32)
    inner = jnp.sum(probs * grad_probs, axis=-1, keepdims=True)
    grad_scores = (probs * (grad_probs - inner)).astype(bf16)
    grad_q = jnp.einsum("hqk,khd->qhd", grad_scores, k, preferred_element_type=f32) * scale_val
    grad_k = jnp.einsum("hqk,qhd->khd", grad_scores, q, preferred_element_type=f32) * scale_val
    grad_v = jnp.einsum("hqk,qhd->khd", probs.astype(bf16), g, preferred_element_type=f32)
    flat = heads * HEAD
    return [a.astype(bf16).reshape(rows, flat) for a in (grad_q, grad_k, grad_v)]


def local_wide(
    latents_in,
    conditions,
    w_ada,
    b_ada,
    w_qkv,
    b_qv,
    w_proj,
    b_proj,
    w_fc1,
    b_fc1,
    w_fc2,
    b_fc2,
    out_grad,
):
    width = latents_in.shape[2]
    tokens = latents_in.shape[1]
    seq_count = lax.axis_size("seq")
    owners = lax.axis_size("fsdp")
    me = lax.axis_index("fsdp")
    place = lax.axis_index("seq")
    core = place % 2
    own_rows = w_ada.shape[0]
    quarter = width // seq_count
    units = w_fc2.shape[0] // 2
    scale_val = HEAD ** (-0.5)

    condition = conditions[0]
    cond_act, silu_pull = jax.vjp(jax.nn.silu, condition)
    cond_low = cond_act.astype(bf16)
    small = jnp.concatenate([cond_low, b_qv, b_proj, b_fc1, b_fc2])
    small_rel = gather_small(small, me)
    cond_rows = lax.dynamic_slice_in_dim(small_rel, me * own_rows, own_rows, 1)
    mod_partial = dot(cond_rows, w_ada, ((1,), (0,)))
    bias_at = b_ada.shape[0]
    placed_bias = jnp.where(
        jnp.arange(owners)[:, None] == me, b_ada.astype(f32)[None, :], 0.0
    ).reshape(1, owners * bias_at)
    mod_partial = mod_partial + placed_bias
    modulation = jnp.sum(deal_small(mod_partial, me), axis=0)
    shift_one, scale_one, gate_one, shift_two, scale_two, gate_two = jnp.split(modulation, 6)

    bias_rel = small_rel[:, width:].astype(f32)
    bias_all = rolled(bias_rel[::-1], jnp.mod(me + 1, owners))
    at = 0
    biases = []
    for b in (b_qv, b_proj, b_fc1, b_fc2):
        biases.append(bias_all[:, at : at + b.shape[0]])
        at += b.shape[0]
    qv_full = biases[0].reshape(2, seq_count, quarter)
    bias_q, bias_v = lax.dynamic_index_in_dim(qv_full, place, 1, keepdims=False)
    bias_proj = biases[1].reshape(width)
    bias_fc1 = lax.dynamic_index_in_dim(
        biases[2].reshape(owners, 2, units), core, 1, keepdims=False
    ).reshape(owners * units)
    bias_fc2 = biases[3].reshape(width)

    mine_qkv = lax.dynamic_index_in_dim(
        w_qkv.reshape(own_rows, 3, seq_count, quarter), place, 2, keepdims=False
    ).reshape(own_rows, 3 * quarter)
    use_qkv = ring_gather(mine_qkv, me)
    mine_proj = lax.dynamic_slice_in_dim(w_proj, core * (width // 2), width // 2, 1)
    proj_half = ring_gather(mine_proj, me)
    proj_other = swap_core(proj_half)
    full_proj = jnp.where(
        core == 0,
        jnp.concatenate([proj_half, proj_other], axis=1),
        jnp.concatenate([proj_other, proj_half], axis=1),
    )
    use_proj = jnp.concatenate(
        [
            lax.dynamic_slice_in_dim(full_proj, (place ^ k) * quarter, quarter, 0)
            for k in range(seq_count)
        ]
    )
    mine_fc1 = lax.dynamic_index_in_dim(
        w_fc1.reshape(own_rows, owners, 2, units), core, 2, keepdims=False
    ).reshape(own_rows, owners * units)
    use_fc1 = ring_gather(mine_fc1, me)
    mine_fc2 = lax.dynamic_slice_in_dim(w_fc2, core * units, units, 0)
    use_fc2 = ring_gather(mine_fc2, me)

    own_latent = latents_in[0]
    from_x = swap_x(own_latent)
    from_core = swap_core(own_latent)
    from_both = swap_core(from_x)
    all_latent = jnp.concatenate([own_latent, from_core, from_x, from_both]).astype(f32)
    latent = own_latent.astype(f32)
    grad_own = out_grad[0]
    grad_pair = jnp.concatenate([grad_own, swap_core(grad_own)]).astype(f32)
    grad_out = grad_own.astype(f32)

    normed_all = layer_norm(all_latent)
    act_one = (normed_all * (1.0 + scale_one) + shift_one).astype(bf16)
    bias_three = jnp.concatenate([bias_q, jnp.zeros_like(bias_q), bias_v])
    qkv = (dot(act_one, use_qkv, ((1,), (0,))) + bias_three).astype(bf16)
    queries, keys, values = jnp.split(qkv, 3, axis=1)
    attn_heads, lse = attend_forward(queries, keys, values, scale_val)

    def to_tokens(blocks):
        return [blocks[0]] + [seq_swap(blocks[k], k) for k in range(1, seq_count)]

    attn_own = jnp.concatenate(
        to_tokens([attn_heads[k * tokens : (k + 1) * tokens] for k in range(seq_count)]), axis=1
    )
    branch_one = dot(attn_own, use_proj, ((1,), (0,))) + bias_proj
    middle = latent + gate_one * branch_one
    normed_two, norm_pull_two = jax.vjp(layer_norm, middle)
    act_two_own = (normed_two * (1.0 + scale_two) + shift_two).astype(bf16)

    act_two = jnp.concatenate([act_two_own, swap_core(act_two_own)])
    hidden_pre = dot(act_two, use_fc1, ((1,), (0,))) + bias_fc1
    hidden_act, gelu_pull = jax.vjp(gelu_tanh, hidden_pre)
    hidden_low = hidden_act.astype(bf16)
    grad_two = (gate_two * grad_pair).astype(bf16)
    grad_hidden = dot(grad_two, use_fc2, ((1,), (1,)))
    grad_pre = gelu_pull(grad_hidden)[0].astype(bf16)
    partial_act = dot(grad_pre, use_fc1, ((1,), (1,)))
    grad_act_two = partial_act[:tokens] + swap_core(partial_act[tokens:])
    grad_shift_two = jnp.sum(grad_act_two, axis=0)
    grad_scale_two = jnp.sum(grad_act_two * normed_two, axis=0)
    grad_middle = grad_out + norm_pull_two(grad_act_two * (1.0 + scale_two))[0]
    grad_one = (gate_one * grad_middle).astype(bf16)
    grad_gate_one = jnp.sum(grad_middle * branch_one, axis=0)
    grad_attn = dot(grad_one, use_proj, ((1,), (1,))).astype(bf16)
    grad_heads = jnp.concatenate(
        to_tokens([grad_attn[:, k * quarter : (k + 1) * quarter] for k in range(seq_count)])
    )

    partial_two = dot(hidden_low, use_fc2, ((1,), (0,)))
    branch_two = partial_two[:tokens] + swap_core(partial_two[tokens:]) + bias_fc2
    result = middle + gate_two * branch_two
    grad_gate_two = jnp.sum(grad_out * branch_two, axis=0)
    grad_b_fc2 = jnp.sum(grad_two[:tokens].astype(f32), axis=0)
    grad_b_fc1 = jnp.sum(grad_pre.astype(f32), axis=0)
    grad_b_proj = jnp.sum(grad_one.astype(f32), axis=0)

    red_fc2 = ring_reduce(dot(hidden_low, grad_two, ((0,), (0,))).astype(bf16), me)
    red_fc1 = ring_reduce(dot(act_two, grad_pre, ((0,), (0,))).astype(bf16), me)

    def add_x(block):
        low = block.astype(bf16)
        return low.astype(f32) + swap_x(low).astype(f32)

    def in_core_order(block):
        other = swap_core(block)
        return jnp.where(core == 0, block, other), jnp.where(core == 0, other, block)

    grad_w_fc2 = jnp.concatenate(in_core_order(add_x(red_fc2)))
    first_fc1, second_fc1 = in_core_order(add_x(red_fc1))
    grad_w_fc1 = jnp.concatenate(
        [first_fc1.reshape(own_rows, owners, 1, units), second_fc1.reshape(own_rows, owners, 1, units)],
        axis=2,
    ).reshape(own_rows, 2 * owners * units)

    proj_rel = dot(attn_own, grad_one, ((0,), (0,))).astype(bf16)
    proj_abs = jnp.concatenate(
        [
            lax.dynamic_slice_in_dim(proj_rel, (place ^ k) * quarter, quarter, 0)
            for k in range(seq_count)
        ]
    )
    half_width = width // 2
    keep = lax.dynamic_slice_in_dim(proj_abs, core * half_width, half_width, 1)
    give = lax.dynamic_slice_in_dim(proj_abs, (1 - core) * half_width, half_width, 1)
    proj_sum = (keep.astype(f32) + swap_core(give).astype(f32)).astype(bf16)
    grad_w_proj = jnp.concatenate(in_core_order(add_x(ring_reduce(proj_sum, me))), axis=1)

    grad_q, grad_k, grad_v = attend_backward(queries, keys, values, grad_heads, lse, scale_val)
    grad_qkv = jnp.concatenate([grad_q, grad_k, grad_v], axis=1)
    red_qkv = ring_reduce(dot(act_one, grad_qkv, ((0,), (0,))).astype(bf16), me).astype(bf16)
    across = swap_x(red_qkv)
    blocks = [red_qkv, swap_core(red_qkv), across, swap_core(across)]
    for bit in (1, 2):
        flip = (place & bit) != 0
        blocks = [jnp.where(flip, blocks[j ^ bit], blocks[j]) for j in range(seq_count)]
    grad_w_qkv = jnp.concatenate(
        [b.astype(f32).reshape(own_rows, 3, 1, quarter) for b in blocks], axis=2
    ).reshape(own_rows, 3 * width)

    partial_one = dot(grad_qkv, use_qkv, ((1,), (1,)))
    grad_shift_one = jnp.sum(partial_one, axis=0)
    grad_scale_one = jnp.sum(partial_one * normed_all, axis=0)
    far_low = partial_one[2 * tokens :].astype(bf16)
    far_sum = far_low[:tokens].astype(f32) + swap_core(far_low[tokens:]).astype(f32)
    near_low = partial_one[tokens : 2 * tokens].astype(bf16)
    near_sum = partial_one[:tokens] + swap_core(near_low).astype(f32)
    grad_act_one = near_sum + swap_x(far_sum.astype(bf16)).astype(f32)
    _, norm_pull_one = jax.vjp(layer_norm, latent)
    grad_latent = grad_middle + norm_pull_one(grad_act_one * (1.0 + scale_one))[0]

    grad_b_qv = jnp.where(
        jnp.arange(seq_count)[None, :, None] == place,
        jnp.stack(
            [jnp.sum(grad_q.astype(f32), axis=0), jnp.sum(grad_v.astype(f32), axis=0)]
        )[:, None, :],
        0.0,
    ).reshape(2 * width)
    placed_fc1 = jnp.where(
        jnp.arange(2)[None, :, None] == core, grad_b_fc1.reshape(owners, 1, units), 0.0
    ).reshape(2 * owners * units)
    terms = jnp.concatenate(
        [
            grad_shift_one,
            grad_scale_one,
            grad_gate_one,
            grad_shift_two,
            grad_scale_two,
            grad_gate_two,
            grad_b_qv,
            grad_b_proj,
            placed_fc1,
            grad_b_fc2,
        ]
    )
    sums = (terms + seq_swap(terms, 1)) + (seq_swap(terms, 2) + seq_swap(terms, 3))
    low_sums = sums.astype(bf16)
    grad_mod = low_sums[: 6 * width]
    at = 6 * width
    by_owner = []
    for b in (b_qv, b_proj, b_fc1, b_fc2):
        size = b.shape[0] * owners
        by_owner.append(low_sums[at : at + size].reshape(owners, b.shape[0]))
        at += size
    by_owner = jnp.concatenate(by_owner, axis=1)
    sent_bias = rolled(by_owner[::-1], jnp.mod(me + 1, owners))
    mail = jnp.concatenate(
        [jnp.broadcast_to(grad_mod[None, :], (owners, 6 * width)), sent_bias], axis=1
    )
    got = deal_small(mail, me)
    mod_rel = got[:, : 6 * width]
    bias_sums = jnp.sum(got[:, 6 * width :].astype(f32), axis=0)
    back_cond = jnp.concatenate([cond_rows[:1], cond_rows[1:][::-1]])
    owned_w_ada = dot(back_cond, mod_rel, ((0,), (0,)))
    owned_b_ada = jnp.sum(
        lax.dynamic_slice_in_dim(mod_rel, me * bias_at, bias_at, 1).astype(f32), axis=0
    )
    cond_partial = dot(mod_rel, w_ada, ((1,), (1,)))
    back_partial = jnp.concatenate([cond_partial[:1], cond_partial[1:][::-1]])
    cond_got = rolled(deal_small(back_partial, me), me)
    grad_cond = silu_pull(cond_got.reshape(width))[0]
    at = 0
    owned_bias = []
    for b in (b_qv, b_proj, b_fc1, b_fc2):
        owned_bias.append(bias_sums[at : at + b.shape[0]])
        at += b.shape[0]
    return (
        result.astype(bf16)[None],
        grad_latent[None],
        grad_cond[None],
        owned_w_ada,
        owned_b_ada,
        grad_w_qkv,
        owned_bias[0],
        grad_w_proj,
        owned_bias[1],
        grad_w_fc1,
        owned_bias[2],
        grad_w_fc2,
        owned_bias[3],
    )


def swap_f(values, bit):
    count = lax.axis_size("fsdp")
    return lax.ppermute(values, "fsdp", [(i, i ^ bit) for i in range(count)])


def cube_bits():
    return [1 << b for b in range(lax.axis_size("fsdp").bit_length() - 1)]


def cube_places():
    places = [0]
    for bit in reversed(cube_bits()):
        places = places + [r | bit for r in places]
    return places


def cube_gather(row):
    rows = row
    for bit in reversed(cube_bits()):
        got = swap_f(rows, bit)
        rows = jnp.concatenate([rows, got])
    return rows


def cube_sum(rows):
    for bit in cube_bits():
        half = rows.shape[0] // 2
        got = swap_f(rows[half:], bit)
        rows = rows[:half] + got
    return rows[0]


def cube_deal(rows):
    count = rows.shape[0]
    done = 1
    for bit in cube_bits():
        parts = rows.reshape((done, 2, count // (2 * done)) + rows.shape[1:])
        got = swap_f(parts[:, 1], bit)
        rows = jnp.stack([parts[:, 0], got], axis=1).reshape(rows.shape)
        done *= 2
    return rows


def cube_to_order(rows, me):
    places = jnp.array(cube_places())
    count = rows.shape[0]
    hit = jnp.arange(count)[:, None] == jnp.bitwise_xor(places, me)[None, :]
    return jnp.sum(jnp.where(hit[:, :, None], rows[None], jnp.zeros_like(rows)[None]), axis=1)


SMEM = pl.BlockSpec(memory_space=pltpu.SMEM)
VMEM = pl.BlockSpec(memory_space=pltpu.VMEM)


def bytes_of(*arrays):
    return sum(a.size * a.dtype.itemsize for a in arrays)


def call_whole(body, outs, table, *arrays):
    return pl.pallas_call(
        body,
        out_shape=outs,
        in_specs=[SMEM] + [VMEM] * len(arrays),
        out_specs=jax.tree.map(lambda _: VMEM, outs),
        cost_estimate=pl.CostEstimate(
            flops=0,
            bytes_accessed=bytes_of(*arrays) + bytes_of(*jax.tree.leaves(outs)),
            transcendentals=0,
        ),
    )(table, *arrays)


def shaped(rows, cols, dtype=bf16):
    return jax.ShapeDtypeStruct((rows, cols), dtype)


def make_table(place, me):
    count = lax.axis_size("fsdp")
    around = [ring_place(me, off) for off in range(count)]
    return jnp.stack([jnp.asarray(v, jnp.int32) for v in [place] + around])


def along(at, offset, count):
    return at[1 + offset % count]


def pack_first(table, w_proj, w_qkv, seq_count):
    rows, width = w_proj.shape
    half = width // 2
    quarter = width // seq_count

    def body(at, proj, qkv, out):
        for s in range(seq_count):

            @pl.when(at[0] == s)
            def _(s=s):
                out[:, :half] = proj[:, (s % 2) * half : (s % 2 + 1) * half]
                for t in range(3):
                    to = half + t * quarter
                    start = t * width + s * quarter
                    out[:, to : to + quarter] = qkv[:, start : start + quarter]

    outs = shaped(rows, half + 3 * quarter)
    return call_whole(body, outs, table, w_proj, w_qkv)


def pack_second(table, w_fc1, w_fc2, owners):
    rows = w_fc1.shape[0]
    width = w_fc2.shape[1]
    units = w_fc2.shape[0] // 2
    span = owners * units
    parts = units // rows

    def body(at, fc1, fc2, out):
        for c in range(2):

            @pl.when(at[0] % 2 == c)
            def _(c=c):
                for f in range(owners):
                    start = (2 * f + c) * units
                    out[:, f * units : (f + 1) * units] = fc1[:, start : start + units]
                for n in range(parts):
                    start = c * units + n * rows
                    to = span + n * width
                    out[:, to : to + width] = fc2[start : start + rows, :]

    outs = shaped(rows, span + parts * width)
    return call_whole(body, outs, table, w_fc1, w_fc2)


def ring_pieces(block):
    count = lax.axis_size("fsdp")
    _, ahead, back = ring_tables(count)
    half = block.shape[0] // 2
    far = count // 2
    pieces = [(0, 0, block)]
    up = down = block
    for step in range(1, far + 1):
        if step == far:
            up, down = up[:half], down[half:]
        up = lax.ppermute(up, "fsdp", ahead)
        down = lax.ppermute(down, "fsdp", back)
        pieces.append((-step, 0, up))
        pieces.append((step, half if step == far else 0, down))
    return pieces


def assemble(pieces, layout, outs, table):
    count = lax.axis_size("fsdp")
    offsets = [off for off, _, _ in pieces]
    shifts = [first for _, first, _ in pieces]

    def body(at, *refs):
        ins, results = refs[: len(pieces)], refs[len(pieces) :]
        for ref, off, shift in zip(ins, offsets, shifts):
            size = ref.shape[0]
            owner = along(at, off, count)
            for out, per, base, col, cols in layout:
                start = pl.multiple_of(owner * per + base + shift, 16)
                results[out][pl.ds(start, size), :] = ref[:, col : col + cols]

    return call_whole(body, outs, table, *[p for _, _, p in pieces])


def mix_proj(table, own, other, seq_count):
    width, half = own.shape
    quarter = width // seq_count

    def body(at, mine, theirs, out):
        for s in range(seq_count):

            @pl.when(at[0] == s)
            def _(s=s):
                c = s % 2
                for k in range(seq_count):
                    src = slice((s ^ k) * quarter, ((s ^ k) + 1) * quarter)
                    dst = slice(k * quarter, (k + 1) * quarter)
                    out[dst, c * half : (c + 1) * half] = mine[src, :]
                    out[dst, (1 - c) * half : (2 - c) * half] = theirs[src, :]

    return call_whole(body, shaped(width, width), table, own, other)


def split_proj(table, values, seq_count):
    width = values.shape[1]
    half = width // 2
    quarter = width // seq_count

    def body(at, ref, keep, give):
        for s in range(seq_count):

            @pl.when(at[0] == s)
            def _(s=s):
                c = s % 2
                for k in range(seq_count):
                    dst = slice((s ^ k) * quarter, ((s ^ k) + 1) * quarter)
                    src = slice(k * quarter, (k + 1) * quarter)
                    keep[dst, :] = ref[src, c * half : (c + 1) * half]
                    give[dst, :] = ref[src, (1 - c) * half : (2 - c) * half]

    return call_whole(body, (shaped(width, half), shaped(width, half)), table, values)


def ring_sum(arrays, layout, table, rows):
    count = lax.axis_size("fsdp")
    _, ahead, back = ring_tables(count)
    half = rows // 2
    far = count // 2
    total = sum(cols for _, _, cols in layout)

    def step_call(step, *got):
        def body(at, *refs):
            blocks, rest = refs[: len(arrays)], refs[len(arrays) :]
            up_at, down_at = along(at, far - step, count), along(at, step - far, count)
            col = 0
            for a, base, cols in layout:
                to = slice(col, col + cols)
                col += cols
                per = blocks[a].shape[0] // count

                def own(owner, lo, hi):
                    start = pl.multiple_of(owner * per + base + lo, 16)
                    return blocks[a][pl.ds(start, hi - lo), :]

                def plus(owner, ref, lo, hi):
                    return (own(owner, lo, hi).astype(f32) + ref[:, to].astype(f32)).astype(bf16)

                if step == 0:
                    rest[0][:, to] = own(up_at, 0, half)
                    rest[1][:, to] = own(down_at, half, rows)
                elif step == far:
                    up, down, out = rest
                    out[:, to] = (
                        own(up_at, 0, rows).astype(f32)
                        + up[:, to].astype(f32)
                        + down[:, to].astype(f32)
                    ).astype(bf16)
                else:
                    up, down, next_up, next_down = rest
                    if step == 1:
                        next_up[:half, to] = plus(up_at, up, 0, half)
                        next_up[half:, to] = own(up_at, half, rows)
                        next_down[:half, to] = own(down_at, 0, half)
                        next_down[half:, to] = plus(down_at, down, half, rows)
                    else:
                        next_up[:, to] = plus(up_at, up, 0, rows)
                        next_down[:, to] = plus(down_at, down, 0, rows)

        out = shaped(half if step == 0 else rows, total)
        outs = out if step == far else (out, out)
        return call_whole(body, outs, table, *arrays, *got)

    up, down = step_call(0)
    for step in range(1, far + 1):
        up = lax.ppermute(up, "fsdp", ahead)
        down = lax.ppermute(down, "fsdp", back)
        if step < far:
            up, down = step_call(step, up, down)
    return step_call(far, up, down)


def place_second(table, own, other, owners, rows, units, width):
    span = owners * units
    parts = units // rows

    def body(at, mine, theirs, fc1, fc2):
        for c in range(2):

            @pl.when(at[0] % 2 == c)
            def _(c=c):
                for ref, cc in ((mine, c), (theirs, 1 - c)):
                    for f in range(owners):
                        start = (2 * f + cc) * units
                        fc1[:, start : start + units] = ref[
                            :, f * units : (f + 1) * units
                        ].astype(f32)
                    for n in range(parts):
                        start = cc * units + n * rows
                        to = span + n * width
                        fc2[start : start + rows, :] = ref[:, to : to + width].astype(f32)

    outs = (shaped(rows, 2 * span, f32), shaped(2 * units, width, f32))
    return call_whole(body, outs, table, own, other)


def place_first(table, own, across, sums, near, seq_count, width):
    rows = own.shape[0]
    half = width // 2
    quarter = width // seq_count
    span = 3 * quarter

    def body(at, own, across, sums, near, proj, qkv):
        for s in range(seq_count):

            @pl.when(at[0] == s)
            def _(s=s):
                c = s % 2
                proj[:, c * half : (c + 1) * half] = sums[...].astype(f32)
                proj[:, (1 - c) * half : (2 - c) * half] = near[:, :half].astype(f32)
                parts = ((own, half), (near, half), (across, half), (near, half + span))
                for k, (ref, base) in enumerate(parts):
                    for t in range(3):
                        start = t * width + (s ^ k) * quarter
                        at_col = base + t * quarter
                        qkv[:, start : start + quarter] = ref[
                            :, at_col : at_col + quarter
                        ].astype(f32)

    outs = (shaped(rows, width, f32), shaped(rows, 3 * width, f32))
    return call_whole(body, outs, table, own, across, sums, near)


def heads_forward(qkv, scale_val):
    length = qkv.shape[0]
    flat = qkv.shape[1] // 3
    heads = flat // HEAD
    block = min(256, length)

    def body(whole, out, lse, q_at, k_at, v_at, o_at):
        i = pl.program_id(0)

        @pl.when(i == 0)
        def _():
            for h in range(heads):
                lo = h * HEAD
                q_at[h] = (whole[:, lo : lo + HEAD].astype(f32) * scale_val).astype(bf16)
                k_at[h] = whole[:, flat + lo : flat + lo + HEAD]
                v_at[h] = whole[:, 2 * flat + lo : 2 * flat + lo + HEAD].T

        rows = pl.ds(pl.multiple_of(i * block, block), block)

        def one_head(h, carry):
            scores = dot(k_at[h], q_at[h, rows], ((1,), (1,)))
            top_val = jnp.max(scores, axis=0, keepdims=True)
            expd = jnp.exp(scores - top_val)
            totals = jnp.sum(expd, axis=0, keepdims=True)
            probs = (expd * (1.0 / totals)).astype(bf16)
            o_at[h] = dot(v_at[h], probs, ((1,), (0,)))
            lse[h] = top_val + jnp.log(totals)
            return carry

        lax.fori_loop(0, heads, one_head, 0)
        for h in range(heads):
            out[:, h * HEAD : (h + 1) * HEAD] = o_at[h].T.astype(bf16)

    return pl.pallas_call(
        body,
        grid=(length // block,),
        in_specs=[pl.BlockSpec((length, 3 * flat), lambda i: (0, 0))],
        out_specs=[
            pl.BlockSpec((block, flat), lambda i: (i, 0)),
            pl.BlockSpec((heads, 1, block), lambda i: (0, 0, i)),
        ],
        out_shape=[shaped(length, flat), jax.ShapeDtypeStruct((heads, 1, length), f32)],
        scratch_shapes=[
            pltpu.VMEM((heads, length, HEAD), bf16),
            pltpu.VMEM((heads, length, HEAD), bf16),
            pltpu.VMEM((heads, HEAD, length), bf16),
            pltpu.VMEM((heads, HEAD, block), f32),
        ],
        cost_estimate=pl.CostEstimate(
            flops=4 * length * length * flat,
            bytes_accessed=8 * length * flat,
            transcendentals=heads * length * length,
        ),
    )(qkv)


def heads_backward(qkv, grad, lse, scale_val):
    length = qkv.shape[0]
    flat = qkv.shape[1] // 3
    heads = flat // HEAD
    block = min(256, length)
    steps = length // block

    def body(whole, grads, lse_here, out, q_at, k_at, kt_at, v_at, g_at, dq_at, sum_k, sum_v):
        i = pl.program_id(0)

        @pl.when(i == 0)
        def _():
            for h in range(heads):
                lo = h * HEAD
                q_at[h] = (whole[:, lo : lo + HEAD].astype(f32) * scale_val).astype(bf16)
                key = whole[:, flat + lo : flat + lo + HEAD]
                k_at[h] = key
                kt_at[h] = key.T
                v_at[h] = whole[:, 2 * flat + lo : 2 * flat + lo + HEAD]
                g_at[h] = grads[:, lo : lo + HEAD]
            sum_k[...] = jnp.zeros_like(sum_k)
            sum_v[...] = jnp.zeros_like(sum_v)

        rows = pl.ds(pl.multiple_of(i * block, block), block)

        def one_head(h, carry):
            q = q_at[h, rows]
            g = g_at[h, rows]
            probs = jnp.exp(dot(k_at[h], q, ((1,), (1,))) - lse_here[h])
            grad_probs = dot(v_at[h], g, ((1,), (1,)))
            inner = jnp.sum(probs * grad_probs, axis=0, keepdims=True)
            grad_scores = (probs * (grad_probs - inner)).astype(bf16)
            dq_at[h] = dot(kt_at[h], grad_scores, ((1,), (0,))) * scale_val
            sum_k[h] += dot(grad_scores, q, ((1,), (0,)))
            sum_v[h] += dot(probs.astype(bf16), g, ((1,), (0,)))
            return carry

        lax.fori_loop(0, heads, one_head, 0)
        for h in range(heads):
            out[rows, h * HEAD : (h + 1) * HEAD] = dq_at[h].T.astype(bf16)

        @pl.when(i == steps - 1)
        def _():
            for h in range(heads):
                lo = flat + h * HEAD
                out[:, lo : lo + HEAD] = sum_k[h].astype(bf16)
                out[:, flat + lo : flat + lo + HEAD] = sum_v[h].astype(bf16)

    return pl.pallas_call(
        body,
        grid=(steps,),
        in_specs=[
            pl.BlockSpec((length, 3 * flat), lambda i: (0, 0)),
            pl.BlockSpec((length, flat), lambda i: (0, 0)),
            pl.BlockSpec((heads, 1, block), lambda i: (0, 0, i)),
        ],
        out_specs=pl.BlockSpec((length, 3 * flat), lambda i: (0, 0)),
        out_shape=shaped(length, 3 * flat),
        scratch_shapes=[
            pltpu.VMEM((heads, length, HEAD), bf16),
            pltpu.VMEM((heads, length, HEAD), bf16),
            pltpu.VMEM((heads, HEAD, length), bf16),
            pltpu.VMEM((heads, length, HEAD), bf16),
            pltpu.VMEM((heads, length, HEAD), bf16),
            pltpu.VMEM((heads, HEAD, block), f32),
            pltpu.VMEM((heads, length, HEAD), f32),
            pltpu.VMEM((heads, length, HEAD), f32),
        ],
        cost_estimate=pl.CostEstimate(
            flops=10 * length * length * flat,
            bytes_accessed=16 * length * flat,
            transcendentals=heads * length * length,
        ),
    )(qkv, grad, lse)


def local_ring(
    latents_in,
    conditions,
    w_ada,
    b_ada,
    w_qkv,
    b_qv,
    w_proj,
    b_proj,
    w_fc1,
    b_fc1,
    w_fc2,
    b_fc2,
    out_grad,
):
    width = latents_in.shape[2]
    tokens = latents_in.shape[1]
    seq_count = lax.axis_size("seq")
    owners = lax.axis_size("fsdp")
    me = lax.axis_index("fsdp")
    place = lax.axis_index("seq")
    core = place % 2
    own_rows = w_ada.shape[0]
    quarter = width // seq_count
    half_width = width // 2
    units = w_fc2.shape[0] // 2
    span = owners * units
    parts = units // own_rows
    scale_val = HEAD ** (-0.5)
    table = make_table(place, me)

    first = ring_pieces(pack_first(table, w_proj, w_qkv, seq_count))
    second = ring_pieces(pack_second(table, w_fc1, w_fc2, owners))

    condition = conditions[0]
    cond_act, silu_pull = jax.vjp(jax.nn.silu, condition)
    cond_low = cond_act.astype(bf16)
    small = jnp.concatenate(
        [v.astype(f32)[None] for v in (cond_low, b_qv, b_proj, b_fc1, b_fc2)], axis=1
    )
    small_rel = cube_gather(small)
    cond_rows = lax.dynamic_slice_in_dim(small_rel, me * own_rows, own_rows, 1).astype(bf16)
    mod_partial = dot(cond_rows, w_ada, ((1,), (0,)))
    bias_at = b_ada.shape[0]
    owned = jnp.arange(owners)[:, None] == me
    placed_bias = jnp.where(owned, b_ada.astype(f32)[None, :], 0.0)
    mod_partial = mod_partial + placed_bias.reshape(1, owners * bias_at)
    modulation = cube_sum(mod_partial)
    shift_one, scale_one, gate_one, shift_two, scale_two, gate_two = jnp.split(modulation, 6)

    bias_all = cube_to_order(small_rel[:, width:], me)
    at = 0
    biases = []
    for b in (b_qv, b_proj, b_fc1, b_fc2):
        biases.append(bias_all[:, at : at + b.shape[0]])
        at += b.shape[0]
    qv_full = biases[0].reshape(2, seq_count, quarter)
    bias_q, bias_v = lax.dynamic_index_in_dim(qv_full, place, 1, keepdims=False)
    bias_proj = biases[1].reshape(width)
    bias_fc1 = lax.dynamic_index_in_dim(
        biases[2].reshape(owners, 2, units), core, 1, keepdims=False
    ).reshape(span)
    bias_fc2 = biases[3].reshape(width)

    own_latent = latents_in[0]
    from_x = seq_swap(own_latent, 2)
    from_core = seq_swap(own_latent, 1)
    from_both = seq_swap(from_x, 1)
    all_latent = jnp.concatenate([own_latent, from_core, from_x, from_both]).astype(f32)
    latent = own_latent.astype(f32)
    grad_own = out_grad[0]
    grad_pair = jnp.concatenate([grad_own, seq_swap(grad_own, 1)]).astype(f32)
    grad_out = grad_own.astype(f32)

    proj_half, use_qkv = assemble(
        first,
        [(0, own_rows, 0, 0, half_width), (1, own_rows, 0, half_width, 3 * quarter)],
        (shaped(width, half_width), shaped(width, 3 * quarter)),
        table,
    )
    use_proj = mix_proj(table, proj_half, seq_swap(proj_half, 1), seq_count)

    normed_all = layer_norm(all_latent)
    act_one = (normed_all * (1.0 + scale_one) + shift_one).astype(bf16)
    bias_three = jnp.concatenate([bias_q, jnp.zeros_like(bias_q), bias_v])
    qkv = (dot(act_one, use_qkv, ((1,), (0,))) + bias_three).astype(bf16)
    attn_heads, lse = heads_forward(qkv, scale_val)

    def to_tokens(blocks):
        return [blocks[0]] + [seq_swap(blocks[k], k) for k in range(1, seq_count)]

    attn_own = jnp.concatenate(
        to_tokens([attn_heads[k * tokens : (k + 1) * tokens] for k in range(seq_count)]),
        axis=1,
    )
    branch_one = dot(attn_own, use_proj, ((1,), (0,))) + bias_proj
    middle = latent + gate_one * branch_one
    normed_two, norm_pull_two = jax.vjp(layer_norm, middle)
    act_two_own = (normed_two * (1.0 + scale_two) + shift_two).astype(bf16)

    act_two = jnp.concatenate([act_two_own, seq_swap(act_two_own, 1)])
    use_fc1, use_fc2 = assemble(
        second,
        [(0, own_rows, 0, 0, span)]
        + [(1, units, n * own_rows, span + n * width, width) for n in range(parts)],
        (shaped(width, span), shaped(span, width)),
        table,
    )
    hidden_pre = dot(act_two, use_fc1, ((1,), (0,))) + bias_fc1
    hidden_act, gelu_pull = jax.vjp(gelu_tanh, hidden_pre)
    hidden_low = hidden_act.astype(bf16)
    grad_two = (gate_two * grad_pair).astype(bf16)
    grad_hidden = dot(grad_two, use_fc2, ((1,), (1,)))
    grad_pre = gelu_pull(grad_hidden)[0].astype(bf16)
    far_act = dot(grad_pre[tokens:], use_fc1, ((1,), (1,)))
    near_act = dot(grad_pre[:tokens], use_fc1, ((1,), (1,)))
    grad_act_two = near_act + seq_swap(far_act, 1)

    grad_fc1 = dot(act_two, grad_pre, ((0,), (0,))).astype(bf16)
    grad_fc2 = dot(hidden_low, grad_two, ((0,), (0,))).astype(bf16)
    second_red = ring_sum(
        [grad_fc1, grad_fc2],
        [(0, 0, span)] + [(1, n * own_rows, width) for n in range(parts)],
        table,
        own_rows,
    )

    grad_shift_two = jnp.sum(grad_act_two, axis=0)
    grad_scale_two = jnp.sum(grad_act_two * normed_two, axis=0)
    grad_middle = grad_out + norm_pull_two(grad_act_two * (1.0 + scale_two))[0]
    grad_one = (gate_one * grad_middle).astype(bf16)
    grad_gate_one = jnp.sum(grad_middle * branch_one, axis=0)
    grad_attn = dot(grad_one, use_proj, ((1,), (1,))).astype(bf16)
    grad_heads = jnp.concatenate(
        to_tokens([grad_attn[:, k * quarter : (k + 1) * quarter] for k in range(seq_count)])
    )

    far_two = dot(hidden_low[tokens:], use_fc2, ((1,), (0,)))
    near_two = dot(hidden_low[:tokens], use_fc2, ((1,), (0,)))
    branch_two = near_two + seq_swap(far_two, 1) + bias_fc2
    result = middle + gate_two * branch_two
    grad_gate_two = jnp.sum(grad_out * branch_two, axis=0)
    grad_b_fc2 = jnp.sum(grad_two[:tokens].astype(f32), axis=0)
    grad_b_fc1 = jnp.sum(grad_pre.astype(f32), axis=0)
    grad_b_proj = jnp.sum(grad_one.astype(f32), axis=0)

    proj_rel = dot(attn_own, grad_one, ((0,), (0,))).astype(bf16)
    keep, give = split_proj(table, proj_rel, seq_count)
    proj_sum = (keep.astype(f32) + seq_swap(give, 1).astype(f32)).astype(bf16)

    grad_qkv = heads_backward(qkv, grad_heads, lse, scale_val)
    grad_own_qkv = dot(act_one, grad_qkv, ((0,), (0,))).astype(bf16)
    first_red = ring_sum(
        [proj_sum, grad_own_qkv], [(0, 0, half_width), (1, 0, 3 * quarter)], table, own_rows
    )
    first_x = seq_swap(first_red, 2)
    own_half = (
        first_red[:, :half_width].astype(f32) + first_x[:, :half_width].astype(f32)
    ).astype(bf16)
    mail = jnp.concatenate([own_half, first_red[:, half_width:], first_x[:, half_width:]], axis=1)
    grad_w_proj, grad_w_qkv = place_first(
        table, first_red, first_x, own_half, seq_swap(mail, 1), seq_count, width
    )
    second_sum = (second_red.astype(f32) + seq_swap(second_red, 2).astype(f32)).astype(bf16)
    grad_w_fc1, grad_w_fc2 = place_second(
        table, second_sum, seq_swap(second_sum, 1), owners, own_rows, units, width
    )

    partial_one = dot(grad_qkv, use_qkv, ((1,), (1,)))
    grad_shift_one = jnp.sum(partial_one, axis=0)
    grad_scale_one = jnp.sum(partial_one * normed_all, axis=0)
    far_low = partial_one[2 * tokens :].astype(bf16)
    far_sum = far_low[:tokens].astype(f32) + seq_swap(far_low[tokens:], 1).astype(f32)
    near_low = partial_one[tokens : 2 * tokens].astype(bf16)
    near_sum = partial_one[:tokens] + seq_swap(near_low, 1).astype(f32)
    grad_act_one = near_sum + seq_swap(far_sum.astype(bf16), 2).astype(f32)
    _, norm_pull_one = jax.vjp(layer_norm, latent)
    grad_latent = grad_middle + norm_pull_one(grad_act_one * (1.0 + scale_one))[0]

    qkv_sums = jnp.sum(grad_qkv.astype(f32), axis=0).reshape(3, 1, quarter)
    grad_b_qv = jnp.where(
        jnp.arange(seq_count)[None, :, None] == place,
        jnp.concatenate([qkv_sums[:1], qkv_sums[2:]]),
        0.0,
    ).reshape(2 * width)
    placed_fc1 = jnp.where(
        jnp.arange(2)[None, :, None] == core, grad_b_fc1.reshape(owners, 1, units), 0.0
    ).reshape(2 * span)
    terms = jnp.concatenate(
        [
            grad_shift_one,
            grad_scale_one,
            grad_gate_one,
            grad_shift_two,
            grad_scale_two,
            grad_gate_two,
            grad_b_qv,
            grad_b_proj,
            placed_fc1,
            grad_b_fc2,
        ]
    )
    pair_sum = terms + seq_swap(terms, 1)
    sums = pair_sum + seq_swap(pair_sum, 2)
    low_sums = sums.astype(bf16)
    got = cube_gather(low_sums[None])
    mod_rel = got[:, : 6 * width]
    all_sums = jnp.sum(got[:, 6 * width :].astype(f32), axis=0)
    owned_w_ada = dot(cond_rows, mod_rel, ((0,), (0,)))
    owned_b_ada = jnp.sum(
        lax.dynamic_slice_in_dim(mod_rel, me * bias_at, bias_at, 1).astype(f32), axis=0
    )
    cond_partial = dot(mod_rel, w_ada, ((1,), (1,)))
    cond_got = cube_to_order(cube_deal(cond_partial), me)
    grad_cond = silu_pull(cond_got.reshape(width))[0]
    at = 0
    owned_bias = []
    for b in (b_qv, b_proj, b_fc1, b_fc2):
        size = b.shape[0]
        owned_bias.append(lax.dynamic_slice_in_dim(all_sums, at + me * size, size, 0))
        at += size * owners
    return (
        result.astype(bf16)[None],
        grad_latent[None],
        grad_cond[None],
        owned_w_ada,
        owned_b_ada,
        grad_w_qkv,
        owned_bias[0],
        grad_w_proj,
        owned_bias[1],
        grad_w_fc1,
        owned_bias[2],
        grad_w_fc2,
        owned_bias[3],
    )


def short_axes(mesh):
    count = mesh.shape["fsdp"]
    return 2 < count <= RING_MAX and count & (count - 1) == 0 and mesh.shape["seq"] == 4


def local(*args):
    return local_ring(*args)


def solution(mesh):
    short = short_axes(mesh)
    return jax.shard_map(
        local if short else local_wide,
        mesh=mesh,
        in_specs=(
            P("fsdp", "seq", None),
            P("fsdp", None),
            P("fsdp", None),
            P("fsdp"),
            P("fsdp", None),
            P("fsdp"),
            P("fsdp", None),
            P("fsdp"),
            P("fsdp", None),
            P("fsdp"),
            P("fsdp", None),
            P("fsdp"),
            P("fsdp", "seq", None),
        ),
        out_specs=(
            P("fsdp", "seq", None),
            P("fsdp", "seq", None),
            P("fsdp", None),
            P("fsdp", None),
            P("fsdp"),
            P("fsdp", None),
            P("fsdp"),
            P("fsdp", None),
            P("fsdp"),
            P("fsdp", None),
            P("fsdp"),
            P("fsdp", None),
            P("fsdp"),
        ),
        check_vma=False,
    )
```

```python
import functools

import jax
import jax.numpy as jnp
from jax import lax
from jax.experimental import pallas as pl
from jax.experimental.pallas import tpu as pltpu
from jax.sharding import PartitionSpec as P


HEAD = 64
RING_MAX = 16

norm_eps = 1e-06
f32 = jnp.float32
bf16 = jnp.bfloat16


def dot(a, b, dims):
    return lax.dot_general(a, b, (dims, ((), ())), preferred_element_type=f32)


def layer_norm(values):
    mean_val = jnp.mean(values, axis=-1, keepdims=True)
    centred = values - mean_val
    var_val = jnp.mean(centred * centred, axis=-1, keepdims=True)
    return centred * lax.rsqrt(var_val + norm_eps)


def gelu_tanh(values):
    return jax.nn.gelu(values, approximate=True)


def seq_swap(values, bit):
    count = lax.axis_size("seq")
    return lax.ppermute(values, "seq", [(i, i ^ bit) for i in range(count)])


swap_core = functools.partial(seq_swap, bit=1)
swap_x = functools.partial(seq_swap, bit=2)


def rolled(rows, shift):
    count = rows.shape[0]
    return lax.dynamic_slice_in_dim(jnp.concatenate([rows, rows]), count - shift, count, 0)


def gather_small(row, me):
    count = lax.axis_size("fsdp")
    if count > RING_MAX:
        rows = lax.all_gather(row, "fsdp", axis=0)
        return rolled(rows[::-1], jnp.mod(me + 1, count))
    got = [row]
    for r in range(1, count):
        got.append(lax.ppermute(row, "fsdp", [(i, (i + r) % count) for i in range(count)]))
    return jnp.stack(got)


def deal_small(rows, me):
    count = lax.axis_size("fsdp")
    if count > RING_MAX:
        placed = rolled(rows[::-1], jnp.mod(me + 1, count))
        got = lax.all_to_all(placed, "fsdp", split_axis=0, concat_axis=0, tiled=True)
        return rolled(got, jnp.mod(count - me, count))
    got = [rows[0]]
    for r in range(1, count):
        got.append(lax.ppermute(rows[r], "fsdp", [(i, (i - r) % count) for i in range(count)]))
    return jnp.stack(got)


def ring_tables(count):
    order = list(range(0, count, 2)) + list(range(count - 1, 0, -2))
    ahead = [(order[i], order[(i + 1) % count]) for i in range(count)]
    return order, ahead, [(b, a) for a, b in ahead]


def ring_place(me, offset):
    count = lax.axis_size("fsdp")
    mine = jnp.where(me % 2 == 0, me // 2, count - 1 - me // 2)
    place = jnp.mod(mine + offset + count, count)
    return jnp.where(place < count // 2, 2 * place, 2 * (count - 1 - place) + 1)


def ring_gather(block, me):
    count = lax.axis_size("fsdp")
    if count > RING_MAX:
        return lax.all_gather(block, "fsdp", axis=0, tiled=True)
    _, ahead, back = ring_tables(count)
    rows = block.shape[0]
    half = rows // 2
    far = count // 2
    out = jnp.zeros((rows * count,) + block.shape[1:], block.dtype)

    def put(out, piece, offset, shift):
        start = ring_place(me, offset) * rows + shift
        return lax.dynamic_update_slice_in_dim(out, piece, start, 0)

    out = put(out, block, 0, 0)
    up = down = block
    for step in range(1, far + 1):
        if step == far:
            up, down = up[:half], down[half:]
        up = lax.ppermute(up, "fsdp", ahead)
        down = lax.ppermute(down, "fsdp", back)
        out = put(out, up, -step, 0)
        out = put(out, down, step, half if step == far else 0)
    return out


def ring_reduce(values, me):
    count = lax.axis_size("fsdp")
    rows = values.shape[0] // count
    if count > RING_MAX:
        return lax.psum_scatter(
            values.astype(bf16), "fsdp", scatter_dimension=0, tiled=True
        ).astype(f32)
    _, ahead, back = ring_tables(count)
    half = rows // 2
    far = count // 2

    def take(offset, start, size):
        return lax.dynamic_slice_in_dim(
            values, ring_place(me, offset) * rows + start, size, 0
        ).astype(f32)

    up = take(far, 0, half)
    down = take(-far, half, half)
    for step in range(1, far + 1):
        up = lax.ppermute(up.astype(bf16), "fsdp", ahead).astype(f32)
        down = lax.ppermute(down.astype(bf16), "fsdp", back).astype(f32)
        if step == far:
            break
        if step == 1:
            up = jnp.concatenate(
                [take(far - 1, 0, half) + up, take(far - 1, half, rows - half)]
            )
            down = jnp.concatenate(
                [take(1 - far, 0, half), take(1 - far, half, rows - half) + down]
            )
        else:
            up = up + take(far - step, 0, rows)
            down = down + take(step - far, 0, rows)
    return take(0, 0, rows) + up + down


def attend_forward(queries, keys, values, scale_val):
    rows = queries.shape[0]
    heads = queries.shape[1] // HEAD
    q = queries.reshape(rows, heads, HEAD)
    k = keys.reshape(rows, heads, HEAD)
    v = values.reshape(rows, heads, HEAD)
    scores = jnp.einsum("qhd,khd->hqk", q, k, preferred_element_type=f32) * scale_val
    top_val = jnp.max(scores, axis=-1, keepdims=True)
    expd_val = jnp.exp(scores - top_val)
    totals = jnp.sum(expd_val, axis=-1, keepdims=True)
    probs = (expd_val / totals).astype(bf16)
    out = jnp.einsum("hqk,khd->qhd", probs, v, preferred_element_type=f32)
    return out.astype(bf16).reshape(rows, heads * HEAD), (top_val + jnp.log(totals))


def attend_backward(queries, keys, values, grad, lse, scale_val):
    rows = queries.shape[0]
    heads = queries.shape[1] // HEAD
    q, k, v, g = (a.reshape(rows, heads, HEAD) for a in (queries, keys, values, grad))
    scores = jnp.einsum("qhd,khd->hqk", q, k, preferred_element_type=f32) * scale_val
    probs = jnp.exp(scores - lse)
    grad_probs = jnp.einsum("qhd,khd->hqk", g, v, preferred_element_type=f32)
    inner = jnp.sum(probs * grad_probs, axis=-1, keepdims=True)
    grad_scores = (probs * (grad_probs - inner)).astype(bf16)
    grad_q = jnp.einsum("hqk,khd->qhd", grad_scores, k, preferred_element_type=f32) * scale_val
    grad_k = jnp.einsum("hqk,qhd->khd", grad_scores, q, preferred_element_type=f32) * scale_val
    grad_v = jnp.einsum("hqk,qhd->khd", probs.astype(bf16), g, preferred_element_type=f32)
    flat = heads * HEAD
    return [a.astype(bf16).reshape(rows, flat) for a in (grad_q, grad_k, grad_v)]


def local_wide(
    latents_in,
    conditions,
    w_ada,
    b_ada,
    w_qkv,
    b_qv,
    w_proj,
    b_proj,
    w_fc1,
    b_fc1,
    w_fc2,
    b_fc2,
    out_grad,
):
    width = latents_in.shape[2]
    tokens = latents_in.shape[1]
    seq_count = lax.axis_size("seq")
    owners = lax.axis_size("fsdp")
    me = lax.axis_index("fsdp")
    place = lax.axis_index("seq")
    core = place % 2
    own_rows = w_ada.shape[0]
    quarter = width // seq_count
    units = w_fc2.shape[0] // 2
    scale_val = HEAD ** (-0.5)

    condition = conditions[0]
    cond_act, silu_pull = jax.vjp(jax.nn.silu, condition)
    cond_low = cond_act.astype(bf16)
    small = jnp.concatenate([cond_low, b_qv, b_proj, b_fc1, b_fc2])
    small_rel = gather_small(small, me)
    cond_rows = lax.dynamic_slice_in_dim(small_rel, me * own_rows, own_rows, 1)
    mod_partial = dot(cond_rows, w_ada, ((1,), (0,)))
    bias_at = b_ada.shape[0]
    placed_bias = jnp.where(
        jnp.arange(owners)[:, None] == me, b_ada.astype(f32)[None, :], 0.0
    ).reshape(1, owners * bias_at)
    mod_partial = mod_partial + placed_bias
    modulation = jnp.sum(deal_small(mod_partial, me), axis=0)
    shift_one, scale_one, gate_one, shift_two, scale_two, gate_two = jnp.split(modulation, 6)

    bias_rel = small_rel[:, width:].astype(f32)
    bias_all = rolled(bias_rel[::-1], jnp.mod(me + 1, owners))
    at = 0
    biases = []
    for b in (b_qv, b_proj, b_fc1, b_fc2):
        biases.append(bias_all[:, at : at + b.shape[0]])
        at += b.shape[0]
    qv_full = biases[0].reshape(2, seq_count, quarter)
    bias_q, bias_v = lax.dynamic_index_in_dim(qv_full, place, 1, keepdims=False)
    bias_proj = biases[1].reshape(width)
    bias_fc1 = lax.dynamic_index_in_dim(
        biases[2].reshape(owners, 2, units), core, 1, keepdims=False
    ).reshape(owners * units)
    bias_fc2 = biases[3].reshape(width)

    mine_qkv = lax.dynamic_index_in_dim(
        w_qkv.reshape(own_rows, 3, seq_count, quarter), place, 2, keepdims=False
    ).reshape(own_rows, 3 * quarter)
    use_qkv = ring_gather(mine_qkv, me)
    mine_proj = lax.dynamic_slice_in_dim(w_proj, core * (width // 2), width // 2, 1)
    proj_half = ring_gather(mine_proj, me)
    proj_other = swap_core(proj_half)
    full_proj = jnp.where(
        core == 0,
        jnp.concatenate([proj_half, proj_other], axis=1),
        jnp.concatenate([proj_other, proj_half], axis=1),
    )
    use_proj = jnp.concatenate(
        [
            lax.dynamic_slice_in_dim(full_proj, (place ^ k) * quarter, quarter, 0)
            for k in range(seq_count)
        ]
    )
    mine_fc1 = lax.dynamic_index_in_dim(
        w_fc1.reshape(own_rows, owners, 2, units), core, 2, keepdims=False
    ).reshape(own_rows, owners * units)
    use_fc1 = ring_gather(mine_fc1, me)
    mine_fc2 = lax.dynamic_slice_in_dim(w_fc2, core * units, units, 0)
    use_fc2 = ring_gather(mine_fc2, me)

    own_latent = latents_in[0]
    from_x = swap_x(own_latent)
    from_core = swap_core(own_latent)
    from_both = swap_core(from_x)
    all_latent = jnp.concatenate([own_latent, from_core, from_x, from_both]).astype(f32)
    latent = own_latent.astype(f32)
    grad_own = out_grad[0]
    grad_pair = jnp.concatenate([grad_own, swap_core(grad_own)]).astype(f32)
    grad_out = grad_own.astype(f32)

    normed_all = layer_norm(all_latent)
    act_one = (normed_all * (1.0 + scale_one) + shift_one).astype(bf16)
    bias_three = jnp.concatenate([bias_q, jnp.zeros_like(bias_q), bias_v])
    qkv = (dot(act_one, use_qkv, ((1,), (0,))) + bias_three).astype(bf16)
    queries, keys, values = jnp.split(qkv, 3, axis=1)
    attn_heads, lse = attend_forward(queries, keys, values, scale_val)

    def to_tokens(blocks):
        return [blocks[0]] + [seq_swap(blocks[k], k) for k in range(1, seq_count)]

    attn_own = jnp.concatenate(
        to_tokens([attn_heads[k * tokens : (k + 1) * tokens] for k in range(seq_count)]), axis=1
    )
    branch_one = dot(attn_own, use_proj, ((1,), (0,))) + bias_proj
    middle = latent + gate_one * branch_one
    normed_two, norm_pull_two = jax.vjp(layer_norm, middle)
    act_two_own = (normed_two * (1.0 + scale_two) + shift_two).astype(bf16)

    act_two = jnp.concatenate([act_two_own, swap_core(act_two_own)])
    hidden_pre = dot(act_two, use_fc1, ((1,), (0,))) + bias_fc1
    hidden_act, gelu_pull = jax.vjp(gelu_tanh, hidden_pre)
    hidden_low = hidden_act.astype(bf16)
    grad_two = (gate_two * grad_pair).astype(bf16)
    grad_hidden = dot(grad_two, use_fc2, ((1,), (1,)))
    grad_pre = gelu_pull(grad_hidden)[0].astype(bf16)
    partial_act = dot(grad_pre, use_fc1, ((1,), (1,)))
    grad_act_two = partial_act[:tokens] + swap_core(partial_act[tokens:])
    grad_shift_two = jnp.sum(grad_act_two, axis=0)
    grad_scale_two = jnp.sum(grad_act_two * normed_two, axis=0)
    grad_middle = grad_out + norm_pull_two(grad_act_two * (1.0 + scale_two))[0]
    grad_one = (gate_one * grad_middle).astype(bf16)
    grad_gate_one = jnp.sum(grad_middle * branch_one, axis=0)
    grad_attn = dot(grad_one, use_proj, ((1,), (1,))).astype(bf16)
    grad_heads = jnp.concatenate(
        to_tokens([grad_attn[:, k * quarter : (k + 1) * quarter] for k in range(seq_count)])
    )

    partial_two = dot(hidden_low, use_fc2, ((1,), (0,)))
    branch_two = partial_two[:tokens] + swap_core(partial_two[tokens:]) + bias_fc2
    result = middle + gate_two * branch_two
    grad_gate_two = jnp.sum(grad_out * branch_two, axis=0)
    grad_b_fc2 = jnp.sum(grad_two[:tokens].astype(f32), axis=0)
    grad_b_fc1 = jnp.sum(grad_pre.astype(f32), axis=0)
    grad_b_proj = jnp.sum(grad_one.astype(f32), axis=0)

    red_fc2 = ring_reduce(dot(hidden_low, grad_two, ((0,), (0,))).astype(bf16), me)
    red_fc1 = ring_reduce(dot(act_two, grad_pre, ((0,), (0,))).astype(bf16), me)

    def add_x(block):
        low = block.astype(bf16)
        return low.astype(f32) + swap_x(low).astype(f32)

    def in_core_order(block):
        other = swap_core(block)
        return jnp.where(core == 0, block, other), jnp.where(core == 0, other, block)

    grad_w_fc2 = jnp.concatenate(in_core_order(add_x(red_fc2)))
    first_fc1, second_fc1 = in_core_order(add_x(red_fc1))
    grad_w_fc1 = jnp.concatenate(
        [first_fc1.reshape(own_rows, owners, 1, units), second_fc1.reshape(own_rows, owners, 1, units)],
        axis=2,
    ).reshape(own_rows, 2 * owners * units)

    proj_rel = dot(attn_own, grad_one, ((0,), (0,))).astype(bf16)
    proj_abs = jnp.concatenate(
        [
            lax.dynamic_slice_in_dim(proj_rel, (place ^ k) * quarter, quarter, 0)
            for k in range(seq_count)
        ]
    )
    half_width = width // 2
    keep = lax.dynamic_slice_in_dim(proj_abs, core * half_width, half_width, 1)
    give = lax.dynamic_slice_in_dim(proj_abs, (1 - core) * half_width, half_width, 1)
    proj_sum = (keep.astype(f32) + swap_core(give).astype(f32)).astype(bf16)
    grad_w_proj = jnp.concatenate(in_core_order(add_x(ring_reduce(proj_sum, me))), axis=1)

    grad_q, grad_k, grad_v = attend_backward(queries, keys, values, grad_heads, lse, scale_val)
    grad_qkv = jnp.concatenate([grad_q, grad_k, grad_v], axis=1)
    red_qkv = ring_reduce(dot(act_one, grad_qkv, ((0,), (0,))).astype(bf16), me).astype(bf16)
    across = swap_x(red_qkv)
    blocks = [red_qkv, swap_core(red_qkv), across, swap_core(across)]
    for bit in (1, 2):
        flip = (place & bit) != 0
        blocks = [jnp.where(flip, blocks[j ^ bit], blocks[j]) for j in range(seq_count)]
    grad_w_qkv = jnp.concatenate(
        [b.astype(f32).reshape(own_rows, 3, 1, quarter) for b in blocks], axis=2
    ).reshape(own_rows, 3 * width)

    partial_one = dot(grad_qkv, use_qkv, ((1,), (1,)))
    grad_shift_one = jnp.sum(partial_one, axis=0)
    grad_scale_one = jnp.sum(partial_one * normed_all, axis=0)
    far_low = partial_one[2 * tokens :].astype(bf16)
    far_sum = far_low[:tokens].astype(f32) + swap_core(far_low[tokens:]).astype(f32)
    near_low = partial_one[tokens : 2 * tokens].astype(bf16)
    near_sum = partial_one[:tokens] + swap_core(near_low).astype(f32)
    grad_act_one = near_sum + swap_x(far_sum.astype(bf16)).astype(f32)
    _, norm_pull_one = jax.vjp(layer_norm, latent)
    grad_latent = grad_middle + norm_pull_one(grad_act_one * (1.0 + scale_one))[0]

    grad_b_qv = jnp.where(
        jnp.arange(seq_count)[None, :, None] == place,
        jnp.stack(
            [jnp.sum(grad_q.astype(f32), axis=0), jnp.sum(grad_v.astype(f32), axis=0)]
        )[:, None, :],
        0.0,
    ).reshape(2 * width)
    placed_fc1 = jnp.where(
        jnp.arange(2)[None, :, None] == core, grad_b_fc1.reshape(owners, 1, units), 0.0
    ).reshape(2 * owners * units)
    terms = jnp.concatenate(
        [
            grad_shift_one,
            grad_scale_one,
            grad_gate_one,
            grad_shift_two,
            grad_scale_two,
            grad_gate_two,
            grad_b_qv,
            grad_b_proj,
            placed_fc1,
            grad_b_fc2,
        ]
    )
    sums = (terms + seq_swap(terms, 1)) + (seq_swap(terms, 2) + seq_swap(terms, 3))
    low_sums = sums.astype(bf16)
    grad_mod = low_sums[: 6 * width]
    at = 6 * width
    by_owner = []
    for b in (b_qv, b_proj, b_fc1, b_fc2):
        size = b.shape[0] * owners
        by_owner.append(low_sums[at : at + size].reshape(owners, b.shape[0]))
        at += size
    by_owner = jnp.concatenate(by_owner, axis=1)
    sent_bias = rolled(by_owner[::-1], jnp.mod(me + 1, owners))
    mail = jnp.concatenate(
        [jnp.broadcast_to(grad_mod[None, :], (owners, 6 * width)), sent_bias], axis=1
    )
    got = deal_small(mail, me)
    mod_rel = got[:, : 6 * width]
    bias_sums = jnp.sum(got[:, 6 * width :].astype(f32), axis=0)
    back_cond = jnp.concatenate([cond_rows[:1], cond_rows[1:][::-1]])
    owned_w_ada = dot(back_cond, mod_rel, ((0,), (0,)))
    owned_b_ada = jnp.sum(
        lax.dynamic_slice_in_dim(mod_rel, me * bias_at, bias_at, 1).astype(f32), axis=0
    )
    cond_partial = dot(mod_rel, w_ada, ((1,), (1,)))
    back_partial = jnp.concatenate([cond_partial[:1], cond_partial[1:][::-1]])
    cond_got = rolled(deal_small(back_partial, me), me)
    grad_cond = silu_pull(cond_got.reshape(width))[0]
    at = 0
    owned_bias = []
    for b in (b_qv, b_proj, b_fc1, b_fc2):
        owned_bias.append(bias_sums[at : at + b.shape[0]])
        at += b.shape[0]
    return (
        result.astype(bf16)[None],
        grad_latent[None],
        grad_cond[None],
        owned_w_ada,
        owned_b_ada,
        grad_w_qkv,
        owned_bias[0],
        grad_w_proj,
        owned_bias[1],
        grad_w_fc1,
        owned_bias[2],
        grad_w_fc2,
        owned_bias[3],
    )


def swap_f(values, bit):
    count = lax.axis_size("fsdp")
    return lax.ppermute(values, "fsdp", [(i, i ^ bit) for i in range(count)])


def cube_bits():
    return [1 << b for b in range(lax.axis_size("fsdp").bit_length() - 1)]


def cube_places():
    places = [0]
    for bit in reversed(cube_bits()):
        places = places + [r | bit for r in places]
    return places


def cube_gather(row):
    rows = row
    for bit in reversed(cube_bits()):
        got = swap_f(rows, bit)
        rows = jnp.concatenate([rows, got])
    return rows


def cube_sum(rows):
    for bit in cube_bits():
        half = rows.shape[0] // 2
        got = swap_f(rows[half:], bit)
        rows = rows[:half] + got
    return rows[0]


def cube_deal(rows):
    count = rows.shape[0]
    done = 1
    for bit in cube_bits():
        parts = rows.reshape((done, 2, count // (2 * done)) + rows.shape[1:])
        got = swap_f(parts[:, 1], bit)
        rows = jnp.stack([parts[:, 0], got], axis=1).reshape(rows.shape)
        done *= 2
    return rows


def cube_to_order(rows, me):
    places = jnp.array(cube_places())
    count = rows.shape[0]
    hit = jnp.arange(count)[:, None] == jnp.bitwise_xor(places, me)[None, :]
    return jnp.sum(jnp.where(hit[:, :, None], rows[None], jnp.zeros_like(rows)[None]), axis=1)


def to_cube(rows, me):
    places = jnp.array(cube_places())
    count = rows.shape[0]
    hit = jnp.arange(count)[None, :] == jnp.bitwise_xor(places, me)[:, None]
    return jnp.sum(jnp.where(hit[:, :, None], rows[None], jnp.zeros_like(rows)[None]), axis=1)


SMEM = pl.BlockSpec(memory_space=pltpu.SMEM)
VMEM = pl.BlockSpec(memory_space=pltpu.VMEM)


def bytes_of(*arrays):
    return sum(a.size * a.dtype.itemsize for a in arrays)


def call_whole(body, outs, table, *arrays, scratch=()):
    return pl.pallas_call(
        body,
        out_shape=outs,
        in_specs=[SMEM] + [VMEM] * len(arrays),
        out_specs=jax.tree.map(lambda _: VMEM, outs),
        scratch_shapes=list(scratch),
        compiler_params=pltpu.CompilerParams(
            vmem_limit_bytes=bytes_of(*arrays) + bytes_of(*jax.tree.leaves(outs)) + 2**21
        ),
        cost_estimate=pl.CostEstimate(
            flops=0,
            bytes_accessed=bytes_of(*arrays) + bytes_of(*jax.tree.leaves(outs)),
            transcendentals=0,
        ),
    )(table, *arrays)


def shaped(rows, cols, dtype=bf16):
    return jax.ShapeDtypeStruct((rows, cols), dtype)


def make_table(place, me):
    count = lax.axis_size("fsdp")
    around = [ring_place(me, off) for off in range(count)]
    return jnp.stack([jnp.asarray(v, jnp.int32) for v in [place] + around])


def along(at, offset, count):
    return at[1 + offset % count]


def pack_first(table, w_proj, w_qkv, rows_extra, seq_count):
    rows, width = w_proj.shape
    half = width // 2
    quarter = width // seq_count
    total = half + 3 * quarter

    def body(at, proj, qkv, *rest):
        small, out, lines = rest[: len(rows_extra)], rest[len(rows_extra)], rest[-1]
        lines[...] = jnp.zeros_like(lines)
        for ref, (line, col) in zip(small, small_places([v.shape[1] for v in rows_extra], total)):
            lines[line : line + 1, col : col + ref.shape[1]] = ref[...].astype(f32)
        out[rows:, :] = lines[...].astype(bf16)
        for s in range(seq_count):

            @pl.when(at[0] == s)
            def _(s=s):
                out[:rows, :half] = proj[:, (s % 2) * half : (s % 2 + 1) * half]
                for t in range(3):
                    to = half + t * quarter
                    start = t * width + s * quarter
                    out[:rows, to : to + quarter] = qkv[:, start : start + quarter]

    outs = shaped(rows + 16, total)
    lines = pltpu.VMEM((16, total), f32)
    return call_whole(body, outs, table, w_proj, w_qkv, *rows_extra, scratch=[lines])


def small_places(sizes, total):
    places, line, col = [], 0, 0
    for size in sizes:
        if col + size > total:
            line, col = line + 1, 0
        places.append((line, col))
        col += size
    return places


def put_first(table, pieces, rows, width, quarter, sizes):
    count = lax.axis_size("fsdp")
    half = width // 2
    total = half + 3 * quarter
    places = small_places(sizes, total)
    offsets = [off for off, _, _ in pieces]
    shifts = [first for _, first, _ in pieces]

    def body(at, *refs):
        ins = refs[: len(pieces)]
        proj, qkv = refs[len(pieces) : len(pieces) + 2]
        small = refs[len(pieces) + 2 :]
        for ref, off, shift in zip(ins, offsets, shifts):
            size = min(ref.shape[0], rows - shift)
            owner = along(at, off, count)
            start = pl.multiple_of(owner * rows + shift, 16)
            proj[pl.ds(start, size), :] = ref[:size, :half]
            qkv[pl.ds(start, size), :] = ref[:size, half:]
            if size < ref.shape[0]:
                lines = ref[size:, :].astype(f32)
                for out, (line, col) in zip(small, places):
                    out[pl.ds(owner, 1), :] = lines[line : line + 1, col : col + out.shape[1]]

    outs = (shaped(width, half), shaped(width, 3 * quarter)) + tuple(
        shaped(count, n, f32) for n in sizes
    )
    return call_whole(body, outs, table, *[p for _, _, p in pieces])


def pack_second(table, w_fc1, w_fc2, owners):
    rows = w_fc1.shape[0]
    width = w_fc2.shape[1]
    units = w_fc2.shape[0] // 2
    span = owners * units
    parts = units // rows

    def body(at, fc1, fc2, out):
        for c in range(2):

            @pl.when(at[0] % 2 == c)
            def _(c=c):
                for f in range(owners):
                    start = (2 * f + c) * units
                    out[:, f * units : (f + 1) * units] = fc1[:, start : start + units]
                for n in range(parts):
                    start = c * units + n * rows
                    to = span + n * width
                    out[:, to : to + width] = fc2[start : start + rows, :]

    outs = shaped(rows, span + parts * width)
    return call_whole(body, outs, table, w_fc1, w_fc2)


def ring_pieces(block, half):
    count = lax.axis_size("fsdp")
    _, ahead, back = ring_tables(count)
    far = count // 2
    pieces = [(0, 0, block)]
    up = down = block
    for step in range(1, far + 1):
        if step == far:
            up, down = up[:half], down[half:]
        up = lax.ppermute(up, "fsdp", ahead)
        down = lax.ppermute(down, "fsdp", back)
        pieces.append((-step, 0, up))
        pieces.append((step, half if step == far else 0, down))
    return pieces


def assemble(pieces, layout, outs, table):
    count = lax.axis_size("fsdp")
    offsets = [off for off, _, _ in pieces]
    shifts = [first for _, first, _ in pieces]

    def body(at, *refs):
        ins, results = refs[: len(pieces)], refs[len(pieces) :]
        for ref, off, shift in zip(ins, offsets, shifts):
            size = ref.shape[0]
            owner = along(at, off, count)
            for out, per, base, col, cols in layout:
                start = pl.multiple_of(owner * per + base + shift, 16)
                results[out][pl.ds(start, size), :] = ref[:, col : col + cols]

    return call_whole(body, outs, table, *[p for _, _, p in pieces])


def mix_proj(table, own, other, seq_count):
    width, half = own.shape
    quarter = width // seq_count

    def body(at, mine, theirs, out):
        for s in range(seq_count):

            @pl.when(at[0] == s)
            def _(s=s):
                c = s % 2
                for k in range(seq_count):
                    src = slice((s ^ k) * quarter, ((s ^ k) + 1) * quarter)
                    dst = slice(k * quarter, (k + 1) * quarter)
                    out[dst, c * half : (c + 1) * half] = mine[src, :]
                    out[dst, (1 - c) * half : (2 - c) * half] = theirs[src, :]

    return call_whole(body, shaped(width, width), table, own, other)


def split_proj(table, values, seq_count):
    width = values.shape[1]
    half = width // 2
    quarter = width // seq_count

    def body(at, ref, keep, give):
        for s in range(seq_count):

            @pl.when(at[0] == s)
            def _(s=s):
                c = s % 2
                for k in range(seq_count):
                    dst = slice((s ^ k) * quarter, ((s ^ k) + 1) * quarter)
                    src = slice(k * quarter, (k + 1) * quarter)
                    keep[dst, :] = ref[src, c * half : (c + 1) * half]
                    give[dst, :] = ref[src, (1 - c) * half : (2 - c) * half]

    return call_whole(body, (shaped(width, half), shaped(width, half)), table, values)


def ring_sum(arrays, layout, table, rows):
    count = lax.axis_size("fsdp")
    _, ahead, back = ring_tables(count)
    half = rows // 2
    far = count // 2
    total = sum(cols for _, _, cols in layout)

    def step_call(step, *got):
        def body(at, *refs):
            blocks, rest = refs[: len(arrays)], refs[len(arrays) :]
            up_at, down_at = along(at, far - step, count), along(at, step - far, count)
            col = 0
            for a, base, cols in layout:
                to = slice(col, col + cols)
                col += cols
                per = blocks[a].shape[0] // count

                def own(owner, lo, hi):
                    start = pl.multiple_of(owner * per + base + lo, 16)
                    return blocks[a][pl.ds(start, hi - lo), :]

                def plus(owner, ref, lo, hi):
                    return (own(owner, lo, hi).astype(f32) + ref[:, to].astype(f32)).astype(bf16)

                if step == 0:
                    rest[0][:, to] = own(up_at, 0, half)
                    rest[1][:, to] = own(down_at, half, rows)
                elif step == far:
                    up, down, out = rest
                    out[:, to] = (
                        own(up_at, 0, rows).astype(f32)
                        + up[:, to].astype(f32)
                        + down[:, to].astype(f32)
                    ).astype(bf16)
                else:
                    up, down, next_up, next_down = rest
                    if step == 1:
                        next_up[:half, to] = plus(up_at, up, 0, half)
                        next_up[half:, to] = own(up_at, half, rows)
                        next_down[:half, to] = own(down_at, 0, half)
                        next_down[half:, to] = plus(down_at, down, half, rows)
                    else:
                        next_up[:, to] = plus(up_at, up, 0, rows)
                        next_down[:, to] = plus(down_at, down, 0, rows)

        out = shaped(half if step == 0 else rows, total)
        outs = out if step == far else (out, out)
        return call_whole(body, outs, table, *arrays, *got)

    up, down = step_call(0)
    for step in range(1, far + 1):
        up = lax.ppermute(up, "fsdp", ahead)
        down = lax.ppermute(down, "fsdp", back)
        if step < far:
            up, down = step_call(step, up, down)
    return step_call(far, up, down)


def cube_reduce(values, table, rows, beside=None):
    bits = cube_bits()
    cols = values.shape[1]

    def block(ref, index):
        return ref[pl.ds(pl.multiple_of(index * rows, 16), rows), :]

    def call(step, held, got):
        left = len(bits) - step
        many = 1 << left

        def body(at, *refs):
            ins, outs = refs[: len(refs) - n_outs], refs[len(refs) - n_outs :]
            me = at[1]

            def summed(n):
                if step == 0:
                    return block(ins[0], n)
                index = 2 * n + lax.rem(me >> (step - 1), 2) if step == 1 else n
                mine = block(ins[0], index)
                return (mine.astype(f32) + block(ins[1], n).astype(f32)).astype(bf16)

            if left == 0:
                if beside is None:
                    outs[0][...] = summed(0)
                else:
                    outs[0][:, : beside.shape[1]] = ins[-1][...]
                    outs[0][:, beside.shape[1] :] = summed(0)
                return
            bit = lax.rem(me >> step, 2)
            for n in range(many // 2):
                rows_n = slice(n * rows, (n + 1) * rows)
                outs[0][rows_n, :] = summed(2 * n + (1 - bit))
                if step > 0:
                    outs[1][rows_n, :] = summed(2 * n + bit)

        if left == 0:
            n_outs = 1
            wide = cols + (0 if beside is None else beside.shape[1])
            more = [] if beside is None else [beside]
            return call_whole(body, shaped(rows, wide), table, held, got, *more)
        n_outs = 1 if step == 0 else 2
        out = shaped(rows * many // 2, cols)
        ins = [held] if step == 0 else [held, got]
        return call_whole(body, out if step == 0 else (out, out), table, *ins)

    held, got = values, None
    for step, bit in enumerate(bits):
        if step == 0:
            send = call(step, held, None)
        else:
            send, held = call(step, held, got)
        got = swap_f(send, bit)
    return call(len(bits), held, got)


def place_second(table, own, other, owners, rows, units, width):
    span = owners * units
    parts = units // rows

    def body(at, mine, theirs, fc1, fc2):
        for c in range(2):

            @pl.when(at[0] % 2 == c)
            def _(c=c):
                for ref, cc in ((mine, c), (theirs, 1 - c)):
                    for f in range(owners):
                        start = (2 * f + cc) * units
                        fc1[:, start : start + units] = ref[
                            :, f * units : (f + 1) * units
                        ].astype(f32)
                    for n in range(parts):
                        start = cc * units + n * rows
                        to = span + n * width
                        fc2[start : start + rows, :] = ref[:, to : to + width].astype(f32)

    outs = (shaped(rows, 2 * span, f32), shaped(2 * units, width, f32))
    return call_whole(body, outs, table, own, other)


def place_first(table, own, across, sums, near, seq_count, width):
    rows = own.shape[0]
    half = width // 2
    quarter = width // seq_count
    span = 3 * quarter

    def body(at, own, across, sums, near, proj, qkv):
        for s in range(seq_count):

            @pl.when(at[0] == s)
            def _(s=s):
                c = s % 2
                proj[:, c * half : (c + 1) * half] = sums[...].astype(f32)
                proj[:, (1 - c) * half : (2 - c) * half] = near[:, :half].astype(f32)
                parts = ((own, half), (near, half), (across, half), (near, half + span))
                for k, (ref, base) in enumerate(parts):
                    for t in range(3):
                        start = t * width + (s ^ k) * quarter
                        at_col = base + t * quarter
                        qkv[:, start : start + quarter] = ref[
                            :, at_col : at_col + quarter
                        ].astype(f32)

    outs = (shaped(rows, width, f32), shaped(rows, 3 * width, f32))
    return call_whole(body, outs, table, own, across, sums, near)


def heads_forward(qkv, scale_val):
    length = qkv.shape[0]
    flat = qkv.shape[1] // 3
    q, k, v = (a.reshape(length, flat // HEAD, HEAD) for a in jnp.split(qkv, 3, axis=1))
    scores = jnp.einsum("khd,qhd->hkq", k, q, preferred_element_type=f32) * scale_val
    top_val = jnp.max(scores, axis=1, keepdims=True)
    expd = jnp.exp(scores - top_val)
    totals = jnp.sum(expd, axis=1, keepdims=True)
    probs = (expd / totals).astype(bf16)
    out = jnp.einsum("hkq,khd->qhd", probs, v, preferred_element_type=f32)
    return out.astype(bf16).reshape(length, flat), top_val + jnp.log(totals)


def heads_backward(qkv, grad, lse, scale_val):
    length = qkv.shape[0]
    flat = qkv.shape[1] // 3
    heads = flat // HEAD
    block = min(256, length)
    steps = length // block

    def body(whole, grads, lse_here, out, q_at, k_at, kt_at, v_at, g_at, dq_at, sum_k, sum_v):
        i = pl.program_id(0)

        @pl.when(i == 0)
        def _():
            for h in range(heads):
                lo = h * HEAD
                q_at[h] = (whole[:, lo : lo + HEAD].astype(f32) * scale_val).astype(bf16)
                key = whole[:, flat + lo : flat + lo + HEAD]
                k_at[h] = key
                kt_at[h] = key.T
                v_at[h] = whole[:, 2 * flat + lo : 2 * flat + lo + HEAD]
                g_at[h] = grads[:, lo : lo + HEAD]
            sum_k[...] = jnp.zeros_like(sum_k)
            sum_v[...] = jnp.zeros_like(sum_v)

        rows = pl.ds(pl.multiple_of(i * block, block), block)

        def one_head(h):
            q = q_at[h, rows]
            g = g_at[h, rows]
            probs = jnp.exp(dot(k_at[h], q, ((1,), (1,))) - lse_here[h])
            grad_probs = dot(v_at[h], g, ((1,), (1,)))
            inner = jnp.sum(probs * grad_probs, axis=0, keepdims=True)
            grad_scores = (probs * (grad_probs - inner)).astype(bf16)
            dq_at[h] = dot(kt_at[h], grad_scores, ((1,), (0,))) * scale_val
            sum_k[h] += dot(grad_scores, q, ((1,), (0,)))
            sum_v[h] += dot(probs.astype(bf16), g, ((1,), (0,)))

        for h in range(heads):
            one_head(h)
        for h in range(heads):
            out[rows, h * HEAD : (h + 1) * HEAD] = dq_at[h].T.astype(bf16)

        @pl.when(i == steps - 1)
        def _():
            for h in range(heads):
                lo = flat + h * HEAD
                out[:, lo : lo + HEAD] = sum_k[h].astype(bf16)
                out[:, flat + lo : flat + lo + HEAD] = sum_v[h].astype(bf16)

    return pl.pallas_call(
        body,
        grid=(steps,),
        in_specs=[
            pl.BlockSpec((length, 3 * flat), lambda i: (0, 0)),
            pl.BlockSpec((length, flat), lambda i: (0, 0)),
            pl.BlockSpec((heads, 1, block), lambda i: (0, 0, i)),
        ],
        out_specs=pl.BlockSpec((length, 3 * flat), lambda i: (0, 0)),
        out_shape=shaped(length, 3 * flat),
        scratch_shapes=[
            pltpu.VMEM((heads, length, HEAD), bf16),
            pltpu.VMEM((heads, length, HEAD), bf16),
            pltpu.VMEM((heads, HEAD, length), bf16),
            pltpu.VMEM((heads, length, HEAD), bf16),
            pltpu.VMEM((heads, length, HEAD), bf16),
            pltpu.VMEM((heads, HEAD, block), f32),
            pltpu.VMEM((heads, length, HEAD), f32),
            pltpu.VMEM((heads, length, HEAD), f32),
        ],
        compiler_params=pltpu.CompilerParams(vmem_limit_bytes=24 * 2**20),
        cost_estimate=pl.CostEstimate(
            flops=10 * length * length * flat,
            bytes_accessed=16 * length * flat,
            transcendentals=heads * length * length,
        ),
    )(qkv, grad, lse)


def local_ring(
    latents_in,
    conditions,
    w_ada,
    b_ada,
    w_qkv,
    b_qv,
    w_proj,
    b_proj,
    w_fc1,
    b_fc1,
    w_fc2,
    b_fc2,
    out_grad,
):
    width = latents_in.shape[2]
    tokens = latents_in.shape[1]
    seq_count = lax.axis_size("seq")
    owners = lax.axis_size("fsdp")
    me = lax.axis_index("fsdp")
    place = lax.axis_index("seq")
    core = place % 2
    own_rows = w_ada.shape[0]
    quarter = width // seq_count
    half_width = width // 2
    units = w_fc2.shape[0] // 2
    span = owners * units
    parts = units // own_rows
    scale_val = HEAD ** (-0.5)
    table = make_table(place, me)

    condition = conditions[0]
    cond_act, silu_pull = jax.vjp(jax.nn.silu, condition)
    cond_low = cond_act.astype(bf16)
    small = [v.astype(f32)[None] for v in (cond_low, b_qv, b_proj, b_fc1, b_fc2)]
    first = ring_pieces(pack_first(table, w_proj, w_qkv, small, seq_count), own_rows // 2)
    second = ring_pieces(pack_second(table, w_fc1, w_fc2, owners), own_rows // 2)
    proj_half, use_qkv, cond_all, *biases = put_first(
        table, first, own_rows, width, quarter, [v.shape[1] for v in small]
    )
    use_proj = mix_proj(table, proj_half, seq_swap(proj_half, 1), seq_count)

    cond_rows = lax.dynamic_slice_in_dim(cond_all, me * own_rows, own_rows, 1)
    cond_rows = to_cube(cond_rows, me).astype(bf16)
    mod_partial = dot(cond_rows, w_ada, ((1,), (0,)))
    bias_at = b_ada.shape[0]
    owned = jnp.arange(owners)[:, None] == me
    placed_bias = jnp.where(owned, b_ada.astype(f32)[None, :], 0.0)
    mod_partial = mod_partial + placed_bias.reshape(1, owners * bias_at)
    modulation = cube_sum(mod_partial)
    shift_one, scale_one, gate_one, shift_two, scale_two, gate_two = jnp.split(modulation, 6)
    qv_full = biases[0].reshape(2, seq_count, quarter)
    bias_q, bias_v = lax.dynamic_index_in_dim(qv_full, place, 1, keepdims=False)
    bias_proj = biases[1].reshape(width)
    bias_fc1 = lax.dynamic_index_in_dim(
        biases[2].reshape(owners, 2, units), core, 1, keepdims=False
    ).reshape(span)
    bias_fc2 = biases[3].reshape(width)

    own_latent = latents_in[0]
    from_x = seq_swap(own_latent, 2)
    from_core = seq_swap(own_latent, 1)
    from_both = seq_swap(from_x, 1)
    all_latent = jnp.concatenate([own_latent, from_core, from_x, from_both]).astype(f32)
    latent = own_latent.astype(f32)
    grad_own = out_grad[0]
    grad_pair = jnp.concatenate([grad_own, seq_swap(grad_own, 1)]).astype(f32)
    grad_out = grad_own.astype(f32)

    normed_all = layer_norm(all_latent)
    act_one = (normed_all * (1.0 + scale_one) + shift_one).astype(bf16)
    bias_three = jnp.concatenate([bias_q, jnp.zeros_like(bias_q), bias_v])
    qkv = (dot(act_one, use_qkv, ((1,), (0,))) + bias_three).astype(bf16)
    attn_heads, lse = heads_forward(qkv, scale_val)

    def to_tokens(blocks):
        return [blocks[0]] + [seq_swap(blocks[k], k) for k in range(1, seq_count)]

    attn_own = jnp.concatenate(
        to_tokens([attn_heads[k * tokens : (k + 1) * tokens] for k in range(seq_count)]),
        axis=1,
    )
    branch_one = dot(attn_own, use_proj, ((1,), (0,))) + bias_proj
    middle = latent + gate_one * branch_one
    normed_two, norm_pull_two = jax.vjp(layer_norm, middle)
    act_two_own = (normed_two * (1.0 + scale_two) + shift_two).astype(bf16)

    act_two = jnp.concatenate([act_two_own, seq_swap(act_two_own, 1)])
    use_fc1, use_fc2 = assemble(
        second,
        [(0, own_rows, 0, 0, span)]
        + [(1, units, n * own_rows, span + n * width, width) for n in range(parts)],
        (shaped(width, span), shaped(span, width)),
        table,
    )
    hidden_pre = dot(act_two, use_fc1, ((1,), (0,))) + bias_fc1
    hidden_act, gelu_pull = jax.vjp(gelu_tanh, hidden_pre)
    hidden_low = hidden_act.astype(bf16)
    grad_two = (gate_two * grad_pair).astype(bf16)
    grad_hidden = dot(grad_two, use_fc2, ((1,), (1,)))
    grad_pre = gelu_pull(grad_hidden)[0].astype(bf16)
    far_act = dot(grad_pre[tokens:], use_fc1, ((1,), (1,)))
    near_act = dot(grad_pre[:tokens], use_fc1, ((1,), (1,)))
    grad_act_two = near_act + seq_swap(far_act, 1)

    grad_fc1 = dot(act_two, grad_pre, ((0,), (0,))).astype(bf16)
    grad_fc2 = dot(hidden_low, grad_two, ((0,), (0,))).astype(bf16)
    second_red = ring_sum(
        [grad_fc1, grad_fc2],
        [(0, 0, span)] + [(1, n * own_rows, width) for n in range(parts)],
        table,
        own_rows,
    )

    grad_shift_two = jnp.sum(grad_act_two, axis=0)
    grad_scale_two = jnp.sum(grad_act_two * normed_two, axis=0)
    grad_middle = grad_out + norm_pull_two(grad_act_two * (1.0 + scale_two))[0]
    grad_one = (gate_one * grad_middle).astype(bf16)
    grad_gate_one = jnp.sum(grad_middle * branch_one, axis=0)
    grad_attn = dot(grad_one, use_proj, ((1,), (1,))).astype(bf16)
    grad_heads = jnp.concatenate(
        to_tokens([grad_attn[:, k * quarter : (k + 1) * quarter] for k in range(seq_count)])
    )

    far_two = dot(hidden_low[tokens:], use_fc2, ((1,), (0,)))
    near_two = dot(hidden_low[:tokens], use_fc2, ((1,), (0,)))
    branch_two = near_two + seq_swap(far_two, 1) + bias_fc2
    result = middle + gate_two * branch_two
    grad_gate_two = jnp.sum(grad_out * branch_two, axis=0)
    grad_b_fc2 = jnp.sum(grad_two[:tokens].astype(f32), axis=0)
    grad_b_fc1 = jnp.sum(grad_pre.astype(f32), axis=0)
    grad_b_proj = jnp.sum(grad_one.astype(f32), axis=0)

    proj_rel = dot(attn_own, grad_one, ((0,), (0,))).astype(bf16)
    keep, give = split_proj(table, proj_rel, seq_count)
    proj_sum = (keep.astype(f32) + seq_swap(give, 1).astype(f32)).astype(bf16)

    grad_qkv = heads_backward(qkv, grad_heads, lse, scale_val)
    grad_own_qkv = dot(act_one, grad_qkv, ((0,), (0,))).astype(bf16)
    first_red = cube_reduce(
        grad_own_qkv, table, own_rows, beside=cube_reduce(proj_sum, table, own_rows)
    )
    first_x = seq_swap(first_red, 2)
    own_half = (
        first_red[:, :half_width].astype(f32) + first_x[:, :half_width].astype(f32)
    ).astype(bf16)
    mail = jnp.concatenate([own_half, first_red[:, half_width:], first_x[:, half_width:]], axis=1)
    grad_w_proj, grad_w_qkv = place_first(
        table, first_red, first_x, own_half, seq_swap(mail, 1), seq_count, width
    )
    second_sum = (second_red.astype(f32) + seq_swap(second_red, 2).astype(f32)).astype(bf16)
    grad_w_fc1, grad_w_fc2 = place_second(
        table, second_sum, seq_swap(second_sum, 1), owners, own_rows, units, width
    )

    partial_one = dot(grad_qkv, use_qkv, ((1,), (1,)))
    grad_shift_one = jnp.sum(partial_one, axis=0)
    grad_scale_one = jnp.sum(partial_one * normed_all, axis=0)
    far_low = partial_one[2 * tokens :].astype(bf16)
    far_sum = far_low[:tokens].astype(f32) + seq_swap(far_low[tokens:], 1).astype(f32)
    near_low = partial_one[tokens : 2 * tokens].astype(bf16)
    near_sum = partial_one[:tokens] + seq_swap(near_low, 1).astype(f32)
    grad_act_one = near_sum + seq_swap(far_sum.astype(bf16), 2).astype(f32)
    _, norm_pull_one = jax.vjp(layer_norm, latent)
    grad_latent = grad_middle + norm_pull_one(grad_act_one * (1.0 + scale_one))[0]

    qkv_sums = jnp.sum(grad_qkv.astype(f32), axis=0).reshape(3, 1, quarter)
    grad_b_qv = jnp.where(
        jnp.arange(seq_count)[None, :, None] == place,
        jnp.concatenate([qkv_sums[:1], qkv_sums[2:]]),
        0.0,
    ).reshape(2 * width)
    placed_fc1 = jnp.where(
        jnp.arange(2)[None, :, None] == core, grad_b_fc1.reshape(owners, 1, units), 0.0
    ).reshape(2 * span)
    terms = jnp.concatenate(
        [
            grad_shift_one,
            grad_scale_one,
            grad_gate_one,
            grad_shift_two,
            grad_scale_two,
            grad_gate_two,
            grad_b_qv,
            grad_b_proj,
            placed_fc1,
            grad_b_fc2,
        ]
    )
    pair_sum = terms + seq_swap(terms, 1)
    sums = pair_sum + seq_swap(pair_sum, 2)
    low_sums = sums.astype(bf16)
    got = cube_gather(low_sums[None])
    mod_rel = got[:, : 6 * width]
    all_sums = jnp.sum(got[:, 6 * width :].astype(f32), axis=0)
    owned_w_ada = dot(cond_rows, mod_rel, ((0,), (0,)))
    owned_b_ada = jnp.sum(
        lax.dynamic_slice_in_dim(mod_rel, me * bias_at, bias_at, 1).astype(f32), axis=0
    )
    cond_partial = dot(mod_rel, w_ada, ((1,), (1,)))
    cond_got = cube_to_order(cube_deal(cond_partial), me)
    grad_cond = silu_pull(cond_got.reshape(width))[0]
    at = 0
    owned_bias = []
    for b in (b_qv, b_proj, b_fc1, b_fc2):
        size = b.shape[0]
        owned_bias.append(lax.dynamic_slice_in_dim(all_sums, at + me * size, size, 0))
        at += size * owners
    return (
        result.astype(bf16)[None],
        grad_latent[None],
        grad_cond[None],
        owned_w_ada,
        owned_b_ada,
        grad_w_qkv,
        owned_bias[0],
        grad_w_proj,
        owned_bias[1],
        grad_w_fc1,
        owned_bias[2],
        grad_w_fc2,
        owned_bias[3],
    )


def short_axes(mesh):
    count = mesh.shape["fsdp"]
    return 2 < count <= RING_MAX and count & (count - 1) == 0 and mesh.shape["seq"] == 4


def local(*args):
    return local_ring(*args)


def solution(mesh):
    short = short_axes(mesh)
    return jax.shard_map(
        local if short else local_wide,
        mesh=mesh,
        in_specs=(
            P("fsdp", "seq", None),
            P("fsdp", None),
            P("fsdp", None),
            P("fsdp"),
            P("fsdp", None),
            P("fsdp"),
            P("fsdp", None),
            P("fsdp"),
            P("fsdp", None),
            P("fsdp"),
            P("fsdp", None),
            P("fsdp"),
            P("fsdp", "seq", None),
        ),
        out_specs=(
            P("fsdp", "seq", None),
            P("fsdp", "seq", None),
            P("fsdp", None),
            P("fsdp", None),
            P("fsdp"),
            P("fsdp", None),
            P("fsdp"),
            P("fsdp", None),
            P("fsdp"),
            P("fsdp", None),
            P("fsdp"),
            P("fsdp", None),
            P("fsdp"),
        ),
        check_vma=False,
    )
```

```python
import functools

import jax
import jax.numpy as jnp
from jax import lax
from jax.experimental import pallas as pl
from jax.experimental.pallas import tpu as pltpu
from jax.sharding import PartitionSpec as P


HEAD = 64
RING_MAX = 16

norm_eps = 1e-06
f32 = jnp.float32
bf16 = jnp.bfloat16


def dot(a, b, dims):
    return lax.dot_general(a, b, (dims, ((), ())), preferred_element_type=f32)


def layer_norm(values):
    mean_val = jnp.mean(values, axis=-1, keepdims=True)
    centred = values - mean_val
    var_val = jnp.mean(centred * centred, axis=-1, keepdims=True)
    return centred * lax.rsqrt(var_val + norm_eps)


def gelu_tanh(values):
    return jax.nn.gelu(values, approximate=True)


def seq_swap(values, bit):
    count = lax.axis_size("seq")
    return lax.ppermute(values, "seq", [(i, i ^ bit) for i in range(count)])


swap_core = functools.partial(seq_swap, bit=1)
swap_x = functools.partial(seq_swap, bit=2)


def rolled(rows, shift):
    count = rows.shape[0]
    return lax.dynamic_slice_in_dim(jnp.concatenate([rows, rows]), count - shift, count, 0)


def gather_small(row, me):
    count = lax.axis_size("fsdp")
    if count > RING_MAX:
        rows = lax.all_gather(row, "fsdp", axis=0)
        return rolled(rows[::-1], jnp.mod(me + 1, count))
    got = [row]
    for r in range(1, count):
        got.append(lax.ppermute(row, "fsdp", [(i, (i + r) % count) for i in range(count)]))
    return jnp.stack(got)


def deal_small(rows, me):
    count = lax.axis_size("fsdp")
    if count > RING_MAX:
        placed = rolled(rows[::-1], jnp.mod(me + 1, count))
        got = lax.all_to_all(placed, "fsdp", split_axis=0, concat_axis=0, tiled=True)
        return rolled(got, jnp.mod(count - me, count))
    got = [rows[0]]
    for r in range(1, count):
        got.append(lax.ppermute(rows[r], "fsdp", [(i, (i - r) % count) for i in range(count)]))
    return jnp.stack(got)


def ring_tables(count):
    order = list(range(0, count, 2)) + list(range(count - 1, 0, -2))
    ahead = [(order[i], order[(i + 1) % count]) for i in range(count)]
    return order, ahead, [(b, a) for a, b in ahead]


def ring_place(me, offset):
    count = lax.axis_size("fsdp")
    mine = jnp.where(me % 2 == 0, me // 2, count - 1 - me // 2)
    place = jnp.mod(mine + offset + count, count)
    return jnp.where(place < count // 2, 2 * place, 2 * (count - 1 - place) + 1)


def ring_gather(block, me):
    count = lax.axis_size("fsdp")
    if count > RING_MAX:
        return lax.all_gather(block, "fsdp", axis=0, tiled=True)
    _, ahead, back = ring_tables(count)
    rows = block.shape[0]
    half = rows // 2
    far = count // 2
    out = jnp.zeros((rows * count,) + block.shape[1:], block.dtype)

    def put(out, piece, offset, shift):
        start = ring_place(me, offset) * rows + shift
        return lax.dynamic_update_slice_in_dim(out, piece, start, 0)

    out = put(out, block, 0, 0)
    up = down = block
    for step in range(1, far + 1):
        if step == far:
            up, down = up[:half], down[half:]
        up = lax.ppermute(up, "fsdp", ahead)
        down = lax.ppermute(down, "fsdp", back)
        out = put(out, up, -step, 0)
        out = put(out, down, step, half if step == far else 0)
    return out


def ring_reduce(values, me):
    count = lax.axis_size("fsdp")
    rows = values.shape[0] // count
    if count > RING_MAX:
        return lax.psum_scatter(
            values.astype(bf16), "fsdp", scatter_dimension=0, tiled=True
        ).astype(f32)
    _, ahead, back = ring_tables(count)
    half = rows // 2
    far = count // 2

    def take(offset, start, size):
        return lax.dynamic_slice_in_dim(
            values, ring_place(me, offset) * rows + start, size, 0
        ).astype(f32)

    up = take(far, 0, half)
    down = take(-far, half, half)
    for step in range(1, far + 1):
        up = lax.ppermute(up.astype(bf16), "fsdp", ahead).astype(f32)
        down = lax.ppermute(down.astype(bf16), "fsdp", back).astype(f32)
        if step == far:
            break
        if step == 1:
            up = jnp.concatenate(
                [take(far - 1, 0, half) + up, take(far - 1, half, rows - half)]
            )
            down = jnp.concatenate(
                [take(1 - far, 0, half), take(1 - far, half, rows - half) + down]
            )
        else:
            up = up + take(far - step, 0, rows)
            down = down + take(step - far, 0, rows)
    return take(0, 0, rows) + up + down


def attend_forward(queries, keys, values, scale_val):
    rows = queries.shape[0]
    heads = queries.shape[1] // HEAD
    q = queries.reshape(rows, heads, HEAD)
    k = keys.reshape(rows, heads, HEAD)
    v = values.reshape(rows, heads, HEAD)
    scores = jnp.einsum("qhd,khd->hqk", q, k, preferred_element_type=f32) * scale_val
    top_val = jnp.max(scores, axis=-1, keepdims=True)
    expd_val = jnp.exp(scores - top_val)
    totals = jnp.sum(expd_val, axis=-1, keepdims=True)
    probs = (expd_val / totals).astype(bf16)
    out = jnp.einsum("hqk,khd->qhd", probs, v, preferred_element_type=f32)
    return out.astype(bf16).reshape(rows, heads * HEAD), (top_val + jnp.log(totals))


def attend_backward(queries, keys, values, grad, lse, scale_val):
    rows = queries.shape[0]
    heads = queries.shape[1] // HEAD
    q, k, v, g = (a.reshape(rows, heads, HEAD) for a in (queries, keys, values, grad))
    scores = jnp.einsum("qhd,khd->hqk", q, k, preferred_element_type=f32) * scale_val
    probs = jnp.exp(scores - lse)
    grad_probs = jnp.einsum("qhd,khd->hqk", g, v, preferred_element_type=f32)
    inner = jnp.sum(probs * grad_probs, axis=-1, keepdims=True)
    grad_scores = (probs * (grad_probs - inner)).astype(bf16)
    grad_q = jnp.einsum("hqk,khd->qhd", grad_scores, k, preferred_element_type=f32) * scale_val
    grad_k = jnp.einsum("hqk,qhd->khd", grad_scores, q, preferred_element_type=f32) * scale_val
    grad_v = jnp.einsum("hqk,qhd->khd", probs.astype(bf16), g, preferred_element_type=f32)
    flat = heads * HEAD
    return [a.astype(bf16).reshape(rows, flat) for a in (grad_q, grad_k, grad_v)]


def local_wide(
    latents_in,
    conditions,
    w_ada,
    b_ada,
    w_qkv,
    b_qv,
    w_proj,
    b_proj,
    w_fc1,
    b_fc1,
    w_fc2,
    b_fc2,
    out_grad,
):
    width = latents_in.shape[2]
    tokens = latents_in.shape[1]
    seq_count = lax.axis_size("seq")
    owners = lax.axis_size("fsdp")
    me = lax.axis_index("fsdp")
    place = lax.axis_index("seq")
    core = place % 2
    own_rows = w_ada.shape[0]
    quarter = width // seq_count
    units = w_fc2.shape[0] // 2
    scale_val = HEAD ** (-0.5)

    condition = conditions[0]
    cond_act, silu_pull = jax.vjp(jax.nn.silu, condition)
    cond_low = cond_act.astype(bf16)
    small = jnp.concatenate([cond_low, b_qv, b_proj, b_fc1, b_fc2])
    small_rel = gather_small(small, me)
    cond_rows = lax.dynamic_slice_in_dim(small_rel, me * own_rows, own_rows, 1)
    mod_partial = dot(cond_rows, w_ada, ((1,), (0,)))
    bias_at = b_ada.shape[0]
    placed_bias = jnp.where(
        jnp.arange(owners)[:, None] == me, b_ada.astype(f32)[None, :], 0.0
    ).reshape(1, owners * bias_at)
    mod_partial = mod_partial + placed_bias
    modulation = jnp.sum(deal_small(mod_partial, me), axis=0)
    shift_one, scale_one, gate_one, shift_two, scale_two, gate_two = jnp.split(modulation, 6)

    bias_rel = small_rel[:, width:].astype(f32)
    bias_all = rolled(bias_rel[::-1], jnp.mod(me + 1, owners))
    at = 0
    biases = []
    for b in (b_qv, b_proj, b_fc1, b_fc2):
        biases.append(bias_all[:, at : at + b.shape[0]])
        at += b.shape[0]
    qv_full = biases[0].reshape(2, seq_count, quarter)
    bias_q, bias_v = lax.dynamic_index_in_dim(qv_full, place, 1, keepdims=False)
    bias_proj = biases[1].reshape(width)
    bias_fc1 = lax.dynamic_index_in_dim(
        biases[2].reshape(owners, 2, units), core, 1, keepdims=False
    ).reshape(owners * units)
    bias_fc2 = biases[3].reshape(width)

    mine_qkv = lax.dynamic_index_in_dim(
        w_qkv.reshape(own_rows, 3, seq_count, quarter), place, 2, keepdims=False
    ).reshape(own_rows, 3 * quarter)
    use_qkv = ring_gather(mine_qkv, me)
    mine_proj = lax.dynamic_slice_in_dim(w_proj, core * (width // 2), width // 2, 1)
    proj_half = ring_gather(mine_proj, me)
    proj_other = swap_core(proj_half)
    full_proj = jnp.where(
        core == 0,
        jnp.concatenate([proj_half, proj_other], axis=1),
        jnp.concatenate([proj_other, proj_half], axis=1),
    )
    use_proj = jnp.concatenate(
        [
            lax.dynamic_slice_in_dim(full_proj, (place ^ k) * quarter, quarter, 0)
            for k in range(seq_count)
        ]
    )
    mine_fc1 = lax.dynamic_index_in_dim(
        w_fc1.reshape(own_rows, owners, 2, units), core, 2, keepdims=False
    ).reshape(own_rows, owners * units)
    use_fc1 = ring_gather(mine_fc1, me)
    mine_fc2 = lax.dynamic_slice_in_dim(w_fc2, core * units, units, 0)
    use_fc2 = ring_gather(mine_fc2, me)

    own_latent = latents_in[0]
    from_x = swap_x(own_latent)
    from_core = swap_core(own_latent)
    from_both = swap_core(from_x)
    all_latent = jnp.concatenate([own_latent, from_core, from_x, from_both]).astype(f32)
    latent = own_latent.astype(f32)
    grad_own = out_grad[0]
    grad_pair = jnp.concatenate([grad_own, swap_core(grad_own)]).astype(f32)
    grad_out = grad_own.astype(f32)

    normed_all = layer_norm(all_latent)
    act_one = (normed_all * (1.0 + scale_one) + shift_one).astype(bf16)
    bias_three = jnp.concatenate([bias_q, jnp.zeros_like(bias_q), bias_v])
    qkv = (dot(act_one, use_qkv, ((1,), (0,))) + bias_three).astype(bf16)
    queries, keys, values = jnp.split(qkv, 3, axis=1)
    attn_heads, lse = attend_forward(queries, keys, values, scale_val)

    def to_tokens(blocks):
        return [blocks[0]] + [seq_swap(blocks[k], k) for k in range(1, seq_count)]

    attn_own = jnp.concatenate(
        to_tokens([attn_heads[k * tokens : (k + 1) * tokens] for k in range(seq_count)]), axis=1
    )
    branch_one = dot(attn_own, use_proj, ((1,), (0,))) + bias_proj
    middle = latent + gate_one * branch_one
    normed_two, norm_pull_two = jax.vjp(layer_norm, middle)
    act_two_own = (normed_two * (1.0 + scale_two) + shift_two).astype(bf16)

    act_two = jnp.concatenate([act_two_own, swap_core(act_two_own)])
    hidden_pre = dot(act_two, use_fc1, ((1,), (0,))) + bias_fc1
    hidden_act, gelu_pull = jax.vjp(gelu_tanh, hidden_pre)
    hidden_low = hidden_act.astype(bf16)
    grad_two = (gate_two * grad_pair).astype(bf16)
    grad_hidden = dot(grad_two, use_fc2, ((1,), (1,)))
    grad_pre = gelu_pull(grad_hidden)[0].astype(bf16)
    partial_act = dot(grad_pre, use_fc1, ((1,), (1,)))
    grad_act_two = partial_act[:tokens] + swap_core(partial_act[tokens:])
    grad_shift_two = jnp.sum(grad_act_two, axis=0)
    grad_scale_two = jnp.sum(grad_act_two * normed_two, axis=0)
    grad_middle = grad_out + norm_pull_two(grad_act_two * (1.0 + scale_two))[0]
    grad_one = (gate_one * grad_middle).astype(bf16)
    grad_gate_one = jnp.sum(grad_middle * branch_one, axis=0)
    grad_attn = dot(grad_one, use_proj, ((1,), (1,))).astype(bf16)
    grad_heads = jnp.concatenate(
        to_tokens([grad_attn[:, k * quarter : (k + 1) * quarter] for k in range(seq_count)])
    )

    partial_two = dot(hidden_low, use_fc2, ((1,), (0,)))
    branch_two = partial_two[:tokens] + swap_core(partial_two[tokens:]) + bias_fc2
    result = middle + gate_two * branch_two
    grad_gate_two = jnp.sum(grad_out * branch_two, axis=0)
    grad_b_fc2 = jnp.sum(grad_two[:tokens].astype(f32), axis=0)
    grad_b_fc1 = jnp.sum(grad_pre.astype(f32), axis=0)
    grad_b_proj = jnp.sum(grad_one.astype(f32), axis=0)

    red_fc2 = ring_reduce(dot(hidden_low, grad_two, ((0,), (0,))).astype(bf16), me)
    red_fc1 = ring_reduce(dot(act_two, grad_pre, ((0,), (0,))).astype(bf16), me)

    def add_x(block):
        low = block.astype(bf16)
        return low.astype(f32) + swap_x(low).astype(f32)

    def in_core_order(block):
        other = swap_core(block)
        return jnp.where(core == 0, block, other), jnp.where(core == 0, other, block)

    grad_w_fc2 = jnp.concatenate(in_core_order(add_x(red_fc2)))
    first_fc1, second_fc1 = in_core_order(add_x(red_fc1))
    grad_w_fc1 = jnp.concatenate(
        [first_fc1.reshape(own_rows, owners, 1, units), second_fc1.reshape(own_rows, owners, 1, units)],
        axis=2,
    ).reshape(own_rows, 2 * owners * units)

    proj_rel = dot(attn_own, grad_one, ((0,), (0,))).astype(bf16)
    proj_abs = jnp.concatenate(
        [
            lax.dynamic_slice_in_dim(proj_rel, (place ^ k) * quarter, quarter, 0)
            for k in range(seq_count)
        ]
    )
    half_width = width // 2
    keep = lax.dynamic_slice_in_dim(proj_abs, core * half_width, half_width, 1)
    give = lax.dynamic_slice_in_dim(proj_abs, (1 - core) * half_width, half_width, 1)
    proj_sum = (keep.astype(f32) + swap_core(give).astype(f32)).astype(bf16)
    grad_w_proj = jnp.concatenate(in_core_order(add_x(ring_reduce(proj_sum, me))), axis=1)

    grad_q, grad_k, grad_v = attend_backward(queries, keys, values, grad_heads, lse, scale_val)
    grad_qkv = jnp.concatenate([grad_q, grad_k, grad_v], axis=1)
    red_qkv = ring_reduce(dot(act_one, grad_qkv, ((0,), (0,))).astype(bf16), me).astype(bf16)
    across = swap_x(red_qkv)
    blocks = [red_qkv, swap_core(red_qkv), across, swap_core(across)]
    for bit in (1, 2):
        flip = (place & bit) != 0
        blocks = [jnp.where(flip, blocks[j ^ bit], blocks[j]) for j in range(seq_count)]
    grad_w_qkv = jnp.concatenate(
        [b.astype(f32).reshape(own_rows, 3, 1, quarter) for b in blocks], axis=2
    ).reshape(own_rows, 3 * width)

    partial_one = dot(grad_qkv, use_qkv, ((1,), (1,)))
    grad_shift_one = jnp.sum(partial_one, axis=0)
    grad_scale_one = jnp.sum(partial_one * normed_all, axis=0)
    far_low = partial_one[2 * tokens :].astype(bf16)
    far_sum = far_low[:tokens].astype(f32) + swap_core(far_low[tokens:]).astype(f32)
    near_low = partial_one[tokens : 2 * tokens].astype(bf16)
    near_sum = partial_one[:tokens] + swap_core(near_low).astype(f32)
    grad_act_one = near_sum + swap_x(far_sum.astype(bf16)).astype(f32)
    _, norm_pull_one = jax.vjp(layer_norm, latent)
    grad_latent = grad_middle + norm_pull_one(grad_act_one * (1.0 + scale_one))[0]

    grad_b_qv = jnp.where(
        jnp.arange(seq_count)[None, :, None] == place,
        jnp.stack(
            [jnp.sum(grad_q.astype(f32), axis=0), jnp.sum(grad_v.astype(f32), axis=0)]
        )[:, None, :],
        0.0,
    ).reshape(2 * width)
    placed_fc1 = jnp.where(
        jnp.arange(2)[None, :, None] == core, grad_b_fc1.reshape(owners, 1, units), 0.0
    ).reshape(2 * owners * units)
    terms = jnp.concatenate(
        [
            grad_shift_one,
            grad_scale_one,
            grad_gate_one,
            grad_shift_two,
            grad_scale_two,
            grad_gate_two,
            grad_b_qv,
            grad_b_proj,
            placed_fc1,
            grad_b_fc2,
        ]
    )
    sums = (terms + seq_swap(terms, 1)) + (seq_swap(terms, 2) + seq_swap(terms, 3))
    low_sums = sums.astype(bf16)
    grad_mod = low_sums[: 6 * width]
    at = 6 * width
    by_owner = []
    for b in (b_qv, b_proj, b_fc1, b_fc2):
        size = b.shape[0] * owners
        by_owner.append(low_sums[at : at + size].reshape(owners, b.shape[0]))
        at += size
    by_owner = jnp.concatenate(by_owner, axis=1)
    sent_bias = rolled(by_owner[::-1], jnp.mod(me + 1, owners))
    mail = jnp.concatenate(
        [jnp.broadcast_to(grad_mod[None, :], (owners, 6 * width)), sent_bias], axis=1
    )
    got = deal_small(mail, me)
    mod_rel = got[:, : 6 * width]
    bias_sums = jnp.sum(got[:, 6 * width :].astype(f32), axis=0)
    back_cond = jnp.concatenate([cond_rows[:1], cond_rows[1:][::-1]])
    owned_w_ada = dot(back_cond, mod_rel, ((0,), (0,)))
    owned_b_ada = jnp.sum(
        lax.dynamic_slice_in_dim(mod_rel, me * bias_at, bias_at, 1).astype(f32), axis=0
    )
    cond_partial = dot(mod_rel, w_ada, ((1,), (1,)))
    back_partial = jnp.concatenate([cond_partial[:1], cond_partial[1:][::-1]])
    cond_got = rolled(deal_small(back_partial, me), me)
    grad_cond = silu_pull(cond_got.reshape(width))[0]
    at = 0
    owned_bias = []
    for b in (b_qv, b_proj, b_fc1, b_fc2):
        owned_bias.append(bias_sums[at : at + b.shape[0]])
        at += b.shape[0]
    return (
        result.astype(bf16)[None],
        grad_latent[None],
        grad_cond[None],
        owned_w_ada,
        owned_b_ada,
        grad_w_qkv,
        owned_bias[0],
        grad_w_proj,
        owned_bias[1],
        grad_w_fc1,
        owned_bias[2],
        grad_w_fc2,
        owned_bias[3],
    )


def swap_f(values, bit):
    count = lax.axis_size("fsdp")
    return lax.ppermute(values, "fsdp", [(i, i ^ bit) for i in range(count)])


def cube_bits():
    return [1 << b for b in range(lax.axis_size("fsdp").bit_length() - 1)]


def cube_places():
    places = [0]
    for bit in reversed(cube_bits()):
        places = places + [r | bit for r in places]
    return places


def cube_gather(row):
    rows = row
    for bit in reversed(cube_bits()):
        got = swap_f(rows, bit)
        rows = jnp.concatenate([rows, got])
    return rows


def cube_sum(rows):
    for bit in cube_bits():
        half = rows.shape[0] // 2
        got = swap_f(rows[half:], bit)
        rows = rows[:half] + got
    return rows[0]


def cube_deal(rows):
    count = rows.shape[0]
    done = 1
    for bit in cube_bits():
        parts = rows.reshape((done, 2, count // (2 * done)) + rows.shape[1:])
        got = swap_f(parts[:, 1], bit)
        rows = jnp.stack([parts[:, 0], got], axis=1).reshape(rows.shape)
        done *= 2
    return rows


def cube_to_order(rows, me):
    places = jnp.array(cube_places())
    count = rows.shape[0]
    hit = jnp.arange(count)[:, None] == jnp.bitwise_xor(places, me)[None, :]
    return jnp.sum(jnp.where(hit[:, :, None], rows[None], jnp.zeros_like(rows)[None]), axis=1)


SMEM = pl.BlockSpec(memory_space=pltpu.SMEM)
VMEM = pl.BlockSpec(memory_space=pltpu.VMEM)


def bytes_of(*arrays):
    return sum(a.size * a.dtype.itemsize for a in arrays)


def call_whole(body, outs, table, *arrays, scratch=()):
    return pl.pallas_call(
        body,
        out_shape=outs,
        in_specs=[SMEM] + [VMEM] * len(arrays),
        out_specs=jax.tree.map(lambda _: VMEM, outs),
        scratch_shapes=list(scratch),
        compiler_params=pltpu.CompilerParams(
            vmem_limit_bytes=bytes_of(*arrays) + bytes_of(*jax.tree.leaves(outs)) + 2**21
        ),
        cost_estimate=pl.CostEstimate(
            flops=0,
            bytes_accessed=bytes_of(*arrays) + bytes_of(*jax.tree.leaves(outs)),
            transcendentals=0,
        ),
    )(table, *arrays)


def shaped(rows, cols, dtype=bf16):
    return jax.ShapeDtypeStruct((rows, cols), dtype)


def make_table(place, me):
    count = lax.axis_size("fsdp")
    around = [ring_place(me, off) for off in range(count)]
    return jnp.stack([jnp.asarray(v, jnp.int32) for v in [place] + around])


def along(at, offset, count):
    return at[1 + offset % count]


def pack_first(table, w_proj, w_qkv, seq_count):
    rows, width = w_proj.shape
    half = width // 2
    quarter = width // seq_count

    def body(at, proj, qkv, out):
        for s in range(seq_count):

            @pl.when(at[0] == s)
            def _(s=s):
                out[:, :half] = proj[:, (s % 2) * half : (s % 2 + 1) * half]
                for t in range(3):
                    to = half + t * quarter
                    start = t * width + s * quarter
                    out[:, to : to + quarter] = qkv[:, start : start + quarter]

    outs = shaped(rows, half + 3 * quarter)
    return call_whole(body, outs, table, w_proj, w_qkv)


def pack_second(table, w_fc1, w_fc2, owners):
    rows = w_fc1.shape[0]
    width = w_fc2.shape[1]
    units = w_fc2.shape[0] // 2
    span = owners * units
    parts = units // rows

    def body(at, fc1, fc2, out):
        for c in range(2):

            @pl.when(at[0] % 2 == c)
            def _(c=c):
                for f in range(owners):
                    start = (2 * f + c) * units
                    out[:, f * units : (f + 1) * units] = fc1[:, start : start + units]
                for n in range(parts):
                    start = c * units + n * rows
                    to = span + n * width
                    out[:, to : to + width] = fc2[start : start + rows, :]

    outs = shaped(rows, span + parts * width)
    return call_whole(body, outs, table, w_fc1, w_fc2)


def ring_pieces(block, half):
    count = lax.axis_size("fsdp")
    _, ahead, back = ring_tables(count)
    far = count // 2
    pieces = [(0, 0, block)]
    up = down = block
    for step in range(1, far + 1):
        if step == far:
            up, down = up[:half], down[half:]
        up = lax.ppermute(up, "fsdp", ahead)
        down = lax.ppermute(down, "fsdp", back)
        pieces.append((-step, 0, up))
        pieces.append((step, half if step == far else 0, down))
    return pieces


def assemble(pieces, layout, outs, table):
    count = lax.axis_size("fsdp")
    offsets = [off for off, _, _ in pieces]
    shifts = [first for _, first, _ in pieces]

    def body(at, *refs):
        ins, results = refs[: len(pieces)], refs[len(pieces) :]
        for ref, off, shift in zip(ins, offsets, shifts):
            size = ref.shape[0]
            owner = along(at, off, count)
            for out, per, base, col, cols in layout:
                start = pl.multiple_of(owner * per + base + shift, 16)
                results[out][pl.ds(start, size), :] = ref[:, col : col + cols]

    return call_whole(body, outs, table, *[p for _, _, p in pieces])


def mix_proj(table, own, other, seq_count):
    width, half = own.shape
    quarter = width // seq_count

    def body(at, mine, theirs, out):
        for s in range(seq_count):

            @pl.when(at[0] == s)
            def _(s=s):
                c = s % 2
                for k in range(seq_count):
                    src = slice((s ^ k) * quarter, ((s ^ k) + 1) * quarter)
                    dst = slice(k * quarter, (k + 1) * quarter)
                    out[dst, c * half : (c + 1) * half] = mine[src, :]
                    out[dst, (1 - c) * half : (2 - c) * half] = theirs[src, :]

    return call_whole(body, shaped(width, width), table, own, other)


def split_proj(table, values, seq_count):
    width = values.shape[1]
    half = width // 2
    quarter = width // seq_count

    def body(at, ref, keep, give):
        for s in range(seq_count):

            @pl.when(at[0] == s)
            def _(s=s):
                c = s % 2
                for k in range(seq_count):
                    dst = slice((s ^ k) * quarter, ((s ^ k) + 1) * quarter)
                    src = slice(k * quarter, (k + 1) * quarter)
                    keep[dst, :] = ref[src, c * half : (c + 1) * half]
                    give[dst, :] = ref[src, (1 - c) * half : (2 - c) * half]

    return call_whole(body, (shaped(width, half), shaped(width, half)), table, values)


def ring_sum(arrays, layout, table, rows):
    count = lax.axis_size("fsdp")
    _, ahead, back = ring_tables(count)
    half = rows // 2
    far = count // 2
    total = sum(cols for _, _, cols in layout)

    def step_call(step, *got):
        def body(at, *refs):
            blocks, rest = refs[: len(arrays)], refs[len(arrays) :]
            up_at, down_at = along(at, far - step, count), along(at, step - far, count)

            def sixteen(line, carry):
                low = pl.ds(pl.multiple_of(line * 16, 16), 16)
                high = pl.ds(pl.multiple_of(half + line * 16, 16), 16)
                col = 0
                for a, base, cols in layout:
                    to = slice(col, col + cols)
                    col += cols
                    per = blocks[a].shape[0] // count

                    def own(owner, lo):
                        start = pl.multiple_of(owner * per + base + lo + line * 16, 16)
                        return blocks[a][pl.ds(start, 16), :]

                    def plus(owner, lo, *others):
                        total_val = own(owner, lo).astype(f32)
                        for ref, at_rows in others:
                            total_val = total_val + ref[at_rows, to].astype(f32)
                        return total_val.astype(bf16)

                    if step == 0:
                        rest[0][low, to] = own(up_at, 0)
                        rest[1][low, to] = own(down_at, half)
                    elif step == far:
                        up, down, out = rest
                        out[low, to] = plus(up_at, 0, (up, low), (down, low))
                        out[high, to] = plus(up_at, half, (up, high), (down, high))
                    else:
                        up, down, next_up, next_down = rest
                        next_up[low, to] = plus(up_at, 0, (up, low))
                        next_down[high, to] = plus(
                            down_at, half, (down, low if step == 1 else high)
                        )
                        if step == 1:
                            next_up[high, to] = own(up_at, half)
                            next_down[low, to] = own(down_at, 0)
                        else:
                            next_up[high, to] = plus(up_at, half, (up, high))
                            next_down[low, to] = plus(down_at, 0, (down, low))
                return carry

            lax.fori_loop(0, half // 16, sixteen, 0)

        out = shaped(half if step == 0 else rows, total)
        outs = out if step == far else (out, out)
        return call_whole(body, outs, table, *arrays, *got)

    up, down = step_call(0)
    for step in range(1, far + 1):
        up = lax.ppermute(up, "fsdp", ahead)
        down = lax.ppermute(down, "fsdp", back)
        if step < far:
            up, down = step_call(step, up, down)
    return step_call(far, up, down)


def cube_reduce(values, table, rows, beside=None):
    bits = cube_bits()
    cols = values.shape[1]

    def block(ref, index):
        return ref[pl.ds(pl.multiple_of(index * rows, 16), rows), :]

    def call(step, held, got):
        left = len(bits) - step
        many = 1 << left

        def body(at, *refs):
            ins, outs = refs[: len(refs) - n_outs], refs[len(refs) - n_outs :]
            me = at[1]

            def summed(n):
                if step == 0:
                    return block(ins[0], n)
                index = 2 * n + lax.rem(me >> (step - 1), 2) if step == 1 else n
                mine = block(ins[0], index)
                return (mine.astype(f32) + block(ins[1], n).astype(f32)).astype(bf16)

            if left == 0:
                if beside is None:
                    outs[0][...] = summed(0)
                else:
                    outs[0][:, : beside.shape[1]] = ins[-1][...]
                    outs[0][:, beside.shape[1] :] = summed(0)
                return
            bit = lax.rem(me >> step, 2)
            for n in range(many // 2):
                rows_n = slice(n * rows, (n + 1) * rows)
                outs[0][rows_n, :] = summed(2 * n + (1 - bit))
                if step > 0:
                    outs[1][rows_n, :] = summed(2 * n + bit)

        if left == 0:
            n_outs = 1
            wide = cols + (0 if beside is None else beside.shape[1])
            more = [] if beside is None else [beside]
            return call_whole(body, shaped(rows, wide), table, held, got, *more)
        n_outs = 1 if step == 0 else 2
        out = shaped(rows * many // 2, cols)
        ins = [held] if step == 0 else [held, got]
        return call_whole(body, out if step == 0 else (out, out), table, *ins)

    held, got = values, None
    for step, bit in enumerate(bits):
        if step == 0:
            send = call(step, held, None)
        else:
            send, held = call(step, held, got)
        got = swap_f(send, bit)
    return call(len(bits), held, got)


def place_second(table, own, other, owners, rows, units, width):
    span = owners * units
    parts = units // rows

    def body(at, mine, theirs, fc1, fc2):
        for c in range(2):

            @pl.when(at[0] % 2 == c)
            def _(c=c):
                for ref, cc in ((mine, c), (theirs, 1 - c)):
                    for f in range(owners):
                        start = (2 * f + cc) * units
                        fc1[:, start : start + units] = ref[
                            :, f * units : (f + 1) * units
                        ].astype(f32)
                    for n in range(parts):
                        start = cc * units + n * rows
                        to = span + n * width
                        fc2[start : start + rows, :] = ref[:, to : to + width].astype(f32)

    outs = (shaped(rows, 2 * span, f32), shaped(2 * units, width, f32))
    return call_whole(body, outs, table, own, other)


def place_first(table, own, across, sums, near, seq_count, width):
    rows = own.shape[0]
    half = width // 2
    quarter = width // seq_count
    span = 3 * quarter

    def body(at, own, across, sums, near, proj, qkv):
        for s in range(seq_count):

            @pl.when(at[0] == s)
            def _(s=s):
                c = s % 2
                proj[:, c * half : (c + 1) * half] = sums[...].astype(f32)
                proj[:, (1 - c) * half : (2 - c) * half] = near[:, :half].astype(f32)
                parts = ((own, half), (near, half), (across, half), (near, half + span))
                for k, (ref, base) in enumerate(parts):
                    for t in range(3):
                        start = t * width + (s ^ k) * quarter
                        at_col = base + t * quarter
                        qkv[:, start : start + quarter] = ref[
                            :, at_col : at_col + quarter
                        ].astype(f32)

    outs = (shaped(rows, width, f32), shaped(rows, 3 * width, f32))
    return call_whole(body, outs, table, own, across, sums, near)


def heads_forward(qkv, scale_val):
    length = qkv.shape[0]
    flat = qkv.shape[1] // 3
    heads = flat // HEAD
    block = min(256, length)

    def body(whole, out, lse, q_at, k_at, v_at, o_at):
        i = pl.program_id(0)

        @pl.when(i == 0)
        def _():
            for h in range(heads):
                lo = h * HEAD
                q_at[h] = (whole[:, lo : lo + HEAD].astype(f32) * scale_val).astype(bf16)
                k_at[h] = whole[:, flat + lo : flat + lo + HEAD]
                v_at[h] = whole[:, 2 * flat + lo : 2 * flat + lo + HEAD].T

        rows = pl.ds(pl.multiple_of(i * block, block), block)

        def one_head(h):
            scores = dot(k_at[h], q_at[h, rows], ((1,), (1,)))
            top_val = jnp.max(scores, axis=0, keepdims=True)
            expd = jnp.exp(scores - top_val)
            totals = jnp.sum(expd, axis=0, keepdims=True)
            probs = (expd * (1.0 / totals)).astype(bf16)
            o_at[h] = dot(v_at[h], probs, ((1,), (0,)))
            lse[h] = top_val + jnp.log(totals)

        for h in range(heads):
            one_head(h)
        for h in range(heads):
            out[:, h * HEAD : (h + 1) * HEAD] = o_at[h].T.astype(bf16)

    return pl.pallas_call(
        body,
        grid=(length // block,),
        in_specs=[pl.BlockSpec((length, 3 * flat), lambda i: (0, 0))],
        out_specs=[
            pl.BlockSpec((block, flat), lambda i: (i, 0)),
            pl.BlockSpec((heads, 1, block), lambda i: (0, 0, i)),
        ],
        out_shape=[shaped(length, flat), jax.ShapeDtypeStruct((heads, 1, length), f32)],
        scratch_shapes=[
            pltpu.VMEM((heads, length, HEAD), bf16),
            pltpu.VMEM((heads, length, HEAD), bf16),
            pltpu.VMEM((heads, HEAD, length), bf16),
            pltpu.VMEM((heads, HEAD, block), f32),
        ],
        compiler_params=pltpu.CompilerParams(vmem_limit_bytes=16 * 2**20),
        cost_estimate=pl.CostEstimate(
            flops=4 * length * length * flat,
            bytes_accessed=8 * length * flat,
            transcendentals=heads * length * length,
        ),
    )(qkv)


def heads_backward(qkv, grad, lse, scale_val, first, last, done=None):
    length = qkv.shape[0]
    flat = qkv.shape[1] // 3
    heads = last - first
    before = 0 if done is None else first * HEAD
    mine = heads * HEAD
    span = before + mine
    block = min(256, length)
    steps = length // block

    def body(whole, grads, lse_here, *refs):
        if done is not None:
            earlier, refs = refs[0], refs[1:]
        out, q_at, k_at, kt_at, v_at, g_at, dq_at, sum_k, sum_v = refs
        i = pl.program_id(0)

        @pl.when(i == 0)
        def _():
            for h in range(heads):
                lo = (first + h) * HEAD
                q_at[h] = (whole[:, lo : lo + HEAD].astype(f32) * scale_val).astype(bf16)
                key = whole[:, flat + lo : flat + lo + HEAD]
                k_at[h] = key
                kt_at[h] = key.T
                v_at[h] = whole[:, 2 * flat + lo : 2 * flat + lo + HEAD]
                g_at[h] = grads[:, lo : lo + HEAD]
            sum_k[...] = jnp.zeros_like(sum_k)
            sum_v[...] = jnp.zeros_like(sum_v)
            if done is not None:
                for t in range(3):
                    out[:, t * span : t * span + before] = earlier[:, t * before : (t + 1) * before]

        rows = pl.ds(pl.multiple_of(i * block, block), block)

        def one_head(h):
            q = q_at[h, rows]
            g = g_at[h, rows]
            probs = jnp.exp(dot(k_at[h], q, ((1,), (1,))) - lse_here[first + h])
            grad_probs = dot(v_at[h], g, ((1,), (1,)))
            inner = jnp.sum(probs * grad_probs, axis=0, keepdims=True)
            grad_scores = (probs * (grad_probs - inner)).astype(bf16)
            dq_at[h] = dot(kt_at[h], grad_scores, ((1,), (0,))) * scale_val
            sum_k[h] += dot(grad_scores, q, ((1,), (0,)))
            sum_v[h] += dot(probs.astype(bf16), g, ((1,), (0,)))

        for h in range(heads):
            one_head(h)
        for h in range(heads):
            lo = before + h * HEAD
            out[rows, lo : lo + HEAD] = dq_at[h].T.astype(bf16)

        @pl.when(i == steps - 1)
        def _():
            for h in range(heads):
                lo = span + before + h * HEAD
                out[:, lo : lo + HEAD] = sum_k[h].astype(bf16)
                out[:, span + lo : span + lo + HEAD] = sum_v[h].astype(bf16)

    def whole_block(shape):
        return pl.BlockSpec(shape, lambda i: (0, 0))

    ins = [qkv, grad, lse] + ([] if done is None else [done])
    more = [] if done is None else [whole_block(done.shape)]
    return pl.pallas_call(
        body,
        grid=(steps,),
        in_specs=[
            whole_block((length, 3 * flat)),
            whole_block((length, flat)),
            pl.BlockSpec((lse.shape[0], 1, block), lambda i: (0, 0, i)),
        ]
        + more,
        out_specs=whole_block((length, 3 * span)),
        out_shape=shaped(length, 3 * span),
        scratch_shapes=[
            pltpu.VMEM((heads, length, HEAD), bf16),
            pltpu.VMEM((heads, length, HEAD), bf16),
            pltpu.VMEM((heads, HEAD, length), bf16),
            pltpu.VMEM((heads, length, HEAD), bf16),
            pltpu.VMEM((heads, length, HEAD), bf16),
            pltpu.VMEM((heads, HEAD, block), f32),
            pltpu.VMEM((heads, length, HEAD), f32),
            pltpu.VMEM((heads, length, HEAD), f32),
        ],
        compiler_params=pltpu.CompilerParams(vmem_limit_bytes=24 * 2**20),
        cost_estimate=pl.CostEstimate(
            flops=10 * length * length * mine,
            bytes_accessed=16 * length * mine,
            transcendentals=heads * length * length,
        ),
    )(*ins)


def local_ring(
    latents_in,
    conditions,
    w_ada,
    b_ada,
    w_qkv,
    b_qv,
    w_proj,
    b_proj,
    w_fc1,
    b_fc1,
    w_fc2,
    b_fc2,
    out_grad,
):
    width = latents_in.shape[2]
    tokens = latents_in.shape[1]
    seq_count = lax.axis_size("seq")
    owners = lax.axis_size("fsdp")
    me = lax.axis_index("fsdp")
    place = lax.axis_index("seq")
    core = place % 2
    own_rows = w_ada.shape[0]
    quarter = width // seq_count
    half_width = width // 2
    units = w_fc2.shape[0] // 2
    span = owners * units
    parts = units // own_rows
    scale_val = HEAD ** (-0.5)
    table = make_table(place, me)

    first = ring_pieces(pack_first(table, w_proj, w_qkv, seq_count), own_rows // 2)
    second = ring_pieces(pack_second(table, w_fc1, w_fc2, owners), own_rows // 2)

    condition = conditions[0]
    cond_act, silu_pull = jax.vjp(jax.nn.silu, condition)
    cond_low = cond_act.astype(bf16)
    small = jnp.concatenate(
        [v.astype(f32)[None] for v in (cond_low, b_qv, b_proj, b_fc1, b_fc2)], axis=1
    )
    small_rel = cube_gather(small)
    cond_rows = lax.dynamic_slice_in_dim(small_rel, me * own_rows, own_rows, 1).astype(bf16)
    mod_partial = dot(cond_rows, w_ada, ((1,), (0,)))
    bias_at = b_ada.shape[0]
    owned = jnp.arange(owners)[:, None] == me
    placed_bias = jnp.where(owned, b_ada.astype(f32)[None, :], 0.0)
    mod_partial = mod_partial + placed_bias.reshape(1, owners * bias_at)
    modulation = cube_sum(mod_partial)
    shift_one, scale_one, gate_one, shift_two, scale_two, gate_two = jnp.split(modulation, 6)

    bias_all = cube_to_order(small_rel[:, width:], me)
    at = 0
    biases = []
    for b in (b_qv, b_proj, b_fc1, b_fc2):
        biases.append(bias_all[:, at : at + b.shape[0]])
        at += b.shape[0]
    qv_full = biases[0].reshape(2, seq_count, quarter)
    bias_q, bias_v = lax.dynamic_index_in_dim(qv_full, place, 1, keepdims=False)
    bias_proj = biases[1].reshape(width)
    bias_fc1 = lax.dynamic_index_in_dim(
        biases[2].reshape(owners, 2, units), core, 1, keepdims=False
    ).reshape(span)
    bias_fc2 = biases[3].reshape(width)

    proj_half, use_qkv = assemble(
        first,
        [(0, own_rows, 0, 0, half_width), (1, own_rows, 0, half_width, 3 * quarter)],
        (shaped(width, half_width), shaped(width, 3 * quarter)),
        table,
    )
    use_proj = mix_proj(table, proj_half, seq_swap(proj_half, 1), seq_count)

    own_latent = latents_in[0]
    from_x = seq_swap(own_latent, 2)
    from_core = seq_swap(own_latent, 1)
    from_both = seq_swap(from_x, 1)
    all_latent = jnp.concatenate([own_latent, from_core, from_x, from_both]).astype(f32)
    latent = own_latent.astype(f32)
    grad_own = out_grad[0]
    grad_pair = jnp.concatenate([grad_own, seq_swap(grad_own, 1)]).astype(f32)
    grad_out = grad_own.astype(f32)

    normed_all = layer_norm(all_latent)
    act_one = (normed_all * (1.0 + scale_one) + shift_one).astype(bf16)
    bias_three = jnp.concatenate([bias_q, jnp.zeros_like(bias_q), bias_v])
    qkv = (dot(act_one, use_qkv, ((1,), (0,))) + bias_three).astype(bf16)
    attn_heads, lse = heads_forward(qkv, scale_val)

    def to_tokens(blocks):
        return [blocks[0]] + [seq_swap(blocks[k], k) for k in range(1, seq_count)]

    attn_own = jnp.concatenate(
        to_tokens([attn_heads[k * tokens : (k + 1) * tokens] for k in range(seq_count)]),
        axis=1,
    )
    branch_one = dot(attn_own, use_proj, ((1,), (0,))) + bias_proj
    middle = latent + gate_one * branch_one
    normed_two, norm_pull_two = jax.vjp(layer_norm, middle)
    act_two_own = (normed_two * (1.0 + scale_two) + shift_two).astype(bf16)

    act_two = jnp.concatenate([act_two_own, seq_swap(act_two_own, 1)])
    use_fc1, use_fc2 = assemble(
        second,
        [(0, own_rows, 0, 0, span)]
        + [(1, units, n * own_rows, span + n * width, width) for n in range(parts)],
        (shaped(width, span), shaped(span, width)),
        table,
    )
    hidden_pre = dot(act_two, use_fc1, ((1,), (0,))) + bias_fc1
    hidden_act, gelu_pull = jax.vjp(gelu_tanh, hidden_pre)
    hidden_low = hidden_act.astype(bf16)
    grad_two = (gate_two * grad_pair).astype(bf16)
    grad_hidden = dot(grad_two, use_fc2, ((1,), (1,)))
    grad_pre = gelu_pull(grad_hidden)[0].astype(bf16)
    far_act = dot(grad_pre[tokens:], use_fc1, ((1,), (1,)))
    near_act = dot(grad_pre[:tokens], use_fc1, ((1,), (1,)))
    grad_act_two = near_act + seq_swap(far_act, 1)

    grad_fc1 = dot(act_two, grad_pre, ((0,), (0,))).astype(bf16)
    grad_fc2 = dot(hidden_low, grad_two, ((0,), (0,))).astype(bf16)
    second_red = ring_sum(
        [grad_fc1, grad_fc2],
        [(0, 0, span)] + [(1, n * own_rows, width) for n in range(parts)],
        table,
        own_rows,
    )

    grad_shift_two = jnp.sum(grad_act_two, axis=0)
    grad_scale_two = jnp.sum(grad_act_two * normed_two, axis=0)
    grad_middle = grad_out + norm_pull_two(grad_act_two * (1.0 + scale_two))[0]
    grad_one = (gate_one * grad_middle).astype(bf16)
    grad_gate_one = jnp.sum(grad_middle * branch_one, axis=0)
    grad_attn = dot(grad_one, use_proj, ((1,), (1,))).astype(bf16)
    grad_heads = jnp.concatenate(
        to_tokens([grad_attn[:, k * quarter : (k + 1) * quarter] for k in range(seq_count)])
    )

    far_two = dot(hidden_low[tokens:], use_fc2, ((1,), (0,)))
    near_two = dot(hidden_low[:tokens], use_fc2, ((1,), (0,)))
    branch_two = near_two + seq_swap(far_two, 1) + bias_fc2
    result = middle + gate_two * branch_two
    grad_gate_two = jnp.sum(grad_out * branch_two, axis=0)
    grad_b_fc2 = jnp.sum(grad_two[:tokens].astype(f32), axis=0)
    grad_b_fc1 = jnp.sum(grad_pre.astype(f32), axis=0)
    grad_b_proj = jnp.sum(grad_one.astype(f32), axis=0)

    proj_rel = dot(attn_own, grad_one, ((0,), (0,))).astype(bf16)
    keep, give = split_proj(table, proj_rel, seq_count)
    proj_sum = (keep.astype(f32) + seq_swap(give, 1).astype(f32)).astype(bf16)

    most = max(1, quarter // HEAD - 1)
    grad_most = heads_backward(qkv, grad_heads, lse, scale_val, 0, most)
    grad_qkv = heads_backward(
        qkv, grad_heads, lse, scale_val, most, quarter // HEAD, done=grad_most
    )
    grad_own_qkv = dot(act_one, grad_qkv, ((0,), (0,))).astype(bf16)
    first_red = cube_reduce(
        grad_own_qkv, table, own_rows, beside=cube_reduce(proj_sum, table, own_rows)
    )
    first_x = seq_swap(first_red, 2)
    own_half = (
        first_red[:, :half_width].astype(f32) + first_x[:, :half_width].astype(f32)
    ).astype(bf16)
    mail = jnp.concatenate([own_half, first_red[:, half_width:], first_x[:, half_width:]], axis=1)
    grad_w_proj, grad_w_qkv = place_first(
        table, first_red, first_x, own_half, seq_swap(mail, 1), seq_count, width
    )
    second_sum = (second_red.astype(f32) + seq_swap(second_red, 2).astype(f32)).astype(bf16)
    grad_w_fc1, grad_w_fc2 = place_second(
        table, second_sum, seq_swap(second_sum, 1), owners, own_rows, units, width
    )

    partial_one = dot(grad_qkv, use_qkv, ((1,), (1,)))
    grad_shift_one = jnp.sum(partial_one, axis=0)
    grad_scale_one = jnp.sum(partial_one * normed_all, axis=0)
    far_low = partial_one[2 * tokens :].astype(bf16)
    far_sum = far_low[:tokens].astype(f32) + seq_swap(far_low[tokens:], 1).astype(f32)
    near_low = partial_one[tokens : 2 * tokens].astype(bf16)
    near_sum = partial_one[:tokens] + seq_swap(near_low, 1).astype(f32)
    from_ox = seq_swap(far_sum.astype(bf16), 2)

    qkv_sums = jnp.sum(grad_qkv.astype(f32), axis=0).reshape(3, 1, quarter)
    grad_b_qv = jnp.where(
        jnp.arange(seq_count)[None, :, None] == place,
        jnp.concatenate([qkv_sums[:1], qkv_sums[2:]]),
        0.0,
    ).reshape(2 * width)
    placed_fc1 = jnp.where(
        jnp.arange(2)[None, :, None] == core, grad_b_fc1.reshape(owners, 1, units), 0.0
    ).reshape(2 * span)
    terms = jnp.concatenate(
        [
            grad_shift_one,
            grad_scale_one,
            grad_gate_one,
            grad_shift_two,
            grad_scale_two,
            grad_gate_two,
            grad_b_qv,
            grad_b_proj,
            placed_fc1,
            grad_b_fc2,
        ]
    )
    pair_sum = terms + seq_swap(terms, 1)
    sums = pair_sum + seq_swap(pair_sum, 2)
    low_sums = sums.astype(bf16)
    late_middle, late_latent, _ = lax.optimization_barrier((grad_middle, latent, low_sums))
    grad_act_one = near_sum + from_ox.astype(f32)
    _, norm_pull_one = jax.vjp(layer_norm, late_latent)
    grad_latent = late_middle + norm_pull_one(grad_act_one * (1.0 + scale_one))[0]
    got = cube_gather(low_sums[None])
    mod_rel = got[:, : 6 * width]
    all_sums = jnp.sum(got[:, 6 * width :].astype(f32), axis=0)
    owned_w_ada = dot(cond_rows, mod_rel, ((0,), (0,)))
    owned_b_ada = jnp.sum(
        lax.dynamic_slice_in_dim(mod_rel, me * bias_at, bias_at, 1).astype(f32), axis=0
    )
    cond_partial = dot(mod_rel, w_ada, ((1,), (1,)))
    cond_got = cube_to_order(cube_deal(cond_partial), me)
    grad_cond = silu_pull(cond_got.reshape(width))[0]
    at = 0
    owned_bias = []
    for b in (b_qv, b_proj, b_fc1, b_fc2):
        size = b.shape[0]
        owned_bias.append(lax.dynamic_slice_in_dim(all_sums, at + me * size, size, 0))
        at += size * owners
    return (
        result.astype(bf16)[None],
        grad_latent[None],
        grad_cond[None],
        owned_w_ada,
        owned_b_ada,
        grad_w_qkv,
        owned_bias[0],
        grad_w_proj,
        owned_bias[1],
        grad_w_fc1,
        owned_bias[2],
        grad_w_fc2,
        owned_bias[3],
    )


def short_axes(mesh):
    count = mesh.shape["fsdp"]
    return 2 < count <= RING_MAX and count & (count - 1) == 0 and mesh.shape["seq"] == 4


def local(*args):
    return local_ring(*args)


def solution(mesh):
    short = short_axes(mesh)
    return jax.shard_map(
        local if short else local_wide,
        mesh=mesh,
        in_specs=(
            P("fsdp", "seq", None),
            P("fsdp", None),
            P("fsdp", None),
            P("fsdp"),
            P("fsdp", None),
            P("fsdp"),
            P("fsdp", None),
            P("fsdp"),
            P("fsdp", None),
            P("fsdp"),
            P("fsdp", None),
            P("fsdp"),
            P("fsdp", "seq", None),
        ),
        out_specs=(
            P("fsdp", "seq", None),
            P("fsdp", "seq", None),
            P("fsdp", None),
            P("fsdp", None),
            P("fsdp"),
            P("fsdp", None),
            P("fsdp"),
            P("fsdp", None),
            P("fsdp"),
            P("fsdp", None),
            P("fsdp"),
            P("fsdp", None),
            P("fsdp"),
        ),
        check_vma=False,
    )
```

```python
import functools

import jax
import jax.numpy as jnp
from jax import lax
from jax.experimental import pallas as pl
from jax.experimental.pallas import tpu as pltpu
from jax.sharding import PartitionSpec as P


HEAD = 64
RING_MAX = 16

norm_eps = 1e-06
f32 = jnp.float32
bf16 = jnp.bfloat16


def dot(a, b, dims):
    return lax.dot_general(a, b, (dims, ((), ())), preferred_element_type=f32)


def layer_norm(values):
    mean_val = jnp.mean(values, axis=-1, keepdims=True)
    centred = values - mean_val
    var_val = jnp.mean(centred * centred, axis=-1, keepdims=True)
    return centred * lax.rsqrt(var_val + norm_eps)


def gelu_tanh(values):
    return jax.nn.gelu(values, approximate=True)


def seq_swap(values, bit):
    count = lax.axis_size("seq")
    return lax.ppermute(values, "seq", [(i, i ^ bit) for i in range(count)])


swap_core = functools.partial(seq_swap, bit=1)
swap_x = functools.partial(seq_swap, bit=2)


def rolled(rows, shift):
    count = rows.shape[0]
    return lax.dynamic_slice_in_dim(jnp.concatenate([rows, rows]), count - shift, count, 0)


def gather_small(row, me):
    count = lax.axis_size("fsdp")
    if count > RING_MAX:
        rows = lax.all_gather(row, "fsdp", axis=0)
        return rolled(rows[::-1], jnp.mod(me + 1, count))
    got = [row]
    for r in range(1, count):
        got.append(lax.ppermute(row, "fsdp", [(i, (i + r) % count) for i in range(count)]))
    return jnp.stack(got)


def deal_small(rows, me):
    count = lax.axis_size("fsdp")
    if count > RING_MAX:
        placed = rolled(rows[::-1], jnp.mod(me + 1, count))
        got = lax.all_to_all(placed, "fsdp", split_axis=0, concat_axis=0, tiled=True)
        return rolled(got, jnp.mod(count - me, count))
    got = [rows[0]]
    for r in range(1, count):
        got.append(lax.ppermute(rows[r], "fsdp", [(i, (i - r) % count) for i in range(count)]))
    return jnp.stack(got)


def ring_tables(count):
    order = list(range(0, count, 2)) + list(range(count - 1, 0, -2))
    ahead = [(order[i], order[(i + 1) % count]) for i in range(count)]
    return order, ahead, [(b, a) for a, b in ahead]


def ring_place(me, offset):
    count = lax.axis_size("fsdp")
    mine = jnp.where(me % 2 == 0, me // 2, count - 1 - me // 2)
    place = jnp.mod(mine + offset + count, count)
    return jnp.where(place < count // 2, 2 * place, 2 * (count - 1 - place) + 1)


def ring_gather(block, me):
    count = lax.axis_size("fsdp")
    if count > RING_MAX:
        return lax.all_gather(block, "fsdp", axis=0, tiled=True)
    _, ahead, back = ring_tables(count)
    rows = block.shape[0]
    half = rows // 2
    far = count // 2
    out = jnp.zeros((rows * count,) + block.shape[1:], block.dtype)

    def put(out, piece, offset, shift):
        start = ring_place(me, offset) * rows + shift
        return lax.dynamic_update_slice_in_dim(out, piece, start, 0)

    out = put(out, block, 0, 0)
    up = down = block
    for step in range(1, far + 1):
        if step == far:
            up, down = up[:half], down[half:]
        up = lax.ppermute(up, "fsdp", ahead)
        down = lax.ppermute(down, "fsdp", back)
        out = put(out, up, -step, 0)
        out = put(out, down, step, half if step == far else 0)
    return out


def ring_reduce(values, me):
    count = lax.axis_size("fsdp")
    rows = values.shape[0] // count
    if count > RING_MAX:
        return lax.psum_scatter(
            values.astype(bf16), "fsdp", scatter_dimension=0, tiled=True
        ).astype(f32)
    _, ahead, back = ring_tables(count)
    half = rows // 2
    far = count // 2

    def take(offset, start, size):
        return lax.dynamic_slice_in_dim(
            values, ring_place(me, offset) * rows + start, size, 0
        ).astype(f32)

    up = take(far, 0, half)
    down = take(-far, half, half)
    for step in range(1, far + 1):
        up = lax.ppermute(up.astype(bf16), "fsdp", ahead).astype(f32)
        down = lax.ppermute(down.astype(bf16), "fsdp", back).astype(f32)
        if step == far:
            break
        if step == 1:
            up = jnp.concatenate(
                [take(far - 1, 0, half) + up, take(far - 1, half, rows - half)]
            )
            down = jnp.concatenate(
                [take(1 - far, 0, half), take(1 - far, half, rows - half) + down]
            )
        else:
            up = up + take(far - step, 0, rows)
            down = down + take(step - far, 0, rows)
    return take(0, 0, rows) + up + down


def attend_forward(queries, keys, values, scale_val):
    rows = queries.shape[0]
    heads = queries.shape[1] // HEAD
    q = queries.reshape(rows, heads, HEAD)
    k = keys.reshape(rows, heads, HEAD)
    v = values.reshape(rows, heads, HEAD)
    scores = jnp.einsum("qhd,khd->hqk", q, k, preferred_element_type=f32) * scale_val
    top_val = jnp.max(scores, axis=-1, keepdims=True)
    expd_val = jnp.exp(scores - top_val)
    totals = jnp.sum(expd_val, axis=-1, keepdims=True)
    probs = (expd_val / totals).astype(bf16)
    out = jnp.einsum("hqk,khd->qhd", probs, v, preferred_element_type=f32)
    return out.astype(bf16).reshape(rows, heads * HEAD), (top_val + jnp.log(totals))


def attend_backward(queries, keys, values, grad, lse, scale_val):
    rows = queries.shape[0]
    heads = queries.shape[1] // HEAD
    q, k, v, g = (a.reshape(rows, heads, HEAD) for a in (queries, keys, values, grad))
    scores = jnp.einsum("qhd,khd->hqk", q, k, preferred_element_type=f32) * scale_val
    probs = jnp.exp(scores - lse)
    grad_probs = jnp.einsum("qhd,khd->hqk", g, v, preferred_element_type=f32)
    inner = jnp.sum(probs * grad_probs, axis=-1, keepdims=True)
    grad_scores = (probs * (grad_probs - inner)).astype(bf16)
    grad_q = jnp.einsum("hqk,khd->qhd", grad_scores, k, preferred_element_type=f32) * scale_val
    grad_k = jnp.einsum("hqk,qhd->khd", grad_scores, q, preferred_element_type=f32) * scale_val
    grad_v = jnp.einsum("hqk,qhd->khd", probs.astype(bf16), g, preferred_element_type=f32)
    flat = heads * HEAD
    return [a.astype(bf16).reshape(rows, flat) for a in (grad_q, grad_k, grad_v)]


def local_wide(
    latents_in,
    conditions,
    w_ada,
    b_ada,
    w_qkv,
    b_qv,
    w_proj,
    b_proj,
    w_fc1,
    b_fc1,
    w_fc2,
    b_fc2,
    out_grad,
):
    width = latents_in.shape[2]
    tokens = latents_in.shape[1]
    seq_count = lax.axis_size("seq")
    owners = lax.axis_size("fsdp")
    me = lax.axis_index("fsdp")
    place = lax.axis_index("seq")
    core = place % 2
    own_rows = w_ada.shape[0]
    quarter = width // seq_count
    units = w_fc2.shape[0] // 2
    scale_val = HEAD ** (-0.5)

    condition = conditions[0]
    cond_act, silu_pull = jax.vjp(jax.nn.silu, condition)
    cond_low = cond_act.astype(bf16)
    small = jnp.concatenate([cond_low, b_qv, b_proj, b_fc1, b_fc2])
    small_rel = gather_small(small, me)
    cond_rows = lax.dynamic_slice_in_dim(small_rel, me * own_rows, own_rows, 1)
    mod_partial = dot(cond_rows, w_ada, ((1,), (0,)))
    bias_at = b_ada.shape[0]
    placed_bias = jnp.where(
        jnp.arange(owners)[:, None] == me, b_ada.astype(f32)[None, :], 0.0
    ).reshape(1, owners * bias_at)
    mod_partial = mod_partial + placed_bias
    modulation = jnp.sum(deal_small(mod_partial, me), axis=0)
    shift_one, scale_one, gate_one, shift_two, scale_two, gate_two = jnp.split(modulation, 6)

    bias_rel = small_rel[:, width:].astype(f32)
    bias_all = rolled(bias_rel[::-1], jnp.mod(me + 1, owners))
    at = 0
    biases = []
    for b in (b_qv, b_proj, b_fc1, b_fc2):
        biases.append(bias_all[:, at : at + b.shape[0]])
        at += b.shape[0]
    qv_full = biases[0].reshape(2, seq_count, quarter)
    bias_q, bias_v = lax.dynamic_index_in_dim(qv_full, place, 1, keepdims=False)
    bias_proj = biases[1].reshape(width)
    bias_fc1 = lax.dynamic_index_in_dim(
        biases[2].reshape(owners, 2, units), core, 1, keepdims=False
    ).reshape(owners * units)
    bias_fc2 = biases[3].reshape(width)

    mine_qkv = lax.dynamic_index_in_dim(
        w_qkv.reshape(own_rows, 3, seq_count, quarter), place, 2, keepdims=False
    ).reshape(own_rows, 3 * quarter)
    use_qkv = ring_gather(mine_qkv, me)
    mine_proj = lax.dynamic_slice_in_dim(w_proj, core * (width // 2), width // 2, 1)
    proj_half = ring_gather(mine_proj, me)
    proj_other = swap_core(proj_half)
    full_proj = jnp.where(
        core == 0,
        jnp.concatenate([proj_half, proj_other], axis=1),
        jnp.concatenate([proj_other, proj_half], axis=1),
    )
    use_proj = jnp.concatenate(
        [
            lax.dynamic_slice_in_dim(full_proj, (place ^ k) * quarter, quarter, 0)
            for k in range(seq_count)
        ]
    )
    mine_fc1 = lax.dynamic_index_in_dim(
        w_fc1.reshape(own_rows, owners, 2, units), core, 2, keepdims=False
    ).reshape(own_rows, owners * units)
    use_fc1 = ring_gather(mine_fc1, me)
    mine_fc2 = lax.dynamic_slice_in_dim(w_fc2, core * units, units, 0)
    use_fc2 = ring_gather(mine_fc2, me)

    own_latent = latents_in[0]
    from_x = swap_x(own_latent)
    from_core = swap_core(own_latent)
    from_both = swap_core(from_x)
    all_latent = jnp.concatenate([own_latent, from_core, from_x, from_both]).astype(f32)
    latent = own_latent.astype(f32)
    grad_own = out_grad[0]
    grad_pair = jnp.concatenate([grad_own, swap_core(grad_own)]).astype(f32)
    grad_out = grad_own.astype(f32)

    normed_all = layer_norm(all_latent)
    act_one = (normed_all * (1.0 + scale_one) + shift_one).astype(bf16)
    bias_three = jnp.concatenate([bias_q, jnp.zeros_like(bias_q), bias_v])
    qkv = (dot(act_one, use_qkv, ((1,), (0,))) + bias_three).astype(bf16)
    queries, keys, values = jnp.split(qkv, 3, axis=1)
    attn_heads, lse = attend_forward(queries, keys, values, scale_val)

    def to_tokens(blocks):
        return [blocks[0]] + [seq_swap(blocks[k], k) for k in range(1, seq_count)]

    attn_own = jnp.concatenate(
        to_tokens([attn_heads[k * tokens : (k + 1) * tokens] for k in range(seq_count)]), axis=1
    )
    branch_one = dot(attn_own, use_proj, ((1,), (0,))) + bias_proj
    middle = latent + gate_one * branch_one
    normed_two, norm_pull_two = jax.vjp(layer_norm, middle)
    act_two_own = (normed_two * (1.0 + scale_two) + shift_two).astype(bf16)

    act_two = jnp.concatenate([act_two_own, swap_core(act_two_own)])
    hidden_pre = dot(act_two, use_fc1, ((1,), (0,))) + bias_fc1
    hidden_act, gelu_pull = jax.vjp(gelu_tanh, hidden_pre)
    hidden_low = hidden_act.astype(bf16)
    grad_two = (gate_two * grad_pair).astype(bf16)
    grad_hidden = dot(grad_two, use_fc2, ((1,), (1,)))
    grad_pre = gelu_pull(grad_hidden)[0].astype(bf16)
    partial_act = dot(grad_pre, use_fc1, ((1,), (1,)))
    grad_act_two = partial_act[:tokens] + swap_core(partial_act[tokens:])
    grad_shift_two = jnp.sum(grad_act_two, axis=0)
    grad_scale_two = jnp.sum(grad_act_two * normed_two, axis=0)
    grad_middle = grad_out + norm_pull_two(grad_act_two * (1.0 + scale_two))[0]
    grad_one = (gate_one * grad_middle).astype(bf16)
    grad_gate_one = jnp.sum(grad_middle * branch_one, axis=0)
    grad_attn = dot(grad_one, use_proj, ((1,), (1,))).astype(bf16)
    grad_heads = jnp.concatenate(
        to_tokens([grad_attn[:, k * quarter : (k + 1) * quarter] for k in range(seq_count)])
    )

    partial_two = dot(hidden_low, use_fc2, ((1,), (0,)))
    branch_two = partial_two[:tokens] + swap_core(partial_two[tokens:]) + bias_fc2
    result = middle + gate_two * branch_two
    grad_gate_two = jnp.sum(grad_out * branch_two, axis=0)
    grad_b_fc2 = jnp.sum(grad_two[:tokens].astype(f32), axis=0)
    grad_b_fc1 = jnp.sum(grad_pre.astype(f32), axis=0)
    grad_b_proj = jnp.sum(grad_one.astype(f32), axis=0)

    red_fc2 = ring_reduce(dot(hidden_low, grad_two, ((0,), (0,))).astype(bf16), me)
    red_fc1 = ring_reduce(dot(act_two, grad_pre, ((0,), (0,))).astype(bf16), me)

    def add_x(block):
        low = block.astype(bf16)
        return low.astype(f32) + swap_x(low).astype(f32)

    def in_core_order(block):
        other = swap_core(block)
        return jnp.where(core == 0, block, other), jnp.where(core == 0, other, block)

    grad_w_fc2 = jnp.concatenate(in_core_order(add_x(red_fc2)))
    first_fc1, second_fc1 = in_core_order(add_x(red_fc1))
    grad_w_fc1 = jnp.concatenate(
        [first_fc1.reshape(own_rows, owners, 1, units), second_fc1.reshape(own_rows, owners, 1, units)],
        axis=2,
    ).reshape(own_rows, 2 * owners * units)

    proj_rel = dot(attn_own, grad_one, ((0,), (0,))).astype(bf16)
    proj_abs = jnp.concatenate(
        [
            lax.dynamic_slice_in_dim(proj_rel, (place ^ k) * quarter, quarter, 0)
            for k in range(seq_count)
        ]
    )
    half_width = width // 2
    keep = lax.dynamic_slice_in_dim(proj_abs, core * half_width, half_width, 1)
    give = lax.dynamic_slice_in_dim(proj_abs, (1 - core) * half_width, half_width, 1)
    proj_sum = (keep.astype(f32) + swap_core(give).astype(f32)).astype(bf16)
    grad_w_proj = jnp.concatenate(in_core_order(add_x(ring_reduce(proj_sum, me))), axis=1)

    grad_q, grad_k, grad_v = attend_backward(queries, keys, values, grad_heads, lse, scale_val)
    grad_qkv = jnp.concatenate([grad_q, grad_k, grad_v], axis=1)
    red_qkv = ring_reduce(dot(act_one, grad_qkv, ((0,), (0,))).astype(bf16), me).astype(bf16)
    across = swap_x(red_qkv)
    blocks = [red_qkv, swap_core(red_qkv), across, swap_core(across)]
    for bit in (1, 2):
        flip = (place & bit) != 0
        blocks = [jnp.where(flip, blocks[j ^ bit], blocks[j]) for j in range(seq_count)]
    grad_w_qkv = jnp.concatenate(
        [b.astype(f32).reshape(own_rows, 3, 1, quarter) for b in blocks], axis=2
    ).reshape(own_rows, 3 * width)

    partial_one = dot(grad_qkv, use_qkv, ((1,), (1,)))
    grad_shift_one = jnp.sum(partial_one, axis=0)
    grad_scale_one = jnp.sum(partial_one * normed_all, axis=0)
    far_low = partial_one[2 * tokens :].astype(bf16)
    far_sum = far_low[:tokens].astype(f32) + swap_core(far_low[tokens:]).astype(f32)
    near_low = partial_one[tokens : 2 * tokens].astype(bf16)
    near_sum = partial_one[:tokens] + swap_core(near_low).astype(f32)
    grad_act_one = near_sum + swap_x(far_sum.astype(bf16)).astype(f32)
    _, norm_pull_one = jax.vjp(layer_norm, latent)
    grad_latent = grad_middle + norm_pull_one(grad_act_one * (1.0 + scale_one))[0]

    grad_b_qv = jnp.where(
        jnp.arange(seq_count)[None, :, None] == place,
        jnp.stack(
            [jnp.sum(grad_q.astype(f32), axis=0), jnp.sum(grad_v.astype(f32), axis=0)]
        )[:, None, :],
        0.0,
    ).reshape(2 * width)
    placed_fc1 = jnp.where(
        jnp.arange(2)[None, :, None] == core, grad_b_fc1.reshape(owners, 1, units), 0.0
    ).reshape(2 * owners * units)
    terms = jnp.concatenate(
        [
            grad_shift_one,
            grad_scale_one,
            grad_gate_one,
            grad_shift_two,
            grad_scale_two,
            grad_gate_two,
            grad_b_qv,
            grad_b_proj,
            placed_fc1,
            grad_b_fc2,
        ]
    )
    sums = (terms + seq_swap(terms, 1)) + (seq_swap(terms, 2) + seq_swap(terms, 3))
    low_sums = sums.astype(bf16)
    grad_mod = low_sums[: 6 * width]
    at = 6 * width
    by_owner = []
    for b in (b_qv, b_proj, b_fc1, b_fc2):
        size = b.shape[0] * owners
        by_owner.append(low_sums[at : at + size].reshape(owners, b.shape[0]))
        at += size
    by_owner = jnp.concatenate(by_owner, axis=1)
    sent_bias = rolled(by_owner[::-1], jnp.mod(me + 1, owners))
    mail = jnp.concatenate(
        [jnp.broadcast_to(grad_mod[None, :], (owners, 6 * width)), sent_bias], axis=1
    )
    got = deal_small(mail, me)
    mod_rel = got[:, : 6 * width]
    bias_sums = jnp.sum(got[:, 6 * width :].astype(f32), axis=0)
    back_cond = jnp.concatenate([cond_rows[:1], cond_rows[1:][::-1]])
    owned_w_ada = dot(back_cond, mod_rel, ((0,), (0,)))
    owned_b_ada = jnp.sum(
        lax.dynamic_slice_in_dim(mod_rel, me * bias_at, bias_at, 1).astype(f32), axis=0
    )
    cond_partial = dot(mod_rel, w_ada, ((1,), (1,)))
    back_partial = jnp.concatenate([cond_partial[:1], cond_partial[1:][::-1]])
    cond_got = rolled(deal_small(back_partial, me), me)
    grad_cond = silu_pull(cond_got.reshape(width))[0]
    at = 0
    owned_bias = []
    for b in (b_qv, b_proj, b_fc1, b_fc2):
        owned_bias.append(bias_sums[at : at + b.shape[0]])
        at += b.shape[0]
    return (
        result.astype(bf16)[None],
        grad_latent[None],
        grad_cond[None],
        owned_w_ada,
        owned_b_ada,
        grad_w_qkv,
        owned_bias[0],
        grad_w_proj,
        owned_bias[1],
        grad_w_fc1,
        owned_bias[2],
        grad_w_fc2,
        owned_bias[3],
    )


def swap_f(values, bit):
    count = lax.axis_size("fsdp")
    return lax.ppermute(values, "fsdp", [(i, i ^ bit) for i in range(count)])


def cube_bits():
    return [1 << b for b in range(lax.axis_size("fsdp").bit_length() - 1)]


def cube_places():
    places = [0]
    for bit in reversed(cube_bits()):
        places = places + [r | bit for r in places]
    return places


def cube_gather(row):
    rows = row
    for bit in reversed(cube_bits()):
        got = swap_f(rows, bit)
        rows = jnp.concatenate([rows, got])
    return rows


def cube_sum(rows):
    for bit in cube_bits():
        half = rows.shape[0] // 2
        got = swap_f(rows[half:], bit)
        rows = rows[:half] + got
    return rows[0]


def cube_deal(rows):
    count = rows.shape[0]
    done = 1
    for bit in cube_bits():
        parts = rows.reshape((done, 2, count // (2 * done)) + rows.shape[1:])
        got = swap_f(parts[:, 1], bit)
        rows = jnp.stack([parts[:, 0], got], axis=1).reshape(rows.shape)
        done *= 2
    return rows


def cube_to_order(rows, me):
    places = jnp.array(cube_places())
    count = rows.shape[0]
    hit = jnp.arange(count)[:, None] == jnp.bitwise_xor(places, me)[None, :]
    return jnp.sum(jnp.where(hit[:, :, None], rows[None], jnp.zeros_like(rows)[None]), axis=1)


SMEM = pl.BlockSpec(memory_space=pltpu.SMEM)
VMEM = pl.BlockSpec(memory_space=pltpu.VMEM)


def bytes_of(*arrays):
    return sum(a.size * a.dtype.itemsize for a in arrays)


def call_whole(body, outs, table, *arrays, scratch=()):
    return pl.pallas_call(
        body,
        out_shape=outs,
        in_specs=[SMEM] + [VMEM] * len(arrays),
        out_specs=jax.tree.map(lambda _: VMEM, outs),
        scratch_shapes=list(scratch),
        compiler_params=pltpu.CompilerParams(
            vmem_limit_bytes=bytes_of(*arrays) + bytes_of(*jax.tree.leaves(outs)) + 2**21
        ),
        cost_estimate=pl.CostEstimate(
            flops=0,
            bytes_accessed=bytes_of(*arrays) + bytes_of(*jax.tree.leaves(outs)),
            transcendentals=0,
        ),
    )(table, *arrays)


def shaped(rows, cols, dtype=bf16):
    return jax.ShapeDtypeStruct((rows, cols), dtype)


def make_table(place, me):
    count = lax.axis_size("fsdp")
    around = [ring_place(me, off) for off in range(count)]
    return jnp.stack([jnp.asarray(v, jnp.int32) for v in [place] + around])


def along(at, offset, count):
    return at[1 + offset % count]


LANES = 128


def bias_lines(sizes):
    lines = []
    for n, size in enumerate(sizes):
        for lo in range(0, size, LANES):
            lines.append((n, lo, min(LANES, size - lo)))
    return lines


def pack_first(table, w_proj, w_qkv, biases, seq_count):
    rows, width = w_proj.shape
    half = width // 2
    quarter = width // seq_count
    total = half + 3 * quarter

    def body(at, proj, qkv, *rest):
        small, out, lines = rest[: len(biases)], rest[len(biases)], rest[-1]
        lines[...] = jnp.zeros_like(lines)
        for line, (n, lo, size) in enumerate(bias_lines([b.shape[1] for b in biases])):
            lines[line : line + 1, :size] = small[n][:, lo : lo + size].astype(f32)
        out[:16, total:] = lines[...].astype(bf16)
        out[16:, total:] = jnp.zeros((rows - 16, LANES), bf16)
        for s in range(seq_count):

            @pl.when(at[0] == s)
            def _(s=s):
                out[:, :half] = proj[:, (s % 2) * half : (s % 2 + 1) * half]
                for t in range(3):
                    to = half + t * quarter
                    start = t * width + s * quarter
                    out[:, to : to + quarter] = qkv[:, start : start + quarter]

    outs = shaped(rows, total + LANES)
    scratch = [pltpu.VMEM((16, LANES), f32)]
    return call_whole(body, outs, table, w_proj, w_qkv, *biases, scratch=scratch)


def put_first(table, pieces, rows, width, quarter, sizes):
    count = lax.axis_size("fsdp")
    half = width // 2
    total = half + 3 * quarter
    offsets = [off for off, _, _ in pieces]
    shifts = [first for _, first, _ in pieces]

    def body(at, *refs):
        ins = refs[: len(pieces)]
        proj, qkv = refs[len(pieces) : len(pieces) + 2]
        kept = refs[-1]
        for ref, off, shift in zip(ins, offsets, shifts):
            size = ref.shape[0]
            owner = along(at, off, count)
            start = pl.multiple_of(owner * rows + shift, 16)
            proj[pl.ds(start, size), :] = ref[:, :half]
            qkv[pl.ds(start, size), :] = ref[:, half:total]
            if shift == 0:
                kept[pl.ds(pl.multiple_of(owner * 16, 16), 16), :] = ref[:16, total:]

    outs = (shaped(width, half), shaped(width, 3 * quarter), shaped(count * 16, LANES))
    proj, qkv, kept = call_whole(body, outs, table, *[p for _, _, p in pieces])
    kept = kept.reshape(count, 16, LANES).astype(f32)
    vectors = []
    for n in range(len(sizes)):
        parts = [kept[:, i, :z] for i, (m, _, z) in enumerate(bias_lines(sizes)) if m == n]
        vectors.append(jnp.concatenate(parts, axis=1))
    return proj, qkv, *vectors


def pack_second(table, w_fc1, w_fc2, owners):
    rows = w_fc1.shape[0]
    width = w_fc2.shape[1]
    units = w_fc2.shape[0] // 2
    span = owners * units
    parts = units // rows

    def body(at, fc1, fc2, out):
        for c in range(2):

            @pl.when(at[0] % 2 == c)
            def _(c=c):
                for f in range(owners):
                    start = (2 * f + c) * units
                    out[:, f * units : (f + 1) * units] = fc1[:, start : start + units]
                for n in range(parts):
                    start = c * units + n * rows
                    to = span + n * width
                    out[:, to : to + width] = fc2[start : start + rows, :]

    outs = shaped(rows, span + parts * width)
    return call_whole(body, outs, table, w_fc1, w_fc2)


def ring_pieces(block, half):
    count = lax.axis_size("fsdp")
    _, ahead, back = ring_tables(count)
    far = count // 2
    pieces = [(0, 0, block)]
    up = down = block
    for step in range(1, far + 1):
        if step == far:
            up, down = up[:half], down[half:]
        up = lax.ppermute(up, "fsdp", ahead)
        down = lax.ppermute(down, "fsdp", back)
        pieces.append((-step, 0, up))
        pieces.append((step, half if step == far else 0, down))
    return pieces


def assemble(pieces, layout, outs, table):
    count = lax.axis_size("fsdp")
    offsets = [off for off, _, _ in pieces]
    shifts = [first for _, first, _ in pieces]

    def body(at, *refs):
        ins, results = refs[: len(pieces)], refs[len(pieces) :]
        for ref, off, shift in zip(ins, offsets, shifts):
            size = ref.shape[0]
            owner = along(at, off, count)
            for out, per, base, col, cols in layout:
                start = pl.multiple_of(owner * per + base + shift, 16)
                results[out][pl.ds(start, size), :] = ref[:, col : col + cols]

    return call_whole(body, outs, table, *[p for _, _, p in pieces])


def mix_proj(table, own, other, seq_count):
    width, half = own.shape
    quarter = width // seq_count

    def body(at, mine, theirs, out):
        for s in range(seq_count):

            @pl.when(at[0] == s)
            def _(s=s):
                c = s % 2
                for k in range(seq_count):
                    src = slice((s ^ k) * quarter, ((s ^ k) + 1) * quarter)
                    dst = slice(k * quarter, (k + 1) * quarter)
                    out[dst, c * half : (c + 1) * half] = mine[src, :]
                    out[dst, (1 - c) * half : (2 - c) * half] = theirs[src, :]

    return call_whole(body, shaped(width, width), table, own, other)


def split_proj(table, values, seq_count):
    width = values.shape[1]
    half = width // 2
    quarter = width // seq_count

    def body(at, ref, keep, give):
        for s in range(seq_count):

            @pl.when(at[0] == s)
            def _(s=s):
                c = s % 2
                for k in range(seq_count):
                    dst = slice((s ^ k) * quarter, ((s ^ k) + 1) * quarter)
                    src = slice(k * quarter, (k + 1) * quarter)
                    keep[dst, :] = ref[src, c * half : (c + 1) * half]
                    give[dst, :] = ref[src, (1 - c) * half : (2 - c) * half]

    return call_whole(body, (shaped(width, half), shaped(width, half)), table, values)


def ring_sum(arrays, layout, table, rows):
    count = lax.axis_size("fsdp")
    _, ahead, back = ring_tables(count)
    half = rows // 2
    far = count // 2
    total = sum(cols for _, _, cols in layout)

    def step_call(step, *got):
        def body(at, *refs):
            blocks, rest = refs[: len(arrays)], refs[len(arrays) :]
            up_at, down_at = along(at, far - step, count), along(at, step - far, count)

            def sixteen(line, carry):
                low = pl.ds(pl.multiple_of(line * 16, 16), 16)
                high = pl.ds(pl.multiple_of(half + line * 16, 16), 16)
                col = 0
                for a, base, cols in layout:
                    to = slice(col, col + cols)
                    col += cols
                    per = blocks[a].shape[0] // count

                    def own(owner, lo):
                        start = pl.multiple_of(owner * per + base + lo + line * 16, 16)
                        return blocks[a][pl.ds(start, 16), :]

                    def plus(owner, lo, *others):
                        total_val = own(owner, lo).astype(f32)
                        for ref, at_rows in others:
                            total_val = total_val + ref[at_rows, to].astype(f32)
                        return total_val.astype(bf16)

                    if step == 0:
                        rest[0][low, to] = own(up_at, 0)
                        rest[1][low, to] = own(down_at, half)
                    elif step == far:
                        up, down, out = rest
                        out[low, to] = plus(up_at, 0, (up, low), (down, low))
                        out[high, to] = plus(up_at, half, (up, high), (down, high))
                    else:
                        up, down, next_up, next_down = rest
                        next_up[low, to] = plus(up_at, 0, (up, low))
                        next_down[high, to] = plus(
                            down_at, half, (down, low if step == 1 else high)
                        )
                        if step == 1:
                            next_up[high, to] = own(up_at, half)
                            next_down[low, to] = own(down_at, 0)
                        else:
                            next_up[high, to] = plus(up_at, half, (up, high))
                            next_down[low, to] = plus(down_at, 0, (down, low))
                return carry

            lax.fori_loop(0, half // 16, sixteen, 0)

        out = shaped(half if step == 0 else rows, total)
        outs = out if step == far else (out, out)
        return call_whole(body, outs, table, *arrays, *got)

    up, down = step_call(0)
    for step in range(1, far + 1):
        up = lax.ppermute(up, "fsdp", ahead)
        down = lax.ppermute(down, "fsdp", back)
        if step < far:
            up, down = step_call(step, up, down)
    return step_call(far, up, down)


def cube_reduce(values, table, rows, beside=None):
    bits = cube_bits()
    cols = values.shape[1]

    def block(ref, index):
        return ref[pl.ds(pl.multiple_of(index * rows, 16), rows), :]

    def call(step, held, got):
        left = len(bits) - step
        many = 1 << left

        def body(at, *refs):
            ins, outs = refs[: len(refs) - n_outs], refs[len(refs) - n_outs :]
            me = at[1]

            def summed(n):
                if step == 0:
                    return block(ins[0], n)
                index = 2 * n + lax.rem(me >> (step - 1), 2) if step == 1 else n
                mine = block(ins[0], index)
                return (mine.astype(f32) + block(ins[1], n).astype(f32)).astype(bf16)

            if left == 0:
                if beside is None:
                    outs[0][...] = summed(0)
                else:
                    outs[0][:, : beside.shape[1]] = ins[-1][...]
                    outs[0][:, beside.shape[1] :] = summed(0)
                return
            bit = lax.rem(me >> step, 2)
            for n in range(many // 2):
                rows_n = slice(n * rows, (n + 1) * rows)
                outs[0][rows_n, :] = summed(2 * n + (1 - bit))
                if step > 0:
                    outs[1][rows_n, :] = summed(2 * n + bit)

        if left == 0:
            n_outs = 1
            wide = cols + (0 if beside is None else beside.shape[1])
            more = [] if beside is None else [beside]
            return call_whole(body, shaped(rows, wide), table, held, got, *more)
        n_outs = 1 if step == 0 else 2
        out = shaped(rows * many // 2, cols)
        ins = [held] if step == 0 else [held, got]
        return call_whole(body, out if step == 0 else (out, out), table, *ins)

    held, got = values, None
    for step, bit in enumerate(bits):
        if step == 0:
            send = call(step, held, None)
        else:
            send, held = call(step, held, got)
        got = swap_f(send, bit)
    return call(len(bits), held, got)


def place_second(table, own, other, owners, rows, units, width):
    span = owners * units
    parts = units // rows

    def body(at, mine, theirs, fc1, fc2):
        for c in range(2):

            @pl.when(at[0] % 2 == c)
            def _(c=c):
                for ref, cc in ((mine, c), (theirs, 1 - c)):
                    for f in range(owners):
                        start = (2 * f + cc) * units
                        fc1[:, start : start + units] = ref[
                            :, f * units : (f + 1) * units
                        ].astype(f32)
                    for n in range(parts):
                        start = cc * units + n * rows
                        to = span + n * width
                        fc2[start : start + rows, :] = ref[:, to : to + width].astype(f32)

    outs = (shaped(rows, 2 * span, f32), shaped(2 * units, width, f32))
    return call_whole(body, outs, table, own, other)


def place_first(table, own, across, sums, near, seq_count, width):
    rows = own.shape[0]
    half = width // 2
    quarter = width // seq_count
    span = 3 * quarter

    def body(at, own, across, sums, near, proj, qkv):
        for s in range(seq_count):

            @pl.when(at[0] == s)
            def _(s=s):
                c = s % 2
                proj[:, c * half : (c + 1) * half] = sums[...].astype(f32)
                proj[:, (1 - c) * half : (2 - c) * half] = near[:, :half].astype(f32)
                parts = ((own, half), (near, half), (across, half), (near, half + span))
                for k, (ref, base) in enumerate(parts):
                    for t in range(3):
                        start = t * width + (s ^ k) * quarter
                        at_col = base + t * quarter
                        qkv[:, start : start + quarter] = ref[
                            :, at_col : at_col + quarter
                        ].astype(f32)

    outs = (shaped(rows, width, f32), shaped(rows, 3 * width, f32))
    return call_whole(body, outs, table, own, across, sums, near)


def heads_forward(qkv, scale_val):
    length = qkv.shape[0]
    flat = qkv.shape[1] // 3
    heads = flat // HEAD
    block = min(512, length)

    def body(whole, out, lse, q_at, k_at, v_at, o_at):
        i = pl.program_id(0)

        @pl.when(i == 0)
        def _():
            for h in range(heads):
                lo = h * HEAD
                q_at[h] = (whole[:, lo : lo + HEAD].astype(f32) * scale_val).astype(bf16)
                k_at[h] = whole[:, flat + lo : flat + lo + HEAD]
                v_at[h] = whole[:, 2 * flat + lo : 2 * flat + lo + HEAD].T

        rows = pl.ds(pl.multiple_of(i * block, block), block)

        def one_head(h):
            scores = dot(k_at[h], q_at[h, rows], ((1,), (1,)))
            top_val = jnp.max(scores, axis=0, keepdims=True)
            expd = jnp.exp(scores - top_val)
            totals = jnp.sum(expd, axis=0, keepdims=True)
            o_at[h] = dot(v_at[h], expd.astype(bf16), ((1,), (0,))) * (1.0 / totals)
            lse[h] = top_val + jnp.log(totals)

        for h in range(heads):
            one_head(h)
        for h in range(heads):
            out[:, h * HEAD : (h + 1) * HEAD] = o_at[h].T.astype(bf16)

    return pl.pallas_call(
        body,
        grid=(length // block,),
        in_specs=[pl.BlockSpec((length, 3 * flat), lambda i: (0, 0))],
        out_specs=[
            pl.BlockSpec((block, flat), lambda i: (i, 0)),
            pl.BlockSpec((heads, 1, block), lambda i: (0, 0, i)),
        ],
        out_shape=[shaped(length, flat), jax.ShapeDtypeStruct((heads, 1, length), f32)],
        scratch_shapes=[
            pltpu.VMEM((heads, length, HEAD), bf16),
            pltpu.VMEM((heads, length, HEAD), bf16),
            pltpu.VMEM((heads, HEAD, length), bf16),
            pltpu.VMEM((heads, HEAD, block), f32),
        ],
        compiler_params=pltpu.CompilerParams(vmem_limit_bytes=16 * 2**20),
        cost_estimate=pl.CostEstimate(
            flops=4 * length * length * flat,
            bytes_accessed=8 * length * flat,
            transcendentals=heads * length * length,
        ),
    )(qkv)


def heads_backward(qkv, grad, lse, scale_val, first, last, done=None):
    length = qkv.shape[0]
    flat = qkv.shape[1] // 3
    heads = last - first
    before = 0 if done is None else first * HEAD
    mine = heads * HEAD
    span = before + mine
    block = min(512, length)
    steps = length // block

    def body(whole, grads, lse_here, *refs):
        if done is not None:
            earlier, refs = refs[0], refs[1:]
        out, q_at, k_at, kt_at, v_at, g_at, dq_at, sum_k, sum_v = refs
        i = pl.program_id(0)

        @pl.when(i == 0)
        def _():
            for h in range(heads):
                lo = (first + h) * HEAD
                q_at[h] = (whole[:, lo : lo + HEAD].astype(f32) * scale_val).astype(bf16)
                key = whole[:, flat + lo : flat + lo + HEAD]
                k_at[h] = key
                kt_at[h] = key.T
                v_at[h] = whole[:, 2 * flat + lo : 2 * flat + lo + HEAD]
                g_at[h] = grads[:, lo : lo + HEAD]
            sum_k[...] = jnp.zeros_like(sum_k)
            sum_v[...] = jnp.zeros_like(sum_v)
            if done is not None:
                for t in range(3):
                    out[:, t * span : t * span + before] = earlier[:, t * before : (t + 1) * before]

        rows = pl.ds(pl.multiple_of(i * block, block), block)

        def one_head(h):
            q = q_at[h, rows]
            g = g_at[h, rows]
            probs = jnp.exp(dot(k_at[h], q, ((1,), (1,))) - lse_here[first + h])
            grad_probs = dot(v_at[h], g, ((1,), (1,)))
            inner = jnp.sum(probs * grad_probs, axis=0, keepdims=True)
            grad_scores = (probs * (grad_probs - inner)).astype(bf16)
            dq_at[h] = dot(kt_at[h], grad_scores, ((1,), (0,))) * scale_val
            sum_k[h] += dot(grad_scores, q, ((1,), (0,)))
            sum_v[h] += dot(probs.astype(bf16), g, ((1,), (0,)))

        for h in range(heads):
            one_head(h)
        for h in range(heads):
            lo = before + h * HEAD
            out[rows, lo : lo + HEAD] = dq_at[h].T.astype(bf16)

        @pl.when(i == steps - 1)
        def _():
            for h in range(heads):
                lo = span + before + h * HEAD
                out[:, lo : lo + HEAD] = sum_k[h].astype(bf16)
                out[:, span + lo : span + lo + HEAD] = sum_v[h].astype(bf16)

    def whole_block(shape):
        return pl.BlockSpec(shape, lambda i: (0, 0))

    ins = [qkv, grad, lse] + ([] if done is None else [done])
    more = [] if done is None else [whole_block(done.shape)]
    return pl.pallas_call(
        body,
        grid=(steps,),
        in_specs=[
            whole_block((length, 3 * flat)),
            whole_block((length, flat)),
            pl.BlockSpec((lse.shape[0], 1, block), lambda i: (0, 0, i)),
        ]
        + more,
        out_specs=whole_block((length, 3 * span)),
        out_shape=shaped(length, 3 * span),
        scratch_shapes=[
            pltpu.VMEM((heads, length, HEAD), bf16),
            pltpu.VMEM((heads, length, HEAD), bf16),
            pltpu.VMEM((heads, HEAD, length), bf16),
            pltpu.VMEM((heads, length, HEAD), bf16),
            pltpu.VMEM((heads, length, HEAD), bf16),
            pltpu.VMEM((heads, HEAD, block), f32),
            pltpu.VMEM((heads, length, HEAD), f32),
            pltpu.VMEM((heads, length, HEAD), f32),
        ],
        compiler_params=pltpu.CompilerParams(vmem_limit_bytes=24 * 2**20),
        cost_estimate=pl.CostEstimate(
            flops=10 * length * length * mine,
            bytes_accessed=16 * length * mine,
            transcendentals=heads * length * length,
        ),
    )(*ins)


def local_ring(
    latents_in,
    conditions,
    w_ada,
    b_ada,
    w_qkv,
    b_qv,
    w_proj,
    b_proj,
    w_fc1,
    b_fc1,
    w_fc2,
    b_fc2,
    out_grad,
):
    width = latents_in.shape[2]
    tokens = latents_in.shape[1]
    seq_count = lax.axis_size("seq")
    owners = lax.axis_size("fsdp")
    me = lax.axis_index("fsdp")
    place = lax.axis_index("seq")
    core = place % 2
    own_rows = w_ada.shape[0]
    quarter = width // seq_count
    half_width = width // 2
    units = w_fc2.shape[0] // 2
    span = owners * units
    parts = units // own_rows
    scale_val = HEAD ** (-0.5)
    table = make_table(place, me)

    small = [b.astype(f32)[None] for b in (b_qv, b_proj, b_fc1, b_fc2)]
    first = ring_pieces(pack_first(table, w_proj, w_qkv, small, seq_count), own_rows // 2)
    second = ring_pieces(pack_second(table, w_fc1, w_fc2, owners), own_rows // 2)

    condition = conditions[0]
    cond_act, silu_pull = jax.vjp(jax.nn.silu, condition)
    cond_low = cond_act.astype(bf16)
    cond_rel = cube_gather(cond_low.astype(f32)[None])
    cond_rows = lax.dynamic_slice_in_dim(cond_rel, me * own_rows, own_rows, 1).astype(bf16)
    mod_partial = dot(cond_rows, w_ada, ((1,), (0,)))
    bias_at = b_ada.shape[0]
    owned = jnp.arange(owners)[:, None] == me
    placed_bias = jnp.where(owned, b_ada.astype(f32)[None, :], 0.0)
    mod_partial = mod_partial + placed_bias.reshape(1, owners * bias_at)
    modulation = cube_sum(mod_partial)
    shift_one, scale_one, gate_one, shift_two, scale_two, gate_two = jnp.split(modulation, 6)

    proj_half, use_qkv, *biases = put_first(
        table, first, own_rows, width, quarter, [v.shape[1] for v in small]
    )
    use_proj = mix_proj(table, proj_half, seq_swap(proj_half, 1), seq_count)
    qv_full = biases[0].reshape(2, seq_count, quarter)
    bias_q, bias_v = lax.dynamic_index_in_dim(qv_full, place, 1, keepdims=False)
    bias_proj = biases[1].reshape(width)
    bias_fc1 = lax.dynamic_index_in_dim(
        biases[2].reshape(owners, 2, units), core, 1, keepdims=False
    ).reshape(span)
    bias_fc2 = biases[3].reshape(width)

    own_latent = latents_in[0]
    from_x = seq_swap(own_latent, 2)
    from_core = seq_swap(own_latent, 1)
    from_both = seq_swap(from_x, 1)
    all_latent = jnp.concatenate([own_latent, from_core, from_x, from_both]).astype(f32)
    latent = own_latent.astype(f32)
    grad_own = out_grad[0]
    grad_pair = jnp.concatenate([grad_own, seq_swap(grad_own, 1)]).astype(f32)
    grad_out = grad_own.astype(f32)

    normed_all = layer_norm(all_latent)
    act_one = (normed_all * (1.0 + scale_one) + shift_one).astype(bf16)
    bias_three = jnp.concatenate([bias_q, jnp.zeros_like(bias_q), bias_v])
    qkv = (dot(act_one, use_qkv, ((1,), (0,))) + bias_three).astype(bf16)
    attn_heads, lse = heads_forward(qkv, scale_val)

    def to_tokens(blocks):
        return [blocks[0]] + [seq_swap(blocks[k], k) for k in range(1, seq_count)]

    attn_own = jnp.concatenate(
        to_tokens([attn_heads[k * tokens : (k + 1) * tokens] for k in range(seq_count)]),
        axis=1,
    )
    branch_one = dot(attn_own, use_proj, ((1,), (0,))) + bias_proj
    middle = latent + gate_one * branch_one
    normed_two, norm_pull_two = jax.vjp(layer_norm, middle)
    act_two_own = (normed_two * (1.0 + scale_two) + shift_two).astype(bf16)

    act_two = jnp.concatenate([act_two_own, seq_swap(act_two_own, 1)])
    use_fc1, use_fc2 = assemble(
        second,
        [(0, own_rows, 0, 0, span)]
        + [(1, units, n * own_rows, span + n * width, width) for n in range(parts)],
        (shaped(width, span), shaped(span, width)),
        table,
    )
    hidden_pre = dot(act_two, use_fc1, ((1,), (0,))) + bias_fc1
    hidden_act, gelu_pull = jax.vjp(gelu_tanh, hidden_pre)
    hidden_low = hidden_act.astype(bf16)
    grad_two = (gate_two * grad_pair).astype(bf16)
    grad_hidden = dot(grad_two, use_fc2, ((1,), (1,)))
    grad_pre = gelu_pull(grad_hidden)[0].astype(bf16)
    far_act = dot(grad_pre[tokens:], use_fc1, ((1,), (1,)))
    near_act = dot(grad_pre[:tokens], use_fc1, ((1,), (1,)))
    grad_act_two = near_act + seq_swap(far_act, 1)

    grad_fc1 = dot(act_two, grad_pre, ((0,), (0,))).astype(bf16)
    grad_fc2 = dot(hidden_low, grad_two, ((0,), (0,))).astype(bf16)
    second_red = ring_sum(
        [grad_fc1, grad_fc2],
        [(0, 0, span)] + [(1, n * own_rows, width) for n in range(parts)],
        table,
        own_rows,
    )

    grad_shift_two = jnp.sum(grad_act_two, axis=0)
    grad_scale_two = jnp.sum(grad_act_two * normed_two, axis=0)
    grad_middle = grad_out + norm_pull_two(grad_act_two * (1.0 + scale_two))[0]
    grad_one = (gate_one * grad_middle).astype(bf16)
    grad_gate_one = jnp.sum(grad_middle * branch_one, axis=0)
    grad_attn = dot(grad_one, use_proj, ((1,), (1,))).astype(bf16)
    grad_heads = jnp.concatenate(
        to_tokens([grad_attn[:, k * quarter : (k + 1) * quarter] for k in range(seq_count)])
    )

    far_two = dot(hidden_low[tokens:], use_fc2, ((1,), (0,)))
    near_two = dot(hidden_low[:tokens], use_fc2, ((1,), (0,)))
    branch_two = near_two + seq_swap(far_two, 1) + bias_fc2
    result = middle + gate_two * branch_two
    grad_gate_two = jnp.sum(grad_out * branch_two, axis=0)
    grad_b_fc2 = jnp.sum(grad_two[:tokens].astype(f32), axis=0)
    grad_b_fc1 = jnp.sum(grad_pre.astype(f32), axis=0)
    grad_b_proj = jnp.sum(grad_one.astype(f32), axis=0)

    proj_rel = dot(attn_own, grad_one, ((0,), (0,))).astype(bf16)
    keep, give = split_proj(table, proj_rel, seq_count)
    proj_sum = (keep.astype(f32) + seq_swap(give, 1).astype(f32)).astype(bf16)

    most = max(1, quarter // HEAD - 1)
    grad_most = heads_backward(qkv, grad_heads, lse, scale_val, 0, most)
    grad_qkv = heads_backward(
        qkv, grad_heads, lse, scale_val, most, quarter // HEAD, done=grad_most
    )
    grad_own_qkv = dot(act_one, grad_qkv, ((0,), (0,))).astype(bf16)
    first_red = cube_reduce(
        grad_own_qkv, table, own_rows, beside=cube_reduce(proj_sum, table, own_rows)
    )
    first_x = seq_swap(first_red, 2)
    own_half = (
        first_red[:, :half_width].astype(f32) + first_x[:, :half_width].astype(f32)
    ).astype(bf16)
    mail = jnp.concatenate([own_half, first_red[:, half_width:], first_x[:, half_width:]], axis=1)
    grad_w_proj, grad_w_qkv = place_first(
        table, first_red, first_x, own_half, seq_swap(mail, 1), seq_count, width
    )
    second_sum = (second_red.astype(f32) + seq_swap(second_red, 2).astype(f32)).astype(bf16)
    grad_w_fc1, grad_w_fc2 = place_second(
        table, second_sum, seq_swap(second_sum, 1), owners, own_rows, units, width
    )

    partial_one = dot(grad_qkv, use_qkv, ((1,), (1,)))
    grad_shift_one = jnp.sum(partial_one, axis=0)
    grad_scale_one = jnp.sum(partial_one * normed_all, axis=0)
    far_low = partial_one[2 * tokens :].astype(bf16)
    far_sum = far_low[:tokens].astype(f32) + seq_swap(far_low[tokens:], 1).astype(f32)
    near_low = partial_one[tokens : 2 * tokens].astype(bf16)
    near_sum = partial_one[:tokens] + seq_swap(near_low, 1).astype(f32)
    from_ox = seq_swap(far_sum.astype(bf16), 2)

    qkv_sums = jnp.sum(grad_qkv.astype(f32), axis=0).reshape(3, 1, quarter)
    grad_b_qv = jnp.where(
        jnp.arange(seq_count)[None, :, None] == place,
        jnp.concatenate([qkv_sums[:1], qkv_sums[2:]]),
        0.0,
    ).reshape(2 * width)
    placed_fc1 = jnp.where(
        jnp.arange(2)[None, :, None] == core, grad_b_fc1.reshape(owners, 1, units), 0.0
    ).reshape(2 * span)
    terms = jnp.concatenate(
        [
            grad_shift_one,
            grad_scale_one,
            grad_gate_one,
            grad_shift_two,
            grad_scale_two,
            grad_gate_two,
            grad_b_qv,
            grad_b_proj,
            placed_fc1,
            grad_b_fc2,
        ]
    )
    pair_sum = terms + seq_swap(terms, 1)
    sums = pair_sum + seq_swap(pair_sum, 2)
    low_sums = sums.astype(bf16)
    late_middle, late_latent, _ = lax.optimization_barrier((grad_middle, latent, low_sums))
    grad_act_one = near_sum + from_ox.astype(f32)
    _, norm_pull_one = jax.vjp(layer_norm, late_latent)
    grad_latent = late_middle + norm_pull_one(grad_act_one * (1.0 + scale_one))[0]
    got = cube_gather(low_sums[None])
    mod_rel = got[:, : 6 * width]
    all_sums = jnp.sum(got[:, 6 * width :].astype(f32), axis=0)
    owned_w_ada = dot(cond_rows, mod_rel, ((0,), (0,)))
    owned_b_ada = jnp.sum(
        lax.dynamic_slice_in_dim(mod_rel, me * bias_at, bias_at, 1).astype(f32), axis=0
    )
    cond_partial = dot(mod_rel, w_ada, ((1,), (1,)))
    cond_got = cube_to_order(cube_deal(cond_partial), me)
    grad_cond = silu_pull(cond_got.reshape(width))[0]
    at = 0
    owned_bias = []
    for b in (b_qv, b_proj, b_fc1, b_fc2):
        size = b.shape[0]
        owned_bias.append(lax.dynamic_slice_in_dim(all_sums, at + me * size, size, 0))
        at += size * owners
    return (
        result.astype(bf16)[None],
        grad_latent[None],
        grad_cond[None],
        owned_w_ada,
        owned_b_ada,
        grad_w_qkv,
        owned_bias[0],
        grad_w_proj,
        owned_bias[1],
        grad_w_fc1,
        owned_bias[2],
        grad_w_fc2,
        owned_bias[3],
    )


def short_axes(mesh):
    count = mesh.shape["fsdp"]
    return 2 < count <= RING_MAX and count & (count - 1) == 0 and mesh.shape["seq"] == 4


def local(*args):
    return local_ring(*args)


def solution(mesh):
    short = short_axes(mesh)
    return jax.shard_map(
        local if short else local_wide,
        mesh=mesh,
        in_specs=(
            P("fsdp", "seq", None),
            P("fsdp", None),
            P("fsdp", None),
            P("fsdp"),
            P("fsdp", None),
            P("fsdp"),
            P("fsdp", None),
            P("fsdp"),
            P("fsdp", None),
            P("fsdp"),
            P("fsdp", None),
            P("fsdp"),
            P("fsdp", "seq", None),
        ),
        out_specs=(
            P("fsdp", "seq", None),
            P("fsdp", "seq", None),
            P("fsdp", None),
            P("fsdp", None),
            P("fsdp"),
            P("fsdp", None),
            P("fsdp"),
            P("fsdp", None),
            P("fsdp"),
            P("fsdp", None),
            P("fsdp"),
            P("fsdp", None),
            P("fsdp"),
        ),
        check_vma=False,
    )
```

```python
import functools

import jax
import jax.numpy as jnp
from jax import lax
from jax.experimental import pallas as pl
from jax.experimental.pallas import tpu as pltpu
from jax.sharding import PartitionSpec as P


HEAD = 64
RING_MAX = 16

norm_eps = 1e-06
f32 = jnp.float32
bf16 = jnp.bfloat16


def dot(a, b, dims):
    return lax.dot_general(a, b, (dims, ((), ())), preferred_element_type=f32)


def layer_norm(values):
    mean_val = jnp.mean(values, axis=-1, keepdims=True)
    centred = values - mean_val
    var_val = jnp.mean(centred * centred, axis=-1, keepdims=True)
    return centred * lax.rsqrt(var_val + norm_eps)


def gelu_tanh(values):
    return jax.nn.gelu(values, approximate=True)


def seq_swap(values, bit):
    count = lax.axis_size("seq")
    return lax.ppermute(values, "seq", [(i, i ^ bit) for i in range(count)])


swap_core = functools.partial(seq_swap, bit=1)
swap_x = functools.partial(seq_swap, bit=2)


def rolled(rows, shift):
    count = rows.shape[0]
    return lax.dynamic_slice_in_dim(jnp.concatenate([rows, rows]), count - shift, count, 0)


def gather_small(row, me):
    count = lax.axis_size("fsdp")
    if count > RING_MAX:
        rows = lax.all_gather(row, "fsdp", axis=0)
        return rolled(rows[::-1], jnp.mod(me + 1, count))
    got = [row]
    for r in range(1, count):
        got.append(lax.ppermute(row, "fsdp", [(i, (i + r) % count) for i in range(count)]))
    return jnp.stack(got)


def deal_small(rows, me):
    count = lax.axis_size("fsdp")
    if count > RING_MAX:
        placed = rolled(rows[::-1], jnp.mod(me + 1, count))
        got = lax.all_to_all(placed, "fsdp", split_axis=0, concat_axis=0, tiled=True)
        return rolled(got, jnp.mod(count - me, count))
    got = [rows[0]]
    for r in range(1, count):
        got.append(lax.ppermute(rows[r], "fsdp", [(i, (i - r) % count) for i in range(count)]))
    return jnp.stack(got)


def ring_tables(count):
    order = list(range(0, count, 2)) + list(range(count - 1, 0, -2))
    ahead = [(order[i], order[(i + 1) % count]) for i in range(count)]
    return order, ahead, [(b, a) for a, b in ahead]


def ring_place(me, offset):
    count = lax.axis_size("fsdp")
    mine = jnp.where(me % 2 == 0, me // 2, count - 1 - me // 2)
    place = jnp.mod(mine + offset + count, count)
    return jnp.where(place < count // 2, 2 * place, 2 * (count - 1 - place) + 1)


def ring_gather(block, me):
    count = lax.axis_size("fsdp")
    if count > RING_MAX:
        return lax.all_gather(block, "fsdp", axis=0, tiled=True)
    _, ahead, back = ring_tables(count)
    rows = block.shape[0]
    half = rows // 2
    far = count // 2
    out = jnp.zeros((rows * count,) + block.shape[1:], block.dtype)

    def put(out, piece, offset, shift):
        start = ring_place(me, offset) * rows + shift
        return lax.dynamic_update_slice_in_dim(out, piece, start, 0)

    out = put(out, block, 0, 0)
    up = down = block
    for step in range(1, far + 1):
        if step == far:
            up, down = up[:half], down[half:]
        up = lax.ppermute(up, "fsdp", ahead)
        down = lax.ppermute(down, "fsdp", back)
        out = put(out, up, -step, 0)
        out = put(out, down, step, half if step == far else 0)
    return out


def ring_reduce(values, me):
    count = lax.axis_size("fsdp")
    rows = values.shape[0] // count
    if count > RING_MAX:
        return lax.psum_scatter(
            values.astype(bf16), "fsdp", scatter_dimension=0, tiled=True
        ).astype(f32)
    _, ahead, back = ring_tables(count)
    half = rows // 2
    far = count // 2

    def take(offset, start, size):
        return lax.dynamic_slice_in_dim(
            values, ring_place(me, offset) * rows + start, size, 0
        ).astype(f32)

    up = take(far, 0, half)
    down = take(-far, half, half)
    for step in range(1, far + 1):
        up = lax.ppermute(up.astype(bf16), "fsdp", ahead).astype(f32)
        down = lax.ppermute(down.astype(bf16), "fsdp", back).astype(f32)
        if step == far:
            break
        if step == 1:
            up = jnp.concatenate(
                [take(far - 1, 0, half) + up, take(far - 1, half, rows - half)]
            )
            down = jnp.concatenate(
                [take(1 - far, 0, half), take(1 - far, half, rows - half) + down]
            )
        else:
            up = up + take(far - step, 0, rows)
            down = down + take(step - far, 0, rows)
    return take(0, 0, rows) + up + down


def attend_forward(queries, keys, values, scale_val):
    rows = queries.shape[0]
    heads = queries.shape[1] // HEAD
    q = queries.reshape(rows, heads, HEAD)
    k = keys.reshape(rows, heads, HEAD)
    v = values.reshape(rows, heads, HEAD)
    scores = jnp.einsum("qhd,khd->hqk", q, k, preferred_element_type=f32) * scale_val
    top_val = jnp.max(scores, axis=-1, keepdims=True)
    expd_val = jnp.exp(scores - top_val)
    totals = jnp.sum(expd_val, axis=-1, keepdims=True)
    probs = (expd_val / totals).astype(bf16)
    out = jnp.einsum("hqk,khd->qhd", probs, v, preferred_element_type=f32)
    return out.astype(bf16).reshape(rows, heads * HEAD), (top_val + jnp.log(totals))


def attend_backward(queries, keys, values, grad, lse, scale_val):
    rows = queries.shape[0]
    heads = queries.shape[1] // HEAD
    q, k, v, g = (a.reshape(rows, heads, HEAD) for a in (queries, keys, values, grad))
    scores = jnp.einsum("qhd,khd->hqk", q, k, preferred_element_type=f32) * scale_val
    probs = jnp.exp(scores - lse)
    grad_probs = jnp.einsum("qhd,khd->hqk", g, v, preferred_element_type=f32)
    inner = jnp.sum(probs * grad_probs, axis=-1, keepdims=True)
    grad_scores = (probs * (grad_probs - inner)).astype(bf16)
    grad_q = jnp.einsum("hqk,khd->qhd", grad_scores, k, preferred_element_type=f32) * scale_val
    grad_k = jnp.einsum("hqk,qhd->khd", grad_scores, q, preferred_element_type=f32) * scale_val
    grad_v = jnp.einsum("hqk,qhd->khd", probs.astype(bf16), g, preferred_element_type=f32)
    flat = heads * HEAD
    return [a.astype(bf16).reshape(rows, flat) for a in (grad_q, grad_k, grad_v)]


def local_wide(
    latents_in,
    conditions,
    w_ada,
    b_ada,
    w_qkv,
    b_qv,
    w_proj,
    b_proj,
    w_fc1,
    b_fc1,
    w_fc2,
    b_fc2,
    out_grad,
):
    width = latents_in.shape[2]
    tokens = latents_in.shape[1]
    seq_count = lax.axis_size("seq")
    owners = lax.axis_size("fsdp")
    me = lax.axis_index("fsdp")
    place = lax.axis_index("seq")
    core = place % 2
    own_rows = w_ada.shape[0]
    quarter = width // seq_count
    units = w_fc2.shape[0] // 2
    scale_val = HEAD ** (-0.5)

    condition = conditions[0]
    cond_act, silu_pull = jax.vjp(jax.nn.silu, condition)
    cond_low = cond_act.astype(bf16)
    small = jnp.concatenate([cond_low, b_qv, b_proj, b_fc1, b_fc2])
    small_rel = gather_small(small, me)
    cond_rows = lax.dynamic_slice_in_dim(small_rel, me * own_rows, own_rows, 1)
    mod_partial = dot(cond_rows, w_ada, ((1,), (0,)))
    bias_at = b_ada.shape[0]
    placed_bias = jnp.where(
        jnp.arange(owners)[:, None] == me, b_ada.astype(f32)[None, :], 0.0
    ).reshape(1, owners * bias_at)
    mod_partial = mod_partial + placed_bias
    modulation = jnp.sum(deal_small(mod_partial, me), axis=0)
    shift_one, scale_one, gate_one, shift_two, scale_two, gate_two = jnp.split(modulation, 6)

    bias_rel = small_rel[:, width:].astype(f32)
    bias_all = rolled(bias_rel[::-1], jnp.mod(me + 1, owners))
    at = 0
    biases = []
    for b in (b_qv, b_proj, b_fc1, b_fc2):
        biases.append(bias_all[:, at : at + b.shape[0]])
        at += b.shape[0]
    qv_full = biases[0].reshape(2, seq_count, quarter)
    bias_q, bias_v = lax.dynamic_index_in_dim(qv_full, place, 1, keepdims=False)
    bias_proj = biases[1].reshape(width)
    bias_fc1 = lax.dynamic_index_in_dim(
        biases[2].reshape(owners, 2, units), core, 1, keepdims=False
    ).reshape(owners * units)
    bias_fc2 = biases[3].reshape(width)

    mine_qkv = lax.dynamic_index_in_dim(
        w_qkv.reshape(own_rows, 3, seq_count, quarter), place, 2, keepdims=False
    ).reshape(own_rows, 3 * quarter)
    use_qkv = ring_gather(mine_qkv, me)
    mine_proj = lax.dynamic_slice_in_dim(w_proj, core * (width // 2), width // 2, 1)
    proj_half = ring_gather(mine_proj, me)
    proj_other = swap_core(proj_half)
    full_proj = jnp.where(
        core == 0,
        jnp.concatenate([proj_half, proj_other], axis=1),
        jnp.concatenate([proj_other, proj_half], axis=1),
    )
    use_proj = jnp.concatenate(
        [
            lax.dynamic_slice_in_dim(full_proj, (place ^ k) * quarter, quarter, 0)
            for k in range(seq_count)
        ]
    )
    mine_fc1 = lax.dynamic_index_in_dim(
        w_fc1.reshape(own_rows, owners, 2, units), core, 2, keepdims=False
    ).reshape(own_rows, owners * units)
    use_fc1 = ring_gather(mine_fc1, me)
    mine_fc2 = lax.dynamic_slice_in_dim(w_fc2, core * units, units, 0)
    use_fc2 = ring_gather(mine_fc2, me)

    own_latent = latents_in[0]
    from_x = swap_x(own_latent)
    from_core = swap_core(own_latent)
    from_both = swap_core(from_x)
    all_latent = jnp.concatenate([own_latent, from_core, from_x, from_both]).astype(f32)
    latent = own_latent.astype(f32)
    grad_own = out_grad[0]
    grad_pair = jnp.concatenate([grad_own, swap_core(grad_own)]).astype(f32)
    grad_out = grad_own.astype(f32)

    normed_all = layer_norm(all_latent)
    act_one = (normed_all * (1.0 + scale_one) + shift_one).astype(bf16)
    bias_three = jnp.concatenate([bias_q, jnp.zeros_like(bias_q), bias_v])
    qkv = (dot(act_one, use_qkv, ((1,), (0,))) + bias_three).astype(bf16)
    queries, keys, values = jnp.split(qkv, 3, axis=1)
    attn_heads, lse = attend_forward(queries, keys, values, scale_val)

    def to_tokens(blocks):
        return [blocks[0]] + [seq_swap(blocks[k], k) for k in range(1, seq_count)]

    attn_own = jnp.concatenate(
        to_tokens([attn_heads[k * tokens : (k + 1) * tokens] for k in range(seq_count)]), axis=1
    )
    branch_one = dot(attn_own, use_proj, ((1,), (0,))) + bias_proj
    middle = latent + gate_one * branch_one
    normed_two, norm_pull_two = jax.vjp(layer_norm, middle)
    act_two_own = (normed_two * (1.0 + scale_two) + shift_two).astype(bf16)

    act_two = jnp.concatenate([act_two_own, swap_core(act_two_own)])
    hidden_pre = dot(act_two, use_fc1, ((1,), (0,))) + bias_fc1
    hidden_act, gelu_pull = jax.vjp(gelu_tanh, hidden_pre)
    hidden_low = hidden_act.astype(bf16)
    grad_two = (gate_two * grad_pair).astype(bf16)
    grad_hidden = dot(grad_two, use_fc2, ((1,), (1,)))
    grad_pre = gelu_pull(grad_hidden)[0].astype(bf16)
    partial_act = dot(grad_pre, use_fc1, ((1,), (1,)))
    grad_act_two = partial_act[:tokens] + swap_core(partial_act[tokens:])
    grad_shift_two = jnp.sum(grad_act_two, axis=0)
    grad_scale_two = jnp.sum(grad_act_two * normed_two, axis=0)
    grad_middle = grad_out + norm_pull_two(grad_act_two * (1.0 + scale_two))[0]
    grad_one = (gate_one * grad_middle).astype(bf16)
    grad_gate_one = jnp.sum(grad_middle * branch_one, axis=0)
    grad_attn = dot(grad_one, use_proj, ((1,), (1,))).astype(bf16)
    grad_heads = jnp.concatenate(
        to_tokens([grad_attn[:, k * quarter : (k + 1) * quarter] for k in range(seq_count)])
    )

    partial_two = dot(hidden_low, use_fc2, ((1,), (0,)))
    branch_two = partial_two[:tokens] + swap_core(partial_two[tokens:]) + bias_fc2
    result = middle + gate_two * branch_two
    grad_gate_two = jnp.sum(grad_out * branch_two, axis=0)
    grad_b_fc2 = jnp.sum(grad_two[:tokens].astype(f32), axis=0)
    grad_b_fc1 = jnp.sum(grad_pre.astype(f32), axis=0)
    grad_b_proj = jnp.sum(grad_one.astype(f32), axis=0)

    red_fc2 = ring_reduce(dot(hidden_low, grad_two, ((0,), (0,))).astype(bf16), me)
    red_fc1 = ring_reduce(dot(act_two, grad_pre, ((0,), (0,))).astype(bf16), me)

    def add_x(block):
        low = block.astype(bf16)
        return low.astype(f32) + swap_x(low).astype(f32)

    def in_core_order(block):
        other = swap_core(block)
        return jnp.where(core == 0, block, other), jnp.where(core == 0, other, block)

    grad_w_fc2 = jnp.concatenate(in_core_order(add_x(red_fc2)))
    first_fc1, second_fc1 = in_core_order(add_x(red_fc1))
    grad_w_fc1 = jnp.concatenate(
        [first_fc1.reshape(own_rows, owners, 1, units), second_fc1.reshape(own_rows, owners, 1, units)],
        axis=2,
    ).reshape(own_rows, 2 * owners * units)

    proj_rel = dot(attn_own, grad_one, ((0,), (0,))).astype(bf16)
    proj_abs = jnp.concatenate(
        [
            lax.dynamic_slice_in_dim(proj_rel, (place ^ k) * quarter, quarter, 0)
            for k in range(seq_count)
        ]
    )
    half_width = width // 2
    keep = lax.dynamic_slice_in_dim(proj_abs, core * half_width, half_width, 1)
    give = lax.dynamic_slice_in_dim(proj_abs, (1 - core) * half_width, half_width, 1)
    proj_sum = (keep.astype(f32) + swap_core(give).astype(f32)).astype(bf16)
    grad_w_proj = jnp.concatenate(in_core_order(add_x(ring_reduce(proj_sum, me))), axis=1)

    grad_q, grad_k, grad_v = attend_backward(queries, keys, values, grad_heads, lse, scale_val)
    grad_qkv = jnp.concatenate([grad_q, grad_k, grad_v], axis=1)
    red_qkv = ring_reduce(dot(act_one, grad_qkv, ((0,), (0,))).astype(bf16), me).astype(bf16)
    across = swap_x(red_qkv)
    blocks = [red_qkv, swap_core(red_qkv), across, swap_core(across)]
    for bit in (1, 2):
        flip = (place & bit) != 0
        blocks = [jnp.where(flip, blocks[j ^ bit], blocks[j]) for j in range(seq_count)]
    grad_w_qkv = jnp.concatenate(
        [b.astype(f32).reshape(own_rows, 3, 1, quarter) for b in blocks], axis=2
    ).reshape(own_rows, 3 * width)

    partial_one = dot(grad_qkv, use_qkv, ((1,), (1,)))
    grad_shift_one = jnp.sum(partial_one, axis=0)
    grad_scale_one = jnp.sum(partial_one * normed_all, axis=0)
    far_low = partial_one[2 * tokens :].astype(bf16)
    far_sum = far_low[:tokens].astype(f32) + swap_core(far_low[tokens:]).astype(f32)
    near_low = partial_one[tokens : 2 * tokens].astype(bf16)
    near_sum = partial_one[:tokens] + swap_core(near_low).astype(f32)
    grad_act_one = near_sum + swap_x(far_sum.astype(bf16)).astype(f32)
    _, norm_pull_one = jax.vjp(layer_norm, latent)
    grad_latent = grad_middle + norm_pull_one(grad_act_one * (1.0 + scale_one))[0]

    grad_b_qv = jnp.where(
        jnp.arange(seq_count)[None, :, None] == place,
        jnp.stack(
            [jnp.sum(grad_q.astype(f32), axis=0), jnp.sum(grad_v.astype(f32), axis=0)]
        )[:, None, :],
        0.0,
    ).reshape(2 * width)
    placed_fc1 = jnp.where(
        jnp.arange(2)[None, :, None] == core, grad_b_fc1.reshape(owners, 1, units), 0.0
    ).reshape(2 * owners * units)
    terms = jnp.concatenate(
        [
            grad_shift_one,
            grad_scale_one,
            grad_gate_one,
            grad_shift_two,
            grad_scale_two,
            grad_gate_two,
            grad_b_qv,
            grad_b_proj,
            placed_fc1,
            grad_b_fc2,
        ]
    )
    sums = (terms + seq_swap(terms, 1)) + (seq_swap(terms, 2) + seq_swap(terms, 3))
    low_sums = sums.astype(bf16)
    grad_mod = low_sums[: 6 * width]
    at = 6 * width
    by_owner = []
    for b in (b_qv, b_proj, b_fc1, b_fc2):
        size = b.shape[0] * owners
        by_owner.append(low_sums[at : at + size].reshape(owners, b.shape[0]))
        at += size
    by_owner = jnp.concatenate(by_owner, axis=1)
    sent_bias = rolled(by_owner[::-1], jnp.mod(me + 1, owners))
    mail = jnp.concatenate(
        [jnp.broadcast_to(grad_mod[None, :], (owners, 6 * width)), sent_bias], axis=1
    )
    got = deal_small(mail, me)
    mod_rel = got[:, : 6 * width]
    bias_sums = jnp.sum(got[:, 6 * width :].astype(f32), axis=0)
    back_cond = jnp.concatenate([cond_rows[:1], cond_rows[1:][::-1]])
    owned_w_ada = dot(back_cond, mod_rel, ((0,), (0,)))
    owned_b_ada = jnp.sum(
        lax.dynamic_slice_in_dim(mod_rel, me * bias_at, bias_at, 1).astype(f32), axis=0
    )
    cond_partial = dot(mod_rel, w_ada, ((1,), (1,)))
    back_partial = jnp.concatenate([cond_partial[:1], cond_partial[1:][::-1]])
    cond_got = rolled(deal_small(back_partial, me), me)
    grad_cond = silu_pull(cond_got.reshape(width))[0]
    at = 0
    owned_bias = []
    for b in (b_qv, b_proj, b_fc1, b_fc2):
        owned_bias.append(bias_sums[at : at + b.shape[0]])
        at += b.shape[0]
    return (
        result.astype(bf16)[None],
        grad_latent[None],
        grad_cond[None],
        owned_w_ada,
        owned_b_ada,
        grad_w_qkv,
        owned_bias[0],
        grad_w_proj,
        owned_bias[1],
        grad_w_fc1,
        owned_bias[2],
        grad_w_fc2,
        owned_bias[3],
    )


def swap_f(values, bit):
    count = lax.axis_size("fsdp")
    return lax.ppermute(values, "fsdp", [(i, i ^ bit) for i in range(count)])


def cube_bits():
    return [1 << b for b in range(lax.axis_size("fsdp").bit_length() - 1)]


def cube_places():
    places = [0]
    for bit in reversed(cube_bits()):
        places = places + [r | bit for r in places]
    return places


def cube_gather(row):
    rows = row
    for bit in reversed(cube_bits()):
        got = swap_f(rows, bit)
        rows = jnp.concatenate([rows, got])
    return rows


def cube_sum(rows):
    for bit in cube_bits():
        half = rows.shape[0] // 2
        got = swap_f(rows[half:], bit)
        rows = rows[:half] + got
    return rows[0]


def cube_deal(rows):
    count = rows.shape[0]
    done = 1
    for bit in cube_bits():
        parts = rows.reshape((done, 2, count // (2 * done)) + rows.shape[1:])
        got = swap_f(parts[:, 1], bit)
        rows = jnp.stack([parts[:, 0], got], axis=1).reshape(rows.shape)
        done *= 2
    return rows


def cube_to_order(rows, me):
    places = jnp.array(cube_places())
    count = rows.shape[0]
    hit = jnp.arange(count)[:, None] == jnp.bitwise_xor(places, me)[None, :]
    return jnp.sum(jnp.where(hit[:, :, None], rows[None], jnp.zeros_like(rows)[None]), axis=1)


SMEM = pl.BlockSpec(memory_space=pltpu.SMEM)
VMEM = pl.BlockSpec(memory_space=pltpu.VMEM)


def bytes_of(*arrays):
    return sum(a.size * a.dtype.itemsize for a in arrays)


def call_whole(body, outs, table, *arrays, scratch=()):
    return pl.pallas_call(
        body,
        out_shape=outs,
        in_specs=[SMEM] + [VMEM] * len(arrays),
        out_specs=jax.tree.map(lambda _: VMEM, outs),
        scratch_shapes=list(scratch),
        compiler_params=pltpu.CompilerParams(
            vmem_limit_bytes=bytes_of(*arrays) + bytes_of(*jax.tree.leaves(outs)) + 2**21
        ),
        cost_estimate=pl.CostEstimate(
            flops=0,
            bytes_accessed=bytes_of(*arrays) + bytes_of(*jax.tree.leaves(outs)),
            transcendentals=0,
        ),
    )(table, *arrays)


def shaped(rows, cols, dtype=bf16):
    return jax.ShapeDtypeStruct((rows, cols), dtype)


def make_table(place, me):
    count = lax.axis_size("fsdp")
    around = [ring_place(me, off) for off in range(count)]
    return jnp.stack([jnp.asarray(v, jnp.int32) for v in [place] + around])


def along(at, offset, count):
    return at[1 + offset % count]


LANES = 128


def bias_lines(sizes):
    lines = []
    for n, size in enumerate(sizes):
        for lo in range(0, size, LANES):
            lines.append((n, lo, min(LANES, size - lo)))
    return lines


def pack_first(table, w_proj, w_qkv, biases, seq_count):
    rows, width = w_proj.shape
    half = width // 2
    quarter = width // seq_count
    total = half + 3 * quarter

    def body(at, proj, qkv, *rest):
        small, out, lines = rest[: len(biases)], rest[len(biases)], rest[-1]
        lines[...] = jnp.zeros_like(lines)
        for line, (n, lo, size) in enumerate(bias_lines([b.shape[1] for b in biases])):
            lines[line : line + 1, :size] = small[n][:, lo : lo + size].astype(f32)
        out[:16, total:] = lines[...].astype(bf16)
        out[16:, total:] = jnp.zeros((rows - 16, LANES), bf16)
        for s in range(seq_count):

            @pl.when(at[0] == s)
            def _(s=s):
                out[:, :half] = proj[:, (s % 2) * half : (s % 2 + 1) * half]
                for t in range(3):
                    to = half + t * quarter
                    start = t * width + s * quarter
                    out[:, to : to + quarter] = qkv[:, start : start + quarter]

    outs = shaped(rows, total + LANES)
    scratch = [pltpu.VMEM((16, LANES), f32)]
    return call_whole(body, outs, table, w_proj, w_qkv, *biases, scratch=scratch)


def put_first(table, pieces, rows, width, quarter, sizes):
    count = lax.axis_size("fsdp")
    half = width // 2
    total = half + 3 * quarter
    offsets = [off for off, _, _ in pieces]
    shifts = [first for _, first, _ in pieces]

    def body(at, *refs):
        ins = refs[: len(pieces)]
        proj, qkv = refs[len(pieces) : len(pieces) + 2]
        kept = refs[-1]
        for ref, off, shift in zip(ins, offsets, shifts):
            size = ref.shape[0]
            owner = along(at, off, count)
            start = pl.multiple_of(owner * rows + shift, 16)
            proj[pl.ds(start, size), :] = ref[:, :half]
            qkv[pl.ds(start, size), :] = ref[:, half:total]
            if shift == 0:
                kept[pl.ds(pl.multiple_of(owner * 16, 16), 16), :] = ref[:16, total:]

    outs = (shaped(width, half), shaped(width, 3 * quarter), shaped(count * 16, LANES))
    proj, qkv, kept = call_whole(body, outs, table, *[p for _, _, p in pieces])
    kept = kept.reshape(count, 16, LANES).astype(f32)
    vectors = []
    for n in range(len(sizes)):
        parts = [kept[:, i, :z] for i, (m, _, z) in enumerate(bias_lines(sizes)) if m == n]
        vectors.append(jnp.concatenate(parts, axis=1))
    return proj, qkv, *vectors


def pack_second(table, w_fc1, w_fc2, owners):
    rows = w_fc1.shape[0]
    width = w_fc2.shape[1]
    units = w_fc2.shape[0] // 2
    span = owners * units
    parts = units // rows

    def body(at, fc1, fc2, out):
        for c in range(2):

            @pl.when(at[0] % 2 == c)
            def _(c=c):
                for f in range(owners):
                    start = (2 * f + c) * units
                    out[:, f * units : (f + 1) * units] = fc1[:, start : start + units]
                for n in range(parts):
                    start = c * units + n * rows
                    to = span + n * width
                    out[:, to : to + width] = fc2[start : start + rows, :]

    outs = shaped(rows, span + parts * width)
    return call_whole(body, outs, table, w_fc1, w_fc2)


def ring_pieces(block, half):
    count = lax.axis_size("fsdp")
    _, ahead, back = ring_tables(count)
    far = count // 2
    pieces = [(0, 0, block)]
    up = down = block
    for step in range(1, far + 1):
        if step == far:
            up, down = up[:half], down[half:]
        up = lax.ppermute(up, "fsdp", ahead)
        down = lax.ppermute(down, "fsdp", back)
        pieces.append((-step, 0, up))
        pieces.append((step, half if step == far else 0, down))
    return pieces


def assemble(pieces, layout, outs, table):
    count = lax.axis_size("fsdp")
    offsets = [off for off, _, _ in pieces]
    shifts = [first for _, first, _ in pieces]

    def body(at, *refs):
        ins, results = refs[: len(pieces)], refs[len(pieces) :]
        for ref, off, shift in zip(ins, offsets, shifts):
            owner = along(at, off, count)

            def some(lo, ref=ref, owner=owner, shift=shift):
                for out, per, base, col, cols in layout:
                    results[out][sixteen(owner * per + base + shift + lo), :] = ref[
                        sixteen(lo), col : col + cols
                    ]

            by_sixteen(ref.shape[0], some)

    return call_whole(body, outs, table, *[p for _, _, p in pieces])


def mix_proj(table, own, other, seq_count):
    width, half = own.shape
    quarter = width // seq_count

    def body(at, mine, theirs, out):
        for s in range(seq_count):

            @pl.when(at[0] == s)
            def _(s=s):
                c = s % 2
                for k in range(seq_count):
                    src = slice((s ^ k) * quarter, ((s ^ k) + 1) * quarter)
                    dst = slice(k * quarter, (k + 1) * quarter)
                    out[dst, c * half : (c + 1) * half] = mine[src, :]
                    out[dst, (1 - c) * half : (2 - c) * half] = theirs[src, :]

    return call_whole(body, shaped(width, width), table, own, other)


def split_proj(table, values, seq_count):
    width = values.shape[1]
    half = width // 2
    quarter = width // seq_count

    def body(at, ref, keep, give):
        for s in range(seq_count):

            @pl.when(at[0] == s)
            def _(s=s):
                c = s % 2
                for k in range(seq_count):
                    dst = slice((s ^ k) * quarter, ((s ^ k) + 1) * quarter)
                    src = slice(k * quarter, (k + 1) * quarter)
                    keep[dst, :] = ref[src, c * half : (c + 1) * half]
                    give[dst, :] = ref[src, (1 - c) * half : (2 - c) * half]

    return call_whole(body, (shaped(width, half), shaped(width, half)), table, values)


def ring_sum(arrays, layout, table, rows):
    count = lax.axis_size("fsdp")
    _, ahead, back = ring_tables(count)
    half = rows // 2
    far = count // 2
    total = sum(cols for _, _, cols in layout)

    def step_call(step, *got):
        def body(at, *refs):
            blocks, rest = refs[: len(arrays)], refs[len(arrays) :]
            up_at, down_at = along(at, far - step, count), along(at, step - far, count)

            def sixteen(line, carry):
                low = pl.ds(pl.multiple_of(line * 16, 16), 16)
                high = pl.ds(pl.multiple_of(half + line * 16, 16), 16)
                col = 0
                for a, base, cols in layout:
                    to = slice(col, col + cols)
                    col += cols
                    per = blocks[a].shape[0] // count

                    def own(owner, lo):
                        start = pl.multiple_of(owner * per + base + lo + line * 16, 16)
                        return blocks[a][pl.ds(start, 16), :]

                    def plus(owner, lo, *others):
                        total_val = own(owner, lo).astype(f32)
                        for ref, at_rows in others:
                            total_val = total_val + ref[at_rows, to].astype(f32)
                        return total_val.astype(bf16)

                    if step == 0:
                        rest[0][low, to] = own(up_at, 0)
                        rest[1][low, to] = own(down_at, half)
                    elif step == far:
                        up, down, out = rest
                        out[low, to] = plus(up_at, 0, (up, low), (down, low))
                        out[high, to] = plus(up_at, half, (up, high), (down, high))
                    else:
                        up, down, next_up, next_down = rest
                        next_up[low, to] = plus(up_at, 0, (up, low))
                        next_down[high, to] = plus(
                            down_at, half, (down, low if step == 1 else high)
                        )
                        if step == 1:
                            next_up[high, to] = own(up_at, half)
                            next_down[low, to] = own(down_at, 0)
                        else:
                            next_up[high, to] = plus(up_at, half, (up, high))
                            next_down[low, to] = plus(down_at, 0, (down, low))
                return carry

            lax.fori_loop(0, half // 16, sixteen, 0)

        out = shaped(half if step == 0 else rows, total)
        outs = out if step == far else (out, out)
        return call_whole(body, outs, table, *arrays, *got)

    up, down = step_call(0)
    for step in range(1, far + 1):
        up = lax.ppermute(up, "fsdp", ahead)
        down = lax.ppermute(down, "fsdp", back)
        if step < far:
            up, down = step_call(step, up, down)
    return step_call(far, up, down)


def by_sixteen(size, step):
    def one(line, carry):
        step(line * 16)
        return carry

    lax.fori_loop(0, size // 16, one, 0)


def sixteen(start):
    return pl.ds(pl.multiple_of(start, 16), 16)


def cube_reduce(values, table, rows):
    bits = cube_bits()
    cols = values.shape[1]

    def call(step, *ins):
        left = len(bits) - step
        n_outs = 2 if 0 < step < len(bits) else 1

        def body(at, *refs):
            held, got = refs[0], refs[1]
            outs = refs[len(refs) - n_outs :]
            me = at[1]

            def emit(out, row, n):
                index = 2 * n + lax.rem(me, 2) if step == 1 else n

                def some(lo):
                    mine = held[sixteen(index * rows + lo), :]
                    if step > 0:
                        theirs = got[sixteen(n * rows + lo), :]
                        mine = (mine.astype(f32) + theirs.astype(f32)).astype(bf16)
                    out[sixteen(row + lo), :] = mine

                by_sixteen(rows, some)

            if left == 0:
                emit(outs[0], 0, 0)
                return
            bit = lax.rem(me >> step, 2)
            for n in range((1 << left) // 2):
                emit(outs[0], n * rows, 2 * n + (1 - bit))
                if step > 0:
                    emit(outs[1], n * rows, 2 * n + bit)

        out = shaped(rows * max(1, (1 << left) // 2), cols)
        outs = (out, out) if n_outs == 2 else out
        return call_whole(body, outs, table, *ins)

    held, got = values, None
    for step, bit in enumerate(bits):
        if step == 0:
            send = call(step, held)
        else:
            send, held = call(step, held, got)
        got = swap_f(send, bit)
    return call(len(bits), held, got)


def place_second(table, own, other, owners, rows, units, width):
    span = owners * units
    parts = units // rows

    def body(at, mine, theirs, fc1, fc2):
        for c in range(2):

            @pl.when(at[0] % 2 == c)
            def _(c=c):
                for ref, cc in ((mine, c), (theirs, 1 - c)):
                    for f in range(owners):
                        start = (2 * f + cc) * units
                        fc1[:, start : start + units] = ref[
                            :, f * units : (f + 1) * units
                        ].astype(f32)
                    for n in range(parts):
                        start = cc * units + n * rows
                        to = span + n * width
                        fc2[start : start + rows, :] = ref[:, to : to + width].astype(f32)

    outs = (shaped(rows, 2 * span, f32), shaped(2 * units, width, f32))
    return call_whole(body, outs, table, own, other)


def place_first(table, own, across, sums, near, seq_count, width):
    rows = own.shape[0]
    half = width // 2
    quarter = width // seq_count
    span = 3 * quarter

    def body(at, own, across, sums, near, proj, qkv):
        for s in range(seq_count):

            @pl.when(at[0] == s)
            def _(s=s):
                c = s % 2
                proj[:, c * half : (c + 1) * half] = sums[...].astype(f32)
                proj[:, (1 - c) * half : (2 - c) * half] = near[:, :half].astype(f32)
                parts = ((own, half), (near, half), (across, half), (near, half + span))
                for k, (ref, base) in enumerate(parts):
                    for t in range(3):
                        start = t * width + (s ^ k) * quarter
                        at_col = base + t * quarter
                        qkv[:, start : start + quarter] = ref[
                            :, at_col : at_col + quarter
                        ].astype(f32)

    outs = (shaped(rows, width, f32), shaped(rows, 3 * width, f32))
    return call_whole(body, outs, table, own, across, sums, near)


def heads_forward(qkv, scale_val):
    length = qkv.shape[0]
    flat = qkv.shape[1] // 3
    heads = flat // HEAD
    block = min(512, length)

    def body(whole, out, lse, q_at, k_at, v_at, o_at):
        i = pl.program_id(0)

        @pl.when(i == 0)
        def _():
            for h in range(heads):
                lo = h * HEAD
                q_at[h] = (whole[:, lo : lo + HEAD].astype(f32) * scale_val).astype(bf16)
                k_at[h] = whole[:, flat + lo : flat + lo + HEAD]
                v_at[h] = whole[:, 2 * flat + lo : 2 * flat + lo + HEAD].T

        rows = pl.ds(pl.multiple_of(i * block, block), block)

        def one_head(h, carry):
            scores = dot(k_at[h], q_at[h, rows], ((1,), (1,)))
            top_val = jnp.max(scores, axis=0, keepdims=True)
            expd = jnp.exp(scores - top_val)
            totals = jnp.sum(expd, axis=0, keepdims=True)
            o_at[h] = dot(v_at[h], expd.astype(bf16), ((1,), (0,))) * (1.0 / totals)
            lse[h] = top_val + jnp.log(totals)
            return carry

        lax.fori_loop(0, heads, one_head, 0)
        for h in range(heads):
            out[:, h * HEAD : (h + 1) * HEAD] = o_at[h].T.astype(bf16)

    return pl.pallas_call(
        body,
        grid=(length // block,),
        in_specs=[pl.BlockSpec((length, 3 * flat), lambda i: (0, 0))],
        out_specs=[
            pl.BlockSpec((block, flat), lambda i: (i, 0)),
            pl.BlockSpec((heads, 1, block), lambda i: (0, 0, i)),
        ],
        out_shape=[shaped(length, flat), jax.ShapeDtypeStruct((heads, 1, length), f32)],
        scratch_shapes=[
            pltpu.VMEM((heads, length, HEAD), bf16),
            pltpu.VMEM((heads, length, HEAD), bf16),
            pltpu.VMEM((heads, HEAD, length), bf16),
            pltpu.VMEM((heads, HEAD, block), f32),
        ],
        compiler_params=pltpu.CompilerParams(vmem_limit_bytes=16 * 2**20),
        cost_estimate=pl.CostEstimate(
            flops=4 * length * length * flat,
            bytes_accessed=8 * length * flat,
            transcendentals=heads * length * length,
        ),
    )(qkv)


def heads_backward(qkv, grad, lse, scale_val, first, last, done=None):
    length = qkv.shape[0]
    flat = qkv.shape[1] // 3
    heads = last - first
    before = 0 if done is None else first * HEAD
    mine = heads * HEAD
    span = before + mine
    block = min(512, length)
    steps = length // block

    def body(whole, grads, lse_here, *refs):
        if done is not None:
            earlier, refs = refs[0], refs[1:]
        out, q_at, k_at, kt_at, v_at, g_at, dq_at, sum_k, sum_v = refs
        i = pl.program_id(0)

        @pl.when(i == 0)
        def _():
            for h in range(heads):
                lo = (first + h) * HEAD
                q_at[h] = (whole[:, lo : lo + HEAD].astype(f32) * scale_val).astype(bf16)
                key = whole[:, flat + lo : flat + lo + HEAD]
                k_at[h] = key
                kt_at[h] = key.T
                v_at[h] = whole[:, 2 * flat + lo : 2 * flat + lo + HEAD]
                g_at[h] = grads[:, lo : lo + HEAD]
            sum_k[...] = jnp.zeros_like(sum_k)
            sum_v[...] = jnp.zeros_like(sum_v)
            if done is not None:
                for t in range(3):
                    out[:, t * span : t * span + before] = earlier[:, t * before : (t + 1) * before]

        rows = pl.ds(pl.multiple_of(i * block, block), block)

        def one_head(h, carry):
            q = q_at[h, rows]
            g = g_at[h, rows]
            probs = jnp.exp(dot(k_at[h], q, ((1,), (1,))) - lse_here[first + h])
            grad_probs = dot(v_at[h], g, ((1,), (1,)))
            inner = jnp.sum(probs * grad_probs, axis=0, keepdims=True)
            grad_scores = (probs * (grad_probs - inner)).astype(bf16)
            dq_at[h] = dot(kt_at[h], grad_scores, ((1,), (0,))) * scale_val
            sum_k[h] += dot(grad_scores, q, ((1,), (0,)))
            sum_v[h] += dot(probs.astype(bf16), g, ((1,), (0,)))
            return carry

        lax.fori_loop(0, heads, one_head, 0)
        for h in range(heads):
            lo = before + h * HEAD
            out[rows, lo : lo + HEAD] = dq_at[h].T.astype(bf16)

        @pl.when(i == steps - 1)
        def _():
            for h in range(heads):
                lo = span + before + h * HEAD
                out[:, lo : lo + HEAD] = sum_k[h].astype(bf16)
                out[:, span + lo : span + lo + HEAD] = sum_v[h].astype(bf16)

    def whole_block(shape):
        return pl.BlockSpec(shape, lambda i: (0, 0))

    ins = [qkv, grad, lse] + ([] if done is None else [done])
    more = [] if done is None else [whole_block(done.shape)]
    return pl.pallas_call(
        body,
        grid=(steps,),
        in_specs=[
            whole_block((length, 3 * flat)),
            whole_block((length, flat)),
            pl.BlockSpec((lse.shape[0], 1, block), lambda i: (0, 0, i)),
        ]
        + more,
        out_specs=whole_block((length, 3 * span)),
        out_shape=shaped(length, 3 * span),
        scratch_shapes=[
            pltpu.VMEM((heads, length, HEAD), bf16),
            pltpu.VMEM((heads, length, HEAD), bf16),
            pltpu.VMEM((heads, HEAD, length), bf16),
            pltpu.VMEM((heads, length, HEAD), bf16),
            pltpu.VMEM((heads, length, HEAD), bf16),
            pltpu.VMEM((heads, HEAD, block), f32),
            pltpu.VMEM((heads, length, HEAD), f32),
            pltpu.VMEM((heads, length, HEAD), f32),
        ],
        compiler_params=pltpu.CompilerParams(vmem_limit_bytes=24 * 2**20),
        cost_estimate=pl.CostEstimate(
            flops=10 * length * length * mine,
            bytes_accessed=16 * length * mine,
            transcendentals=heads * length * length,
        ),
    )(*ins)


def local_ring(
    latents_in,
    conditions,
    w_ada,
    b_ada,
    w_qkv,
    b_qv,
    w_proj,
    b_proj,
    w_fc1,
    b_fc1,
    w_fc2,
    b_fc2,
    out_grad,
):
    width = latents_in.shape[2]
    tokens = latents_in.shape[1]
    seq_count = lax.axis_size("seq")
    owners = lax.axis_size("fsdp")
    me = lax.axis_index("fsdp")
    place = lax.axis_index("seq")
    core = place % 2
    own_rows = w_ada.shape[0]
    quarter = width // seq_count
    half_width = width // 2
    units = w_fc2.shape[0] // 2
    span = owners * units
    parts = units // own_rows
    scale_val = HEAD ** (-0.5)
    table = make_table(place, me)

    small = [b.astype(f32)[None] for b in (b_qv, b_proj, b_fc1, b_fc2)]
    first = ring_pieces(pack_first(table, w_proj, w_qkv, small, seq_count), own_rows // 2)
    second = ring_pieces(pack_second(table, w_fc1, w_fc2, owners), own_rows // 2)

    condition = conditions[0]
    cond_act, silu_pull = jax.vjp(jax.nn.silu, condition)
    cond_low = cond_act.astype(bf16)
    cond_rel = cube_gather(cond_low.astype(f32)[None])
    cond_rows = lax.dynamic_slice_in_dim(cond_rel, me * own_rows, own_rows, 1).astype(bf16)
    mod_partial = dot(cond_rows, w_ada, ((1,), (0,)))
    bias_at = b_ada.shape[0]
    owned = jnp.arange(owners)[:, None] == me
    placed_bias = jnp.where(owned, b_ada.astype(f32)[None, :], 0.0)
    mod_partial = mod_partial + placed_bias.reshape(1, owners * bias_at)
    modulation = cube_sum(mod_partial)
    shift_one, scale_one, gate_one, shift_two, scale_two, gate_two = jnp.split(modulation, 6)

    proj_half, use_qkv, *biases = put_first(
        table, first, own_rows, width, quarter, [v.shape[1] for v in small]
    )
    use_proj = mix_proj(table, proj_half, seq_swap(proj_half, 1), seq_count)
    qv_full = biases[0].reshape(2, seq_count, quarter)
    bias_q, bias_v = lax.dynamic_index_in_dim(qv_full, place, 1, keepdims=False)
    bias_proj = biases[1].reshape(width)
    bias_fc1 = lax.dynamic_index_in_dim(
        biases[2].reshape(owners, 2, units), core, 1, keepdims=False
    ).reshape(span)
    bias_fc2 = biases[3].reshape(width)

    own_latent = latents_in[0]
    from_x = seq_swap(own_latent, 2)
    from_core = seq_swap(own_latent, 1)
    from_both = seq_swap(from_x, 1)
    all_latent = jnp.concatenate([own_latent, from_core, from_x, from_both]).astype(f32)
    latent = own_latent.astype(f32)
    grad_own = out_grad[0]
    grad_pair = jnp.concatenate([grad_own, seq_swap(grad_own, 1)]).astype(f32)
    grad_out = grad_own.astype(f32)

    normed_all = layer_norm(all_latent)
    act_one = (normed_all * (1.0 + scale_one) + shift_one).astype(bf16)
    bias_three = jnp.concatenate([bias_q, jnp.zeros_like(bias_q), bias_v])
    qkv = (dot(act_one, use_qkv, ((1,), (0,))) + bias_three).astype(bf16)
    attn_heads, lse = heads_forward(qkv, scale_val)

    def to_tokens(blocks):
        return [blocks[0]] + [seq_swap(blocks[k], k) for k in range(1, seq_count)]

    attn_own = jnp.concatenate(
        to_tokens([attn_heads[k * tokens : (k + 1) * tokens] for k in range(seq_count)]),
        axis=1,
    )
    branch_one = dot(attn_own, use_proj, ((1,), (0,))) + bias_proj
    middle = latent + gate_one * branch_one
    normed_two, norm_pull_two = jax.vjp(layer_norm, middle)
    act_two_own = (normed_two * (1.0 + scale_two) + shift_two).astype(bf16)

    act_two = jnp.concatenate([act_two_own, seq_swap(act_two_own, 1)])
    use_fc1, use_fc2 = assemble(
        second,
        [(0, own_rows, 0, 0, span)]
        + [(1, units, n * own_rows, span + n * width, width) for n in range(parts)],
        (shaped(width, span), shaped(span, width)),
        table,
    )
    hidden_pre = dot(act_two, use_fc1, ((1,), (0,))) + bias_fc1
    hidden_act, gelu_pull = jax.vjp(gelu_tanh, hidden_pre)
    hidden_low = hidden_act.astype(bf16)
    grad_two = (gate_two * grad_pair).astype(bf16)
    grad_hidden = dot(grad_two, use_fc2, ((1,), (1,)))
    grad_pre = gelu_pull(grad_hidden)[0].astype(bf16)
    far_act = dot(grad_pre[tokens:], use_fc1, ((1,), (1,)))
    near_act = dot(grad_pre[:tokens], use_fc1, ((1,), (1,)))
    grad_act_two = near_act + seq_swap(far_act, 1)

    grad_fc1 = dot(act_two, grad_pre, ((0,), (0,))).astype(bf16)
    grad_fc2 = dot(hidden_low, grad_two, ((0,), (0,))).astype(bf16)
    second_red = ring_sum(
        [grad_fc1, grad_fc2],
        [(0, 0, span)] + [(1, n * own_rows, width) for n in range(parts)],
        table,
        own_rows,
    )

    grad_shift_two = jnp.sum(grad_act_two, axis=0)
    grad_scale_two = jnp.sum(grad_act_two * normed_two, axis=0)
    grad_middle = grad_out + norm_pull_two(grad_act_two * (1.0 + scale_two))[0]
    grad_one = (gate_one * grad_middle).astype(bf16)
    grad_gate_one = jnp.sum(grad_middle * branch_one, axis=0)
    grad_attn = dot(grad_one, use_proj, ((1,), (1,))).astype(bf16)
    grad_heads = jnp.concatenate(
        to_tokens([grad_attn[:, k * quarter : (k + 1) * quarter] for k in range(seq_count)])
    )

    far_two = dot(hidden_low[tokens:], use_fc2, ((1,), (0,)))
    near_two = dot(hidden_low[:tokens], use_fc2, ((1,), (0,)))
    branch_two = near_two + seq_swap(far_two, 1) + bias_fc2
    result = middle + gate_two * branch_two
    grad_gate_two = jnp.sum(grad_out * branch_two, axis=0)
    grad_b_fc2 = jnp.sum(grad_two[:tokens].astype(f32), axis=0)
    grad_b_fc1 = jnp.sum(grad_pre.astype(f32), axis=0)
    grad_b_proj = jnp.sum(grad_one.astype(f32), axis=0)

    proj_rel = dot(attn_own, grad_one, ((0,), (0,))).astype(bf16)
    keep, give = split_proj(table, proj_rel, seq_count)
    proj_sum = (keep.astype(f32) + seq_swap(give, 1).astype(f32)).astype(bf16)

    most = max(1, quarter // HEAD - 1)
    grad_most = heads_backward(qkv, grad_heads, lse, scale_val, 0, most)
    grad_qkv = heads_backward(
        qkv, grad_heads, lse, scale_val, most, quarter // HEAD, done=grad_most
    )
    grad_own_qkv = dot(act_one, grad_qkv, ((0,), (0,))).astype(bf16)
    first_red = cube_reduce(jnp.concatenate([proj_sum, grad_own_qkv], axis=1), table, own_rows)
    first_x = seq_swap(first_red, 2)
    own_half = (
        first_red[:, :half_width].astype(f32) + first_x[:, :half_width].astype(f32)
    ).astype(bf16)
    mail = jnp.concatenate([own_half, first_red[:, half_width:], first_x[:, half_width:]], axis=1)
    grad_w_proj, grad_w_qkv = place_first(
        table, first_red, first_x, own_half, seq_swap(mail, 1), seq_count, width
    )
    second_sum = (second_red.astype(f32) + seq_swap(second_red, 2).astype(f32)).astype(bf16)
    grad_w_fc1, grad_w_fc2 = place_second(
        table, second_sum, seq_swap(second_sum, 1), owners, own_rows, units, width
    )

    partial_one = dot(grad_qkv, use_qkv, ((1,), (1,)))
    grad_shift_one = jnp.sum(partial_one, axis=0)
    grad_scale_one = jnp.sum(partial_one * normed_all, axis=0)
    far_low = partial_one[2 * tokens :].astype(bf16)
    far_sum = far_low[:tokens].astype(f32) + seq_swap(far_low[tokens:], 1).astype(f32)
    near_low = partial_one[tokens : 2 * tokens].astype(bf16)
    near_sum = partial_one[:tokens] + seq_swap(near_low, 1).astype(f32)
    from_ox = seq_swap(far_sum.astype(bf16), 2)

    qkv_sums = jnp.sum(grad_qkv.astype(f32), axis=0).reshape(3, 1, quarter)
    grad_b_qv = jnp.where(
        jnp.arange(seq_count)[None, :, None] == place,
        jnp.concatenate([qkv_sums[:1], qkv_sums[2:]]),
        0.0,
    ).reshape(2 * width)
    placed_fc1 = jnp.where(
        jnp.arange(2)[None, :, None] == core, grad_b_fc1.reshape(owners, 1, units), 0.0
    ).reshape(2 * span)
    terms = jnp.concatenate(
        [
            grad_shift_one,
            grad_scale_one,
            grad_gate_one,
            grad_shift_two,
            grad_scale_two,
            grad_gate_two,
            grad_b_qv,
            grad_b_proj,
            placed_fc1,
            grad_b_fc2,
        ]
    )
    pair_sum = terms + seq_swap(terms, 1)
    sums = pair_sum + seq_swap(pair_sum, 2)
    low_sums = sums.astype(bf16)
    late_middle, late_latent, _ = lax.optimization_barrier((grad_middle, latent, low_sums))
    grad_act_one = near_sum + from_ox.astype(f32)
    _, norm_pull_one = jax.vjp(layer_norm, late_latent)
    grad_latent = late_middle + norm_pull_one(grad_act_one * (1.0 + scale_one))[0]
    got = cube_gather(low_sums[None])
    mod_rel = got[:, : 6 * width]
    all_sums = jnp.sum(got[:, 6 * width :].astype(f32), axis=0)
    owned_w_ada = dot(cond_rows, mod_rel, ((0,), (0,)))
    owned_b_ada = jnp.sum(
        lax.dynamic_slice_in_dim(mod_rel, me * bias_at, bias_at, 1).astype(f32), axis=0
    )
    cond_partial = dot(mod_rel, w_ada, ((1,), (1,)))
    cond_got = cube_to_order(cube_deal(cond_partial), me)
    grad_cond = silu_pull(cond_got.reshape(width))[0]
    at = 0
    owned_bias = []
    for b in (b_qv, b_proj, b_fc1, b_fc2):
        size = b.shape[0]
        owned_bias.append(lax.dynamic_slice_in_dim(all_sums, at + me * size, size, 0))
        at += size * owners
    return (
        result.astype(bf16)[None],
        grad_latent[None],
        grad_cond[None],
        owned_w_ada,
        owned_b_ada,
        grad_w_qkv,
        owned_bias[0],
        grad_w_proj,
        owned_bias[1],
        grad_w_fc1,
        owned_bias[2],
        grad_w_fc2,
        owned_bias[3],
    )


def short_axes(mesh):
    count = mesh.shape["fsdp"]
    return 2 < count <= RING_MAX and count & (count - 1) == 0 and mesh.shape["seq"] == 4


def local(*args):
    return local_ring(*args)


def solution(mesh):
    short = short_axes(mesh)
    return jax.shard_map(
        local if short else local_wide,
        mesh=mesh,
        in_specs=(
            P("fsdp", "seq", None),
            P("fsdp", None),
            P("fsdp", None),
            P("fsdp"),
            P("fsdp", None),
            P("fsdp"),
            P("fsdp", None),
            P("fsdp"),
            P("fsdp", None),
            P("fsdp"),
            P("fsdp", None),
            P("fsdp"),
            P("fsdp", "seq", None),
        ),
        out_specs=(
            P("fsdp", "seq", None),
            P("fsdp", "seq", None),
            P("fsdp", None),
            P("fsdp", None),
            P("fsdp"),
            P("fsdp", None),
            P("fsdp"),
            P("fsdp", None),
            P("fsdp"),
            P("fsdp", None),
            P("fsdp"),
            P("fsdp", None),
            P("fsdp"),
        ),
        check_vma=False,
    )
```

```python
import functools

import jax
import jax.numpy as jnp
from jax import lax
from jax.experimental import pallas as pl
from jax.experimental.pallas import tpu as pltpu
from jax.sharding import PartitionSpec as P


HEAD = 64
RING_MAX = 16

norm_eps = 1e-06
f32 = jnp.float32
bf16 = jnp.bfloat16


def dot(a, b, dims):
    return lax.dot_general(a, b, (dims, ((), ())), preferred_element_type=f32)


def layer_norm(values):
    mean_val = jnp.mean(values, axis=-1, keepdims=True)
    centred = values - mean_val
    var_val = jnp.mean(centred * centred, axis=-1, keepdims=True)
    return centred * lax.rsqrt(var_val + norm_eps)


def gelu_tanh(values):
    return jax.nn.gelu(values, approximate=True)


def seq_swap(values, bit):
    count = lax.axis_size("seq")
    return lax.ppermute(values, "seq", [(i, i ^ bit) for i in range(count)])


swap_core = functools.partial(seq_swap, bit=1)
swap_x = functools.partial(seq_swap, bit=2)


def rolled(rows, shift):
    count = rows.shape[0]
    return lax.dynamic_slice_in_dim(jnp.concatenate([rows, rows]), count - shift, count, 0)


def gather_small(row, me):
    count = lax.axis_size("fsdp")
    if count > RING_MAX:
        rows = lax.all_gather(row, "fsdp", axis=0)
        return rolled(rows[::-1], jnp.mod(me + 1, count))
    got = [row]
    for r in range(1, count):
        got.append(lax.ppermute(row, "fsdp", [(i, (i + r) % count) for i in range(count)]))
    return jnp.stack(got)


def deal_small(rows, me):
    count = lax.axis_size("fsdp")
    if count > RING_MAX:
        placed = rolled(rows[::-1], jnp.mod(me + 1, count))
        got = lax.all_to_all(placed, "fsdp", split_axis=0, concat_axis=0, tiled=True)
        return rolled(got, jnp.mod(count - me, count))
    got = [rows[0]]
    for r in range(1, count):
        got.append(lax.ppermute(rows[r], "fsdp", [(i, (i - r) % count) for i in range(count)]))
    return jnp.stack(got)


def ring_tables(count):
    order = list(range(0, count, 2)) + list(range(count - 1, 0, -2))
    ahead = [(order[i], order[(i + 1) % count]) for i in range(count)]
    return order, ahead, [(b, a) for a, b in ahead]


def ring_place(me, offset):
    count = lax.axis_size("fsdp")
    mine = jnp.where(me % 2 == 0, me // 2, count - 1 - me // 2)
    place = jnp.mod(mine + offset + count, count)
    return jnp.where(place < count // 2, 2 * place, 2 * (count - 1 - place) + 1)


def ring_gather(block, me):
    count = lax.axis_size("fsdp")
    if count > RING_MAX:
        return lax.all_gather(block, "fsdp", axis=0, tiled=True)
    _, ahead, back = ring_tables(count)
    rows = block.shape[0]
    half = rows // 2
    far = count // 2
    out = jnp.zeros((rows * count,) + block.shape[1:], block.dtype)

    def put(out, piece, offset, shift):
        start = ring_place(me, offset) * rows + shift
        return lax.dynamic_update_slice_in_dim(out, piece, start, 0)

    out = put(out, block, 0, 0)
    up = down = block
    for step in range(1, far + 1):
        if step == far:
            up, down = up[:half], down[half:]
        up = lax.ppermute(up, "fsdp", ahead)
        down = lax.ppermute(down, "fsdp", back)
        out = put(out, up, -step, 0)
        out = put(out, down, step, half if step == far else 0)
    return out


def ring_reduce(values, me):
    count = lax.axis_size("fsdp")
    rows = values.shape[0] // count
    if count > RING_MAX:
        return lax.psum_scatter(
            values.astype(bf16), "fsdp", scatter_dimension=0, tiled=True
        ).astype(f32)
    _, ahead, back = ring_tables(count)
    half = rows // 2
    far = count // 2

    def take(offset, start, size):
        return lax.dynamic_slice_in_dim(
            values, ring_place(me, offset) * rows + start, size, 0
        ).astype(f32)

    up = take(far, 0, half)
    down = take(-far, half, half)
    for step in range(1, far + 1):
        up = lax.ppermute(up.astype(bf16), "fsdp", ahead).astype(f32)
        down = lax.ppermute(down.astype(bf16), "fsdp", back).astype(f32)
        if step == far:
            break
        if step == 1:
            up = jnp.concatenate(
                [take(far - 1, 0, half) + up, take(far - 1, half, rows - half)]
            )
            down = jnp.concatenate(
                [take(1 - far, 0, half), take(1 - far, half, rows - half) + down]
            )
        else:
            up = up + take(far - step, 0, rows)
            down = down + take(step - far, 0, rows)
    return take(0, 0, rows) + up + down


def attend_forward(queries, keys, values, scale_val):
    rows = queries.shape[0]
    heads = queries.shape[1] // HEAD
    q = queries.reshape(rows, heads, HEAD)
    k = keys.reshape(rows, heads, HEAD)
    v = values.reshape(rows, heads, HEAD)
    scores = jnp.einsum("qhd,khd->hqk", q, k, preferred_element_type=f32) * scale_val
    top_val = jnp.max(scores, axis=-1, keepdims=True)
    expd_val = jnp.exp(scores - top_val)
    totals = jnp.sum(expd_val, axis=-1, keepdims=True)
    probs = (expd_val / totals).astype(bf16)
    out = jnp.einsum("hqk,khd->qhd", probs, v, preferred_element_type=f32)
    return out.astype(bf16).reshape(rows, heads * HEAD), (top_val + jnp.log(totals))


def attend_backward(queries, keys, values, grad, lse, scale_val):
    rows = queries.shape[0]
    heads = queries.shape[1] // HEAD
    q, k, v, g = (a.reshape(rows, heads, HEAD) for a in (queries, keys, values, grad))
    scores = jnp.einsum("qhd,khd->hqk", q, k, preferred_element_type=f32) * scale_val
    probs = jnp.exp(scores - lse)
    grad_probs = jnp.einsum("qhd,khd->hqk", g, v, preferred_element_type=f32)
    inner = jnp.sum(probs * grad_probs, axis=-1, keepdims=True)
    grad_scores = (probs * (grad_probs - inner)).astype(bf16)
    grad_q = jnp.einsum("hqk,khd->qhd", grad_scores, k, preferred_element_type=f32) * scale_val
    grad_k = jnp.einsum("hqk,qhd->khd", grad_scores, q, preferred_element_type=f32) * scale_val
    grad_v = jnp.einsum("hqk,qhd->khd", probs.astype(bf16), g, preferred_element_type=f32)
    flat = heads * HEAD
    return [a.astype(bf16).reshape(rows, flat) for a in (grad_q, grad_k, grad_v)]


def local_wide(
    latents_in,
    conditions,
    w_ada,
    b_ada,
    w_qkv,
    b_qv,
    w_proj,
    b_proj,
    w_fc1,
    b_fc1,
    w_fc2,
    b_fc2,
    out_grad,
):
    width = latents_in.shape[2]
    tokens = latents_in.shape[1]
    seq_count = lax.axis_size("seq")
    owners = lax.axis_size("fsdp")
    me = lax.axis_index("fsdp")
    place = lax.axis_index("seq")
    core = place % 2
    own_rows = w_ada.shape[0]
    quarter = width // seq_count
    units = w_fc2.shape[0] // 2
    scale_val = HEAD ** (-0.5)

    condition = conditions[0]
    cond_act, silu_pull = jax.vjp(jax.nn.silu, condition)
    cond_low = cond_act.astype(bf16)
    small = jnp.concatenate([cond_low, b_qv, b_proj, b_fc1, b_fc2])
    small_rel = gather_small(small, me)
    cond_rows = lax.dynamic_slice_in_dim(small_rel, me * own_rows, own_rows, 1)
    mod_partial = dot(cond_rows, w_ada, ((1,), (0,)))
    bias_at = b_ada.shape[0]
    placed_bias = jnp.where(
        jnp.arange(owners)[:, None] == me, b_ada.astype(f32)[None, :], 0.0
    ).reshape(1, owners * bias_at)
    mod_partial = mod_partial + placed_bias
    modulation = jnp.sum(deal_small(mod_partial, me), axis=0)
    shift_one, scale_one, gate_one, shift_two, scale_two, gate_two = jnp.split(modulation, 6)

    bias_rel = small_rel[:, width:].astype(f32)
    bias_all = rolled(bias_rel[::-1], jnp.mod(me + 1, owners))
    at = 0
    biases = []
    for b in (b_qv, b_proj, b_fc1, b_fc2):
        biases.append(bias_all[:, at : at + b.shape[0]])
        at += b.shape[0]
    qv_full = biases[0].reshape(2, seq_count, quarter)
    bias_q, bias_v = lax.dynamic_index_in_dim(qv_full, place, 1, keepdims=False)
    bias_proj = biases[1].reshape(width)
    bias_fc1 = lax.dynamic_index_in_dim(
        biases[2].reshape(owners, 2, units), core, 1, keepdims=False
    ).reshape(owners * units)
    bias_fc2 = biases[3].reshape(width)

    mine_qkv = lax.dynamic_index_in_dim(
        w_qkv.reshape(own_rows, 3, seq_count, quarter), place, 2, keepdims=False
    ).reshape(own_rows, 3 * quarter)
    use_qkv = ring_gather(mine_qkv, me)
    mine_proj = lax.dynamic_slice_in_dim(w_proj, core * (width // 2), width // 2, 1)
    proj_half = ring_gather(mine_proj, me)
    proj_other = swap_core(proj_half)
    full_proj = jnp.where(
        core == 0,
        jnp.concatenate([proj_half, proj_other], axis=1),
        jnp.concatenate([proj_other, proj_half], axis=1),
    )
    use_proj = jnp.concatenate(
        [
            lax.dynamic_slice_in_dim(full_proj, (place ^ k) * quarter, quarter, 0)
            for k in range(seq_count)
        ]
    )
    mine_fc1 = lax.dynamic_index_in_dim(
        w_fc1.reshape(own_rows, owners, 2, units), core, 2, keepdims=False
    ).reshape(own_rows, owners * units)
    use_fc1 = ring_gather(mine_fc1, me)
    mine_fc2 = lax.dynamic_slice_in_dim(w_fc2, core * units, units, 0)
    use_fc2 = ring_gather(mine_fc2, me)

    own_latent = latents_in[0]
    from_x = swap_x(own_latent)
    from_core = swap_core(own_latent)
    from_both = swap_core(from_x)
    all_latent = jnp.concatenate([own_latent, from_core, from_x, from_both]).astype(f32)
    latent = own_latent.astype(f32)
    grad_own = out_grad[0]
    grad_pair = jnp.concatenate([grad_own, swap_core(grad_own)]).astype(f32)
    grad_out = grad_own.astype(f32)

    normed_all = layer_norm(all_latent)
    act_one = (normed_all * (1.0 + scale_one) + shift_one).astype(bf16)
    bias_three = jnp.concatenate([bias_q, jnp.zeros_like(bias_q), bias_v])
    qkv = (dot(act_one, use_qkv, ((1,), (0,))) + bias_three).astype(bf16)
    queries, keys, values = jnp.split(qkv, 3, axis=1)
    attn_heads, lse = attend_forward(queries, keys, values, scale_val)

    def to_tokens(blocks):
        return [blocks[0]] + [seq_swap(blocks[k], k) for k in range(1, seq_count)]

    attn_own = jnp.concatenate(
        to_tokens([attn_heads[k * tokens : (k + 1) * tokens] for k in range(seq_count)]), axis=1
    )
    branch_one = dot(attn_own, use_proj, ((1,), (0,))) + bias_proj
    middle = latent + gate_one * branch_one
    normed_two, norm_pull_two = jax.vjp(layer_norm, middle)
    act_two_own = (normed_two * (1.0 + scale_two) + shift_two).astype(bf16)

    act_two = jnp.concatenate([act_two_own, swap_core(act_two_own)])
    hidden_pre = dot(act_two, use_fc1, ((1,), (0,))) + bias_fc1
    hidden_act, gelu_pull = jax.vjp(gelu_tanh, hidden_pre)
    hidden_low = hidden_act.astype(bf16)
    grad_two = (gate_two * grad_pair).astype(bf16)
    grad_hidden = dot(grad_two, use_fc2, ((1,), (1,)))
    grad_pre = gelu_pull(grad_hidden)[0].astype(bf16)
    partial_act = dot(grad_pre, use_fc1, ((1,), (1,)))
    grad_act_two = partial_act[:tokens] + swap_core(partial_act[tokens:])
    grad_shift_two = jnp.sum(grad_act_two, axis=0)
    grad_scale_two = jnp.sum(grad_act_two * normed_two, axis=0)
    grad_middle = grad_out + norm_pull_two(grad_act_two * (1.0 + scale_two))[0]
    grad_one = (gate_one * grad_middle).astype(bf16)
    grad_gate_one = jnp.sum(grad_middle * branch_one, axis=0)
    grad_attn = dot(grad_one, use_proj, ((1,), (1,))).astype(bf16)
    grad_heads = jnp.concatenate(
        to_tokens([grad_attn[:, k * quarter : (k + 1) * quarter] for k in range(seq_count)])
    )

    partial_two = dot(hidden_low, use_fc2, ((1,), (0,)))
    branch_two = partial_two[:tokens] + swap_core(partial_two[tokens:]) + bias_fc2
    result = middle + gate_two * branch_two
    grad_gate_two = jnp.sum(grad_out * branch_two, axis=0)
    grad_b_fc2 = jnp.sum(grad_two[:tokens].astype(f32), axis=0)
    grad_b_fc1 = jnp.sum(grad_pre.astype(f32), axis=0)
    grad_b_proj = jnp.sum(grad_one.astype(f32), axis=0)

    red_fc2 = ring_reduce(dot(hidden_low, grad_two, ((0,), (0,))).astype(bf16), me)
    red_fc1 = ring_reduce(dot(act_two, grad_pre, ((0,), (0,))).astype(bf16), me)

    def add_x(block):
        low = block.astype(bf16)
        return low.astype(f32) + swap_x(low).astype(f32)

    def in_core_order(block):
        other = swap_core(block)
        return jnp.where(core == 0, block, other), jnp.where(core == 0, other, block)

    grad_w_fc2 = jnp.concatenate(in_core_order(add_x(red_fc2)))
    first_fc1, second_fc1 = in_core_order(add_x(red_fc1))
    grad_w_fc1 = jnp.concatenate(
        [first_fc1.reshape(own_rows, owners, 1, units), second_fc1.reshape(own_rows, owners, 1, units)],
        axis=2,
    ).reshape(own_rows, 2 * owners * units)

    proj_rel = dot(attn_own, grad_one, ((0,), (0,))).astype(bf16)
    proj_abs = jnp.concatenate(
        [
            lax.dynamic_slice_in_dim(proj_rel, (place ^ k) * quarter, quarter, 0)
            for k in range(seq_count)
        ]
    )
    half_width = width // 2
    keep = lax.dynamic_slice_in_dim(proj_abs, core * half_width, half_width, 1)
    give = lax.dynamic_slice_in_dim(proj_abs, (1 - core) * half_width, half_width, 1)
    proj_sum = (keep.astype(f32) + swap_core(give).astype(f32)).astype(bf16)
    grad_w_proj = jnp.concatenate(in_core_order(add_x(ring_reduce(proj_sum, me))), axis=1)

    grad_q, grad_k, grad_v = attend_backward(queries, keys, values, grad_heads, lse, scale_val)
    grad_qkv = jnp.concatenate([grad_q, grad_k, grad_v], axis=1)
    red_qkv = ring_reduce(dot(act_one, grad_qkv, ((0,), (0,))).astype(bf16), me).astype(bf16)
    across = swap_x(red_qkv)
    blocks = [red_qkv, swap_core(red_qkv), across, swap_core(across)]
    for bit in (1, 2):
        flip = (place & bit) != 0
        blocks = [jnp.where(flip, blocks[j ^ bit], blocks[j]) for j in range(seq_count)]
    grad_w_qkv = jnp.concatenate(
        [b.astype(f32).reshape(own_rows, 3, 1, quarter) for b in blocks], axis=2
    ).reshape(own_rows, 3 * width)

    partial_one = dot(grad_qkv, use_qkv, ((1,), (1,)))
    grad_shift_one = jnp.sum(partial_one, axis=0)
    grad_scale_one = jnp.sum(partial_one * normed_all, axis=0)
    far_low = partial_one[2 * tokens :].astype(bf16)
    far_sum = far_low[:tokens].astype(f32) + swap_core(far_low[tokens:]).astype(f32)
    near_low = partial_one[tokens : 2 * tokens].astype(bf16)
    near_sum = partial_one[:tokens] + swap_core(near_low).astype(f32)
    grad_act_one = near_sum + swap_x(far_sum.astype(bf16)).astype(f32)
    _, norm_pull_one = jax.vjp(layer_norm, latent)
    grad_latent = grad_middle + norm_pull_one(grad_act_one * (1.0 + scale_one))[0]

    grad_b_qv = jnp.where(
        jnp.arange(seq_count)[None, :, None] == place,
        jnp.stack(
            [jnp.sum(grad_q.astype(f32), axis=0), jnp.sum(grad_v.astype(f32), axis=0)]
        )[:, None, :],
        0.0,
    ).reshape(2 * width)
    placed_fc1 = jnp.where(
        jnp.arange(2)[None, :, None] == core, grad_b_fc1.reshape(owners, 1, units), 0.0
    ).reshape(2 * owners * units)
    terms = jnp.concatenate(
        [
            grad_shift_one,
            grad_scale_one,
            grad_gate_one,
            grad_shift_two,
            grad_scale_two,
            grad_gate_two,
            grad_b_qv,
            grad_b_proj,
            placed_fc1,
            grad_b_fc2,
        ]
    )
    sums = (terms + seq_swap(terms, 1)) + (seq_swap(terms, 2) + seq_swap(terms, 3))
    low_sums = sums.astype(bf16)
    grad_mod = low_sums[: 6 * width]
    at = 6 * width
    by_owner = []
    for b in (b_qv, b_proj, b_fc1, b_fc2):
        size = b.shape[0] * owners
        by_owner.append(low_sums[at : at + size].reshape(owners, b.shape[0]))
        at += size
    by_owner = jnp.concatenate(by_owner, axis=1)
    sent_bias = rolled(by_owner[::-1], jnp.mod(me + 1, owners))
    mail = jnp.concatenate(
        [jnp.broadcast_to(grad_mod[None, :], (owners, 6 * width)), sent_bias], axis=1
    )
    got = deal_small(mail, me)
    mod_rel = got[:, : 6 * width]
    bias_sums = jnp.sum(got[:, 6 * width :].astype(f32), axis=0)
    back_cond = jnp.concatenate([cond_rows[:1], cond_rows[1:][::-1]])
    owned_w_ada = dot(back_cond, mod_rel, ((0,), (0,)))
    owned_b_ada = jnp.sum(
        lax.dynamic_slice_in_dim(mod_rel, me * bias_at, bias_at, 1).astype(f32), axis=0
    )
    cond_partial = dot(mod_rel, w_ada, ((1,), (1,)))
    back_partial = jnp.concatenate([cond_partial[:1], cond_partial[1:][::-1]])
    cond_got = rolled(deal_small(back_partial, me), me)
    grad_cond = silu_pull(cond_got.reshape(width))[0]
    at = 0
    owned_bias = []
    for b in (b_qv, b_proj, b_fc1, b_fc2):
        owned_bias.append(bias_sums[at : at + b.shape[0]])
        at += b.shape[0]
    return (
        result.astype(bf16)[None],
        grad_latent[None],
        grad_cond[None],
        owned_w_ada,
        owned_b_ada,
        grad_w_qkv,
        owned_bias[0],
        grad_w_proj,
        owned_bias[1],
        grad_w_fc1,
        owned_bias[2],
        grad_w_fc2,
        owned_bias[3],
    )


def swap_f(values, bit):
    count = lax.axis_size("fsdp")
    return lax.ppermute(values, "fsdp", [(i, i ^ bit) for i in range(count)])


def cube_bits():
    return [1 << b for b in range(lax.axis_size("fsdp").bit_length() - 1)]


def cube_places():
    places = [0]
    for bit in reversed(cube_bits()):
        places = places + [r | bit for r in places]
    return places


def cube_gather(row):
    rows = row
    for bit in reversed(cube_bits()):
        got = swap_f(rows, bit)
        rows = jnp.concatenate([rows, got])
    return rows


def cube_sum(rows):
    for bit in cube_bits():
        half = rows.shape[0] // 2
        got = swap_f(rows[half:], bit)
        rows = rows[:half] + got
    return rows[0]


def cube_deal(rows):
    count = rows.shape[0]
    done = 1
    for bit in cube_bits():
        parts = rows.reshape((done, 2, count // (2 * done)) + rows.shape[1:])
        got = swap_f(parts[:, 1], bit)
        rows = jnp.stack([parts[:, 0], got], axis=1).reshape(rows.shape)
        done *= 2
    return rows


def cube_to_order(rows, me):
    places = jnp.array(cube_places())
    count = rows.shape[0]
    hit = jnp.arange(count)[:, None] == jnp.bitwise_xor(places, me)[None, :]
    return jnp.sum(jnp.where(hit[:, :, None], rows[None], jnp.zeros_like(rows)[None]), axis=1)


SMEM = pl.BlockSpec(memory_space=pltpu.SMEM)
VMEM = pl.BlockSpec(memory_space=pltpu.VMEM)


def bytes_of(*arrays):
    return sum(a.size * a.dtype.itemsize for a in arrays)


def call_whole(body, outs, table, *arrays, scratch=()):
    return pl.pallas_call(
        body,
        out_shape=outs,
        in_specs=[SMEM] + [VMEM] * len(arrays),
        out_specs=jax.tree.map(lambda _: VMEM, outs),
        scratch_shapes=list(scratch),
        compiler_params=pltpu.CompilerParams(
            vmem_limit_bytes=bytes_of(*arrays) + bytes_of(*jax.tree.leaves(outs)) + 2**21
        ),
        cost_estimate=pl.CostEstimate(
            flops=0,
            bytes_accessed=bytes_of(*arrays) + bytes_of(*jax.tree.leaves(outs)),
            transcendentals=0,
        ),
    )(table, *arrays)


def shaped(rows, cols, dtype=bf16):
    return jax.ShapeDtypeStruct((rows, cols), dtype)


def make_table(place, me):
    count = lax.axis_size("fsdp")
    around = [ring_place(me, off) for off in range(count)]
    return jnp.stack([jnp.asarray(v, jnp.int32) for v in [place] + around])


def along(at, offset, count):
    return at[1 + offset % count]


LANES = 128


def bias_lines(sizes):
    lines = []
    for n, size in enumerate(sizes):
        for lo in range(0, size, LANES):
            lines.append((n, lo, min(LANES, size - lo)))
    return lines


def pack_first(table, w_proj, w_qkv, biases, seq_count):
    rows, width = w_proj.shape
    half = width // 2
    quarter = width // seq_count
    total = half + 3 * quarter

    def body(at, proj, qkv, *rest):
        small, out, lines = rest[: len(biases)], rest[len(biases)], rest[-1]
        lines[...] = jnp.zeros_like(lines)
        for line, (n, lo, size) in enumerate(bias_lines([b.shape[1] for b in biases])):
            lines[line : line + 1, :size] = small[n][:, lo : lo + size].astype(f32)
        out[:16, total:] = lines[...].astype(bf16)
        out[16:, total:] = jnp.zeros((rows - 16, LANES), bf16)
        for s in range(seq_count):

            @pl.when(at[0] == s)
            def _(s=s):
                out[:, :half] = proj[:, (s % 2) * half : (s % 2 + 1) * half]
                for t in range(3):
                    to = half + t * quarter
                    start = t * width + s * quarter
                    out[:, to : to + quarter] = qkv[:, start : start + quarter]

    outs = shaped(rows, total + LANES)
    scratch = [pltpu.VMEM((16, LANES), f32)]
    return call_whole(body, outs, table, w_proj, w_qkv, *biases, scratch=scratch)


def put_first(table, pieces, rows, width, quarter, sizes):
    count = lax.axis_size("fsdp")
    half = width // 2
    total = half + 3 * quarter
    offsets = [off for off, _, _ in pieces]
    shifts = [first for _, first, _ in pieces]

    def body(at, *refs):
        ins = refs[: len(pieces)]
        proj, qkv = refs[len(pieces) : len(pieces) + 2]
        kept = refs[-1]
        for ref, off, shift in zip(ins, offsets, shifts):
            size = ref.shape[0]
            owner = along(at, off, count)
            start = pl.multiple_of(owner * rows + shift, 16)
            proj[pl.ds(start, size), :] = ref[:, :half]
            qkv[pl.ds(start, size), :] = ref[:, half:total]
            if shift == 0:
                kept[pl.ds(pl.multiple_of(owner * 16, 16), 16), :] = ref[:16, total:]

    outs = (shaped(width, half), shaped(width, 3 * quarter), shaped(count * 16, LANES))
    proj, qkv, kept = call_whole(body, outs, table, *[p for _, _, p in pieces])
    kept = kept.reshape(count, 16, LANES).astype(f32)
    vectors = []
    for n in range(len(sizes)):
        parts = [kept[:, i, :z] for i, (m, _, z) in enumerate(bias_lines(sizes)) if m == n]
        vectors.append(jnp.concatenate(parts, axis=1))
    return proj, qkv, *vectors


def pack_second(table, w_fc1, w_fc2, owners):
    rows = w_fc1.shape[0]
    width = w_fc2.shape[1]
    units = w_fc2.shape[0] // 2
    span = owners * units
    parts = units // rows

    def body(at, fc1, fc2, out):
        for c in range(2):

            @pl.when(at[0] % 2 == c)
            def _(c=c):
                for f in range(owners):
                    start = (2 * f + c) * units
                    out[:, f * units : (f + 1) * units] = fc1[:, start : start + units]
                for n in range(parts):
                    start = c * units + n * rows
                    to = span + n * width
                    out[:, to : to + width] = fc2[start : start + rows, :]

    outs = shaped(rows, span + parts * width)
    return call_whole(body, outs, table, w_fc1, w_fc2)


def ring_pieces(block, half):
    count = lax.axis_size("fsdp")
    _, ahead, back = ring_tables(count)
    far = count // 2
    pieces = [(0, 0, block)]
    up = down = block
    for step in range(1, far + 1):
        if step == far:
            up, down = up[:half], down[half:]
        up = lax.ppermute(up, "fsdp", ahead)
        down = lax.ppermute(down, "fsdp", back)
        pieces.append((-step, 0, up))
        pieces.append((step, half if step == far else 0, down))
    return pieces


def assemble(pieces, layout, outs, table):
    count = lax.axis_size("fsdp")
    offsets = [off for off, _, _ in pieces]
    shifts = [first for _, first, _ in pieces]

    def body(at, *refs):
        ins, results = refs[: len(pieces)], refs[len(pieces) :]
        for ref, off, shift in zip(ins, offsets, shifts):
            owner = along(at, off, count)

            def some(lo, ref=ref, owner=owner, shift=shift):
                for out, per, base, col, cols in layout:
                    results[out][sixteen(owner * per + base + shift + lo), :] = ref[
                        sixteen(lo), col : col + cols
                    ]

            by_sixteen(ref.shape[0], some)

    return call_whole(body, outs, table, *[p for _, _, p in pieces])


def mix_proj(table, own, other, seq_count):
    width, half = own.shape
    quarter = width // seq_count

    def body(at, mine, theirs, out):
        for s in range(seq_count):

            @pl.when(at[0] == s)
            def _(s=s):
                c = s % 2
                for k in range(seq_count):
                    src = slice((s ^ k) * quarter, ((s ^ k) + 1) * quarter)
                    dst = slice(k * quarter, (k + 1) * quarter)
                    out[dst, c * half : (c + 1) * half] = mine[src, :]
                    out[dst, (1 - c) * half : (2 - c) * half] = theirs[src, :]

    return call_whole(body, shaped(width, width), table, own, other)


def split_proj(table, values, seq_count):
    width = values.shape[1]
    half = width // 2
    quarter = width // seq_count

    def body(at, ref, keep, give):
        for s in range(seq_count):

            @pl.when(at[0] == s)
            def _(s=s):
                c = s % 2
                for k in range(seq_count):
                    dst = slice((s ^ k) * quarter, ((s ^ k) + 1) * quarter)
                    src = slice(k * quarter, (k + 1) * quarter)
                    keep[dst, :] = ref[src, c * half : (c + 1) * half]
                    give[dst, :] = ref[src, (1 - c) * half : (2 - c) * half]

    return call_whole(body, (shaped(width, half), shaped(width, half)), table, values)


def ring_sum(arrays, layout, table, rows):
    count = lax.axis_size("fsdp")
    _, ahead, back = ring_tables(count)
    half = rows // 2
    far = count // 2
    total = sum(cols for _, _, cols in layout)

    def step_call(step, *got):
        def body(at, *refs):
            blocks, rest = refs[: len(arrays)], refs[len(arrays) :]
            up_at, down_at = along(at, far - step, count), along(at, step - far, count)

            def sixteen(line, carry):
                low = pl.ds(pl.multiple_of(line * 16, 16), 16)
                high = pl.ds(pl.multiple_of(half + line * 16, 16), 16)
                col = 0
                for a, base, cols in layout:
                    to = slice(col, col + cols)
                    col += cols
                    per = blocks[a].shape[0] // count

                    def own(owner, lo):
                        start = pl.multiple_of(owner * per + base + lo + line * 16, 16)
                        return blocks[a][pl.ds(start, 16), :]

                    def plus(owner, lo, *others):
                        total_val = own(owner, lo).astype(f32)
                        for ref, at_rows in others:
                            total_val = total_val + ref[at_rows, to].astype(f32)
                        return total_val.astype(bf16)

                    if step == 0:
                        rest[0][low, to] = own(up_at, 0)
                        rest[1][low, to] = own(down_at, half)
                    elif step == far:
                        up, down, out = rest
                        out[low, to] = plus(up_at, 0, (up, low), (down, low))
                        out[high, to] = plus(up_at, half, (up, high), (down, high))
                    else:
                        up, down, next_up, next_down = rest
                        next_up[low, to] = plus(up_at, 0, (up, low))
                        next_down[high, to] = plus(
                            down_at, half, (down, low if step == 1 else high)
                        )
                        if step == 1:
                            next_up[high, to] = own(up_at, half)
                            next_down[low, to] = own(down_at, 0)
                        else:
                            next_up[high, to] = plus(up_at, half, (up, high))
                            next_down[low, to] = plus(down_at, 0, (down, low))
                return carry

            lax.fori_loop(0, half // 16, sixteen, 0)

        out = shaped(half if step == 0 else rows, total)
        outs = out if step == far else (out, out)
        return call_whole(body, outs, table, *arrays, *got)

    up, down = step_call(0)
    for step in range(1, far + 1):
        up = lax.ppermute(up, "fsdp", ahead)
        down = lax.ppermute(down, "fsdp", back)
        if step < far:
            up, down = step_call(step, up, down)
    return step_call(far, up, down)


def by_sixteen(size, step):
    def one(line, carry):
        step(line * 16)
        return carry

    lax.fori_loop(0, size // 16, one, 0)


def sixteen(start):
    return pl.ds(pl.multiple_of(start, 16), 16)


def cube_reduce(values, table, rows):
    bits = cube_bits()
    cols = sum(v.shape[1] for v in values)

    def call(step, *ins):
        left = len(bits) - step
        n_outs = 2 if 0 < step < len(bits) else 1

        def body(at, *refs):
            held = refs[: len(values) if step < 2 else 1]
            got = refs[len(held)]
            outs = refs[len(refs) - n_outs :]
            me = at[1]

            def emit(out, row, n):
                index = 2 * n + lax.rem(me, 2) if step == 1 else n

                def some(lo):
                    col = 0
                    for part in held:
                        to = slice(col, col + part.shape[1])
                        col += part.shape[1]
                        mine = part[sixteen(index * rows + lo), :]
                        if step > 0:
                            theirs = got[sixteen(n * rows + lo), to]
                            mine = (mine.astype(f32) + theirs.astype(f32)).astype(bf16)
                        out[sixteen(row + lo), to] = mine

                by_sixteen(rows, some)

            if left == 0:
                emit(outs[0], 0, 0)
                return
            bit = lax.rem(me >> step, 2)
            for n in range((1 << left) // 2):
                emit(outs[0], n * rows, 2 * n + (1 - bit))
                if step > 0:
                    emit(outs[1], n * rows, 2 * n + bit)

        out = shaped(rows * max(1, (1 << left) // 2), cols)
        outs = (out, out) if n_outs == 2 else out
        return call_whole(body, outs, table, *ins)

    held, got = values, None
    for step, bit in enumerate(bits):
        if step == 0:
            send = call(step, *held)
        else:
            send, kept = call(step, *held, got)
            held = [kept]
        got = swap_f(send, bit)
    return call(len(bits), *held, got)


def place_second(table, own, other, owners, rows, units, width):
    span = owners * units
    parts = units // rows

    def body(at, mine, theirs, fc1, fc2):
        for c in range(2):

            @pl.when(at[0] % 2 == c)
            def _(c=c):
                for ref, cc in ((mine, c), (theirs, 1 - c)):
                    for f in range(owners):
                        start = (2 * f + cc) * units
                        fc1[:, start : start + units] = ref[
                            :, f * units : (f + 1) * units
                        ].astype(f32)
                    for n in range(parts):
                        start = cc * units + n * rows
                        to = span + n * width
                        fc2[start : start + rows, :] = ref[:, to : to + width].astype(f32)

    outs = (shaped(rows, 2 * span, f32), shaped(2 * units, width, f32))
    return call_whole(body, outs, table, own, other)


def place_first(table, own, across, sums, near, seq_count, width):
    rows = own.shape[0]
    half = width // 2
    quarter = width // seq_count
    span = 3 * quarter

    def body(at, own, across, sums, near, proj, qkv):
        for s in range(seq_count):

            @pl.when(at[0] == s)
            def _(s=s):
                c = s % 2
                proj[:, c * half : (c + 1) * half] = sums[...].astype(f32)
                proj[:, (1 - c) * half : (2 - c) * half] = near[:, :half].astype(f32)
                parts = ((own, half), (near, half), (across, half), (near, half + span))
                for k, (ref, base) in enumerate(parts):
                    for t in range(3):
                        start = t * width + (s ^ k) * quarter
                        at_col = base + t * quarter
                        qkv[:, start : start + quarter] = ref[
                            :, at_col : at_col + quarter
                        ].astype(f32)

    outs = (shaped(rows, width, f32), shaped(rows, 3 * width, f32))
    return call_whole(body, outs, table, own, across, sums, near)


def heads_forward(qkv, scale_val):
    length = qkv.shape[0]
    flat = qkv.shape[1] // 3
    heads = flat // HEAD
    block = min(512, length)

    def body(whole, out, lse, q_at, k_at, v_at, o_at):
        i = pl.program_id(0)

        @pl.when(i == 0)
        def _():
            for h in range(heads):
                lo = h * HEAD
                q_at[h] = (whole[:, lo : lo + HEAD].astype(f32) * scale_val).astype(bf16)
                k_at[h] = whole[:, flat + lo : flat + lo + HEAD]
                v_at[h] = whole[:, 2 * flat + lo : 2 * flat + lo + HEAD].T

        rows = pl.ds(pl.multiple_of(i * block, block), block)

        def one_head(h, carry):
            scores = dot(k_at[h], q_at[h, rows], ((1,), (1,)))
            top_val = jnp.max(scores, axis=0, keepdims=True)
            expd = jnp.exp(scores - top_val)
            totals = jnp.sum(expd, axis=0, keepdims=True)
            o_at[h] = dot(v_at[h], expd.astype(bf16), ((1,), (0,))) * (1.0 / totals)
            lse[h] = top_val + jnp.log(totals)
            return carry

        lax.fori_loop(0, heads, one_head, 0)
        for h in range(heads):
            out[:, h * HEAD : (h + 1) * HEAD] = o_at[h].T.astype(bf16)

    return pl.pallas_call(
        body,
        grid=(length // block,),
        in_specs=[pl.BlockSpec((length, 3 * flat), lambda i: (0, 0))],
        out_specs=[
            pl.BlockSpec((block, flat), lambda i: (i, 0)),
            pl.BlockSpec((heads, 1, block), lambda i: (0, 0, i)),
        ],
        out_shape=[shaped(length, flat), jax.ShapeDtypeStruct((heads, 1, length), f32)],
        scratch_shapes=[
            pltpu.VMEM((heads, length, HEAD), bf16),
            pltpu.VMEM((heads, length, HEAD), bf16),
            pltpu.VMEM((heads, HEAD, length), bf16),
            pltpu.VMEM((heads, HEAD, block), f32),
        ],
        compiler_params=pltpu.CompilerParams(vmem_limit_bytes=16 * 2**20),
        cost_estimate=pl.CostEstimate(
            flops=4 * length * length * flat,
            bytes_accessed=8 * length * flat,
            transcendentals=heads * length * length,
        ),
    )(qkv)


def heads_backward(qkv, grad, lse, scale_val, first, last, done=None):
    length = qkv.shape[0]
    flat = qkv.shape[1] // 3
    heads = last - first
    before = 0 if done is None else first * HEAD
    mine = heads * HEAD
    span = before + mine
    block = min(512, length)
    steps = length // block

    def body(whole, grads, lse_here, *refs):
        if done is not None:
            earlier, refs = refs[0], refs[1:]
        out, q_at, k_at, kt_at, v_at, g_at, dq_at, sum_k, sum_v = refs
        i = pl.program_id(0)

        @pl.when(i == 0)
        def _():
            for h in range(heads):
                lo = (first + h) * HEAD
                q_at[h] = (whole[:, lo : lo + HEAD].astype(f32) * scale_val).astype(bf16)
                key = whole[:, flat + lo : flat + lo + HEAD]
                k_at[h] = key
                kt_at[h] = key.T
                v_at[h] = whole[:, 2 * flat + lo : 2 * flat + lo + HEAD]
                g_at[h] = grads[:, lo : lo + HEAD]
            sum_k[...] = jnp.zeros_like(sum_k)
            sum_v[...] = jnp.zeros_like(sum_v)
            if done is not None:
                for t in range(3):
                    out[:, t * span : t * span + before] = earlier[:, t * before : (t + 1) * before]

        rows = pl.ds(pl.multiple_of(i * block, block), block)

        def one_head(h, carry):
            q = q_at[h, rows]
            g = g_at[h, rows]
            probs = jnp.exp(dot(k_at[h], q, ((1,), (1,))) - lse_here[first + h])
            grad_probs = dot(v_at[h], g, ((1,), (1,)))
            inner = jnp.sum(probs * grad_probs, axis=0, keepdims=True)
            grad_scores = (probs * (grad_probs - inner)).astype(bf16)
            dq_at[h] = dot(kt_at[h], grad_scores, ((1,), (0,))) * scale_val
            sum_k[h] += dot(grad_scores, q, ((1,), (0,)))
            sum_v[h] += dot(probs.astype(bf16), g, ((1,), (0,)))
            return carry

        lax.fori_loop(0, heads, one_head, 0)
        for h in range(heads):
            lo = before + h * HEAD
            out[rows, lo : lo + HEAD] = dq_at[h].T.astype(bf16)

        @pl.when(i == steps - 1)
        def _():
            for h in range(heads):
                lo = span + before + h * HEAD
                out[:, lo : lo + HEAD] = sum_k[h].astype(bf16)
                out[:, span + lo : span + lo + HEAD] = sum_v[h].astype(bf16)

    def whole_block(shape):
        return pl.BlockSpec(shape, lambda i: (0, 0))

    ins = [qkv, grad, lse] + ([] if done is None else [done])
    more = [] if done is None else [whole_block(done.shape)]
    return pl.pallas_call(
        body,
        grid=(steps,),
        in_specs=[
            whole_block((length, 3 * flat)),
            whole_block((length, flat)),
            pl.BlockSpec((lse.shape[0], 1, block), lambda i: (0, 0, i)),
        ]
        + more,
        out_specs=whole_block((length, 3 * span)),
        out_shape=shaped(length, 3 * span),
        scratch_shapes=[
            pltpu.VMEM((heads, length, HEAD), bf16),
            pltpu.VMEM((heads, length, HEAD), bf16),
            pltpu.VMEM((heads, HEAD, length), bf16),
            pltpu.VMEM((heads, length, HEAD), bf16),
            pltpu.VMEM((heads, length, HEAD), bf16),
            pltpu.VMEM((heads, HEAD, block), f32),
            pltpu.VMEM((heads, length, HEAD), f32),
            pltpu.VMEM((heads, length, HEAD), f32),
        ],
        compiler_params=pltpu.CompilerParams(vmem_limit_bytes=24 * 2**20),
        cost_estimate=pl.CostEstimate(
            flops=10 * length * length * mine,
            bytes_accessed=16 * length * mine,
            transcendentals=heads * length * length,
        ),
    )(*ins)


def local_ring(
    latents_in,
    conditions,
    w_ada,
    b_ada,
    w_qkv,
    b_qv,
    w_proj,
    b_proj,
    w_fc1,
    b_fc1,
    w_fc2,
    b_fc2,
    out_grad,
):
    width = latents_in.shape[2]
    tokens = latents_in.shape[1]
    seq_count = lax.axis_size("seq")
    owners = lax.axis_size("fsdp")
    me = lax.axis_index("fsdp")
    place = lax.axis_index("seq")
    core = place % 2
    own_rows = w_ada.shape[0]
    quarter = width // seq_count
    half_width = width // 2
    units = w_fc2.shape[0] // 2
    span = owners * units
    parts = units // own_rows
    scale_val = HEAD ** (-0.5)
    table = make_table(place, me)

    small = [b.astype(f32)[None] for b in (b_qv, b_proj, b_fc1, b_fc2)]
    first = ring_pieces(pack_first(table, w_proj, w_qkv, small, seq_count), own_rows // 2)
    second = ring_pieces(pack_second(table, w_fc1, w_fc2, owners), own_rows // 2)

    condition = conditions[0]
    cond_act, silu_pull = jax.vjp(jax.nn.silu, condition)
    cond_low = cond_act.astype(bf16)
    cond_rel = cube_gather(cond_low.astype(f32)[None])
    cond_rows = lax.dynamic_slice_in_dim(cond_rel, me * own_rows, own_rows, 1).astype(bf16)
    mod_partial = dot(cond_rows, w_ada, ((1,), (0,)))
    bias_at = b_ada.shape[0]
    owned = jnp.arange(owners)[:, None] == me
    placed_bias = jnp.where(owned, b_ada.astype(f32)[None, :], 0.0)
    mod_partial = mod_partial + placed_bias.reshape(1, owners * bias_at)
    modulation = cube_sum(mod_partial)
    shift_one, scale_one, gate_one, shift_two, scale_two, gate_two = jnp.split(modulation, 6)

    proj_half, use_qkv, *biases = put_first(
        table, first, own_rows, width, quarter, [v.shape[1] for v in small]
    )
    use_proj = mix_proj(table, proj_half, seq_swap(proj_half, 1), seq_count)
    qv_full = biases[0].reshape(2, seq_count, quarter)
    bias_q, bias_v = lax.dynamic_index_in_dim(qv_full, place, 1, keepdims=False)
    bias_proj = biases[1].reshape(width)
    bias_fc1 = lax.dynamic_index_in_dim(
        biases[2].reshape(owners, 2, units), core, 1, keepdims=False
    ).reshape(span)
    bias_fc2 = biases[3].reshape(width)

    own_latent = latents_in[0]
    from_x = seq_swap(own_latent, 2)
    from_core = seq_swap(own_latent, 1)
    from_both = seq_swap(from_x, 1)
    all_latent = jnp.concatenate([own_latent, from_core, from_x, from_both]).astype(f32)
    latent = own_latent.astype(f32)
    grad_own = out_grad[0]
    grad_pair = jnp.concatenate([grad_own, seq_swap(grad_own, 1)]).astype(f32)
    grad_out = grad_own.astype(f32)

    normed_all = layer_norm(all_latent)
    act_one = (normed_all * (1.0 + scale_one) + shift_one).astype(bf16)
    bias_three = jnp.concatenate([bias_q, jnp.zeros_like(bias_q), bias_v])
    qkv = (dot(act_one, use_qkv, ((1,), (0,))) + bias_three).astype(bf16)
    attn_heads, lse = heads_forward(qkv, scale_val)

    def to_tokens(blocks):
        return [blocks[0]] + [seq_swap(blocks[k], k) for k in range(1, seq_count)]

    attn_own = jnp.concatenate(
        to_tokens([attn_heads[k * tokens : (k + 1) * tokens] for k in range(seq_count)]),
        axis=1,
    )
    branch_one = dot(attn_own, use_proj, ((1,), (0,))) + bias_proj
    middle = latent + gate_one * branch_one
    normed_two, norm_pull_two = jax.vjp(layer_norm, middle)
    act_two_own = (normed_two * (1.0 + scale_two) + shift_two).astype(bf16)

    act_two = jnp.concatenate([act_two_own, seq_swap(act_two_own, 1)])
    use_fc1, use_fc2 = assemble(
        second,
        [(0, own_rows, 0, 0, span)]
        + [(1, units, n * own_rows, span + n * width, width) for n in range(parts)],
        (shaped(width, span), shaped(span, width)),
        table,
    )
    hidden_pre = dot(act_two, use_fc1, ((1,), (0,))) + bias_fc1
    hidden_act, gelu_pull = jax.vjp(gelu_tanh, hidden_pre)
    hidden_low = hidden_act.astype(bf16)
    grad_two = (gate_two * grad_pair).astype(bf16)
    grad_hidden = dot(grad_two, use_fc2, ((1,), (1,)))
    grad_pre = gelu_pull(grad_hidden)[0].astype(bf16)
    far_act = dot(grad_pre[tokens:], use_fc1, ((1,), (1,)))
    near_act = dot(grad_pre[:tokens], use_fc1, ((1,), (1,)))
    grad_act_two = near_act + seq_swap(far_act, 1)

    grad_fc1 = dot(act_two, grad_pre, ((0,), (0,))).astype(bf16)
    grad_fc2 = dot(hidden_low, grad_two, ((0,), (0,))).astype(bf16)
    second_red = ring_sum(
        [grad_fc1, grad_fc2],
        [(0, 0, span)] + [(1, n * own_rows, width) for n in range(parts)],
        table,
        own_rows,
    )

    grad_shift_two = jnp.sum(grad_act_two, axis=0)
    grad_scale_two = jnp.sum(grad_act_two * normed_two, axis=0)
    grad_middle = grad_out + norm_pull_two(grad_act_two * (1.0 + scale_two))[0]
    grad_one = (gate_one * grad_middle).astype(bf16)
    grad_gate_one = jnp.sum(grad_middle * branch_one, axis=0)
    grad_attn = dot(grad_one, use_proj, ((1,), (1,))).astype(bf16)
    grad_heads = jnp.concatenate(
        to_tokens([grad_attn[:, k * quarter : (k + 1) * quarter] for k in range(seq_count)])
    )

    far_two = dot(hidden_low[tokens:], use_fc2, ((1,), (0,)))
    near_two = dot(hidden_low[:tokens], use_fc2, ((1,), (0,)))
    branch_two = near_two + seq_swap(far_two, 1) + bias_fc2
    result = middle + gate_two * branch_two
    grad_gate_two = jnp.sum(grad_out * branch_two, axis=0)
    grad_b_fc2 = jnp.sum(grad_two[:tokens].astype(f32), axis=0)
    grad_b_fc1 = jnp.sum(grad_pre.astype(f32), axis=0)
    grad_b_proj = jnp.sum(grad_one.astype(f32), axis=0)

    proj_rel = dot(attn_own, grad_one, ((0,), (0,))).astype(bf16)
    keep, give = split_proj(table, proj_rel, seq_count)
    proj_sum = (keep.astype(f32) + seq_swap(give, 1).astype(f32)).astype(bf16)

    most = max(1, quarter // HEAD - 1)
    grad_most = heads_backward(qkv, grad_heads, lse, scale_val, 0, most)
    grad_qkv = heads_backward(
        qkv, grad_heads, lse, scale_val, most, quarter // HEAD, done=grad_most
    )
    grad_own_qkv = dot(act_one, grad_qkv, ((0,), (0,))).astype(bf16)
    first_red = cube_reduce([proj_sum, grad_own_qkv], table, own_rows)
    first_x = seq_swap(first_red, 2)
    own_half = (
        first_red[:, :half_width].astype(f32) + first_x[:, :half_width].astype(f32)
    ).astype(bf16)
    mail = jnp.concatenate([own_half, first_red[:, half_width:], first_x[:, half_width:]], axis=1)
    grad_w_proj, grad_w_qkv = place_first(
        table, first_red, first_x, own_half, seq_swap(mail, 1), seq_count, width
    )
    second_sum = (second_red.astype(f32) + seq_swap(second_red, 2).astype(f32)).astype(bf16)
    grad_w_fc1, grad_w_fc2 = place_second(
        table, second_sum, seq_swap(second_sum, 1), owners, own_rows, units, width
    )

    partial_one = dot(grad_qkv, use_qkv, ((1,), (1,)))
    grad_shift_one = jnp.sum(partial_one, axis=0)
    grad_scale_one = jnp.sum(partial_one * normed_all, axis=0)
    far_low = partial_one[2 * tokens :].astype(bf16)
    far_sum = far_low[:tokens].astype(f32) + seq_swap(far_low[tokens:], 1).astype(f32)
    near_low = partial_one[tokens : 2 * tokens].astype(bf16)
    near_sum = partial_one[:tokens] + seq_swap(near_low, 1).astype(f32)
    from_ox = seq_swap(far_sum.astype(bf16), 2)

    qkv_sums = jnp.sum(grad_qkv.astype(f32), axis=0).reshape(3, 1, quarter)
    grad_b_qv = jnp.where(
        jnp.arange(seq_count)[None, :, None] == place,
        jnp.concatenate([qkv_sums[:1], qkv_sums[2:]]),
        0.0,
    ).reshape(2 * width)
    placed_fc1 = jnp.where(
        jnp.arange(2)[None, :, None] == core, grad_b_fc1.reshape(owners, 1, units), 0.0
    ).reshape(2 * span)
    terms = jnp.concatenate(
        [
            grad_shift_one,
            grad_scale_one,
            grad_gate_one,
            grad_shift_two,
            grad_scale_two,
            grad_gate_two,
            grad_b_qv,
            grad_b_proj,
            placed_fc1,
            grad_b_fc2,
        ]
    )
    pair_sum = terms + seq_swap(terms, 1)
    sums = pair_sum + seq_swap(pair_sum, 2)
    low_sums = sums.astype(bf16)
    late_middle, late_latent, _ = lax.optimization_barrier((grad_middle, latent, low_sums))
    grad_act_one = near_sum + from_ox.astype(f32)
    _, norm_pull_one = jax.vjp(layer_norm, late_latent)
    grad_latent = late_middle + norm_pull_one(grad_act_one * (1.0 + scale_one))[0]
    got = cube_gather(low_sums[None])
    mod_rel = got[:, : 6 * width]
    all_sums = jnp.sum(got[:, 6 * width :].astype(f32), axis=0)
    owned_w_ada = dot(cond_rows, mod_rel, ((0,), (0,)))
    owned_b_ada = jnp.sum(
        lax.dynamic_slice_in_dim(mod_rel, me * bias_at, bias_at, 1).astype(f32), axis=0
    )
    cond_partial = dot(mod_rel, w_ada, ((1,), (1,)))
    cond_got = cube_to_order(cube_deal(cond_partial), me)
    grad_cond = silu_pull(cond_got.reshape(width))[0]
    at = 0
    owned_bias = []
    for b in (b_qv, b_proj, b_fc1, b_fc2):
        size = b.shape[0]
        owned_bias.append(lax.dynamic_slice_in_dim(all_sums, at + me * size, size, 0))
        at += size * owners
    return (
        result.astype(bf16)[None],
        grad_latent[None],
        grad_cond[None],
        owned_w_ada,
        owned_b_ada,
        grad_w_qkv,
        owned_bias[0],
        grad_w_proj,
        owned_bias[1],
        grad_w_fc1,
        owned_bias[2],
        grad_w_fc2,
        owned_bias[3],
    )


def short_axes(mesh):
    count = mesh.shape["fsdp"]
    return 2 < count <= RING_MAX and count & (count - 1) == 0 and mesh.shape["seq"] == 4


def local(*args):
    return local_ring(*args)


def solution(mesh):
    short = short_axes(mesh)
    return jax.shard_map(
        local if short else local_wide,
        mesh=mesh,
        in_specs=(
            P("fsdp", "seq", None),
            P("fsdp", None),
            P("fsdp", None),
            P("fsdp"),
            P("fsdp", None),
            P("fsdp"),
            P("fsdp", None),
            P("fsdp"),
            P("fsdp", None),
            P("fsdp"),
            P("fsdp", None),
            P("fsdp"),
            P("fsdp", "seq", None),
        ),
        out_specs=(
            P("fsdp", "seq", None),
            P("fsdp", "seq", None),
            P("fsdp", None),
            P("fsdp", None),
            P("fsdp"),
            P("fsdp", None),
            P("fsdp"),
            P("fsdp", None),
            P("fsdp"),
            P("fsdp", None),
            P("fsdp"),
            P("fsdp", None),
            P("fsdp"),
        ),
        check_vma=False,
    )
```
